512 devices in a mesh: gz: 128 (over z, y, core), gy: 4 (over x).
Axes of the slice: x: 4, y: 4, z: 16, core: 2. Of those that a mesh axis runs over, the one named last changes fastest.
Arguments:
- field: float32 [32, 128, 128, 256], P(None, 'gz', 'gy'), may hold values from -6 to 6
- spectral_filter: float32 [2, 16, 16, 1024], P(None, None, 'gy', 'gz'), may hold values from -6 to 6
- depth_weight: float32 [32, 27], replicated, may hold values from -1.25 to 1.25
- point_weight: float32 [32, 32], replicated, may hold values from -1 to 1
- bias_vector: float32 [32], replicated, may hold values from -3 to 3
Outputs:
- layer_out: float32 [32, 128, 128, 256], P(None, 'gz', 'gy')
The draws below stay inside these ranges and needn't reach their ends.
All inputs are finite; a program needn't handle non-finite values.
Results may differ from the reference program's by a relative error of at most 0.000057.
Values sent between devices are 32-bit elements; how exact they have to be, the bound alone decides.
A program may use at most 64 MiB of HBM per device.

```python
import math
import jax
import jax.numpy as jnp
from jax import lax

CHANNELS = 32
NX = 256
NY = 128
MX = 32
MY = 16
MZ = 16
NZ = 128


def levels(rng, dims, pieces, smallest, top_value):
    level, own = 1.0, jax.random.fold_in(rng, 6)
    for dim, shards_of in pieces:
        heights = jnp.exp(jax.random.uniform(jax.random.fold_in(own, dim), (shards_of,), jnp.float32, smallest / len(pieces), top_value / len(pieces)))
        level = level * jnp.repeat(heights, dims[dim] // shards_of).reshape([-1 if axis == dim else 1 for axis in range(len(dims))])
    return level


def normal_values(stream_key, shape, width, reach, cuts=(), kind=jnp.bfloat16):
    array = jax.random.normal(stream_key, shape, jnp.float32) * width
    if len(cuts) > 0:
        array = levels(stream_key, shape, cuts, -0.22, 0.18) * array
    return jnp.clip(array, min=-reach, max=reach).astype(kind)


def setup_inputs(seed: int = 0) -> dict:
    splits = jax.random.split(jax.random.key(seed), 6)
    field = normal_values(splits[0], (CHANNELS, NZ, NY, NX), 1.0, 6.0, ((1, 128), (2, 4)), jnp.float32)
    spectral_filter = normal_values(splits[1], (2, MZ, MY, CHANNELS * MX), 1.0, 6.0, ((2, 4), (3, 128)), jnp.float32)
    depth_weight = normal_values(splits[2], (CHANNELS, 27), 27 ** -0.5, 1.25, (), jnp.float32)
    point_weight = normal_values(splits[3], (CHANNELS, CHANNELS), CHANNELS ** -0.5, 1.0, (), jnp.float32)
    bias_vector = normal_values(splits[4], (CHANNELS,), 0.5, 3.0, (), jnp.float32)
    return {"field": field, "spectral_filter": spectral_filter, "depth_weight": depth_weight, "point_weight": point_weight, "bias_vector": bias_vector}


def kept_freqs(count, total):
    series = jnp.arange(count, dtype=jnp.int32)
    return jnp.where(series < count // 2, series, total - count + series).astype(jnp.int32)

def reference(field, spectral_filter, depth_weight, point_weight, bias_vector):
    layout = spectral_filter.reshape(2, MZ, MY, CHANNELS, MX)
    gains = jnp.transpose(lax.complex(layout[0], layout[1]), (2, 0, 1, 3))
    z_keep = kept_freqs(MZ, NZ)
    y_keep = kept_freqs(MY, NY)
    factor = NX * NY * NZ / math.sqrt(2.0 * MX * MY * MZ)

    def one_channel(pack):
        plane, gain_set, taps = pack
        spectrum = jnp.fft.rfftn(plane, norm='ortho')
        kept = spectrum[z_keep][:, y_keep][:, :, :MX]
        product = kept * gain_set
        placed = jnp.zeros(spectrum.shape, spectrum.dtype).at[z_keep[:, None], y_keep[None, :], :MX].set(product)
        back = jnp.fft.irfftn(placed, s=plane.shape) * factor
        depth = jnp.zeros_like(plane)
        for off_z in (-1, 0, 1):
            for off_y in (-1, 0, 1):
                for off_x in (-1, 0, 1):
                    tap_index = (off_z + 1) * 9 + (off_y + 1) * 3 + (off_x + 1)
                    moved = jnp.roll(plane, (-off_z, -off_y, -off_x), axis=(0, 1, 2))
                    depth = depth + taps[tap_index] * moved
        return (back, depth)
    spectral, depth = lax.map(one_channel, (field, gains, depth_weight))
    point = jnp.einsum('dc,czyx->dzyx', point_weight, depth, precision=lax.Precision.HIGHEST)
    return jax.nn.gelu(spectral + point + bias_vector[:, None, None, None], approximate=False)
```

```python
import functools

import jax
import jax.numpy as jnp
import ml_dtypes
import numpy as np
from jax import lax
from jax.experimental import pallas as pl
from jax.experimental.pallas import tpu as pltpu
from jax.sharding import PartitionSpec as P

C = 32
NX = 256
NY = 128
NZ = 128
MX = 32
MY = 16
MZ = 16
GY = 4
ZC = 16
W = 8
YL = NY // GY
MESH = pl.DeviceIdType.MESH
F32 = jnp.float32
BF16 = jnp.bfloat16
VMEM = pltpu.VMEM
DMA = pltpu.SemaphoreType.DMA


def halves(table):
    high = table.astype(ml_dtypes.bfloat16)
    low = (table - high.astype(np.float64)).astype(ml_dtypes.bfloat16)
    return high, low


def kept(count, total):
    series = np.arange(count)
    return np.where(series < count // 2, series, total - count + series)


def make_tables():
    tables = {}
    angle = 2 * np.pi * (np.arange(NX)[:, None] * np.arange(MX)[None, :] % NX) / NX
    cos = np.cos(angle).reshape(NX, 4, 8)
    sin = np.sin(angle).reshape(NX, 4, 8)
    plain = np.stack([cos, -sin], axis=2).reshape(NX, 64)
    swapped = np.stack([-sin, -cos], axis=2).reshape(NX, 64)
    zero = np.zeros_like(plain)
    tx = np.stack(
        [
            np.concatenate([plain, zero, swapped, zero], axis=1),
            np.concatenate([zero, plain, zero, swapped], axis=1),
        ]
    )
    tables["tx"] = np.stack(halves(tx))
    places = np.arange(NY)
    angle = 2 * np.pi * (kept(MY, NY)[:, None] * places[None, :] % NY) / NY
    parts = []
    for value in (np.cos(angle), np.sin(angle)):
        parts.extend(part.astype(np.float32) for part in halves(value))
    stack = np.stack(parts)
    mine = stack.reshape(4, MY, GY, YL).transpose(2, 0, 1, 3)
    tables["ty"] = np.tile(mine, (1, 1, 1, 8))
    tables["tyi"] = np.repeat(mine.transpose(0, 1, 3, 2), 8, axis=3)
    angle = 2 * np.pi * (kept(MZ, NZ)[:, None] * np.arange(NZ)[None, :] % NZ) / NZ
    high, low = halves(np.concatenate([np.cos(angle), np.sin(angle)], axis=0))
    tables["tz"] = np.concatenate([high, low], axis=0)
    scale = (NX * NY * NZ) ** -0.5 * (2.0 * MX * MY * MZ) ** -0.5
    both = np.concatenate([np.cos(angle), np.sin(angle)], axis=0).T * scale
    high, low = halves(both)
    tables["tzi"] = np.concatenate(
        [high.reshape(ZC, W, 32), low.reshape(ZC, W, 32)], axis=1
    ).astype(np.float32)
    row = np.arange(128)[:, None]
    col = np.arange(512)[None, :]
    tables["te"] = (
        (row // 32 == col // 128) & (row % 32 // 8 == col % 64 // 16) & (row % 8 == col % 8)
    ).astype(ml_dtypes.bfloat16)
    weight = np.where(np.arange(MX) == 0, 1.0, 2.0)[:, None]
    angle = 2 * np.pi * (np.arange(MX)[:, None] * np.arange(NX)[None, :] % NX) / NX
    cos = (weight * np.cos(angle)).reshape(4, 8, NX)
    sin = (weight * np.sin(angle)).reshape(4, 8, NX)
    from_c = np.stack([cos, -sin], axis=1).reshape(64, NX)
    from_s = np.stack([-sin, -cos], axis=1).reshape(64, NX)
    zero = np.zeros_like(from_c)
    txi = np.block([[from_c, zero], [zero, from_c], [from_s, zero], [zero, from_s]])
    tables["txi"] = np.stack(halves(txi))
    return tables


TABLES = make_tables()


def split(value):
    high = value.astype(BF16)
    return high, (value - high.astype(F32)).astype(BF16)


def dot(left, right):
    return jnp.dot(left, right, preferred_element_type=F32)


def iota(shape, dim):
    return lax.broadcasted_iota(jnp.int32, shape, dim)


def swapped(value):
    pieces = []
    for k in range(value.shape[1] // 128):
        piece = value[:, k * 128 : (k + 1) * 128]
        real_lane = iota(piece.shape, 1) % 16 < 8
        pieces.append(jnp.where(real_lane, pltpu.roll(piece, 120, 1), -pltpu.roll(piece, 8, 1)))
    return jnp.concatenate(pieces, axis=1)


def moved(value, blocks):
    return value if blocks % 8 == 0 else pltpu.roll(value, blocks % 8 * 16, 1)


def wide_kernel(
    field3, filt, depth_w, point_w, tx, ty, tz, tzi, te,
    tiles_out, point_out,
    fv, pad, edge, hrow, xh, xl, yout, send1, recv1, tmp, send2, agbuf, gains,
    fscr, ftile, fbuf, tmp3, depth, pacc,
    ld_sem, s1, r1, sf, rf, sh, rh, sz, rz, s2, r2, s3, r3, so,
):
    gz = lax.axis_index("gz")
    gy = lax.axis_index("gy")
    zc = gz // W
    w = gz % W
    core = gz % 2
    me = gy * W + w

    def plane_peer(i):
        t = (me + i) % 32
        return (zc * W + t % W, t // W), t

    def ring_peer(i):
        return ((zc + i) % ZC) * W + w

    def halo_peer(dz, dy):
        return ((gz + NZ + dz) % NZ, (gy + GY + dy) % GY)

    barrier = pltpu.get_barrier_semaphore()

    def signal(target):
        pl.semaphore_signal(barrier, inc=1, device_id=target, device_id_type=MESH)

    def greet_ring(i, carry):
        signal((ring_peer(i), gy))
        return carry

    def greet_plane(i, carry):
        signal(plane_peer(i)[0])
        return carry

    lax.fori_loop(1, ZC, greet_ring, 0)
    for dz in (-1, 1):
        for dy in (-1, 0, 1):
            signal(halo_peer(dz, dy))
    lax.fori_loop(1, 32, greet_plane, 0)

    load = pltpu.make_async_copy(field3, fv, ld_sem.at[0])
    load.start()
    load_mid = pltpu.make_async_copy(field3, pad.at[1, :, 8:40, :], ld_sem.at[1])
    load_mid.start()

    fscr[...] = jnp.zeros_like(fscr)
    fscr[:, 0:8] = filt[...]
    tile = jnp.zeros((8, 128), F32)
    for b in range(4):
        for ky in range(4):
            piece = fscr[pl.ds(b * 32 + ky, 8, stride=4), :]
            shift = b * 32 + ky * 8
            tile = tile + (piece if shift == 0 else pltpu.roll(piece, shift, 1))
    ftile[...] = tile

    load.wait()
    for side, row in ((0, YL - 1), (1, 0)):
        edge[side] = fv[:, row, :]

    for p in range(2):
        total = None
        for ml in range(2):
            g = 2 * ml + p
            rows = jnp.concatenate(
                [fv[4 * s + g] for s in range(8)], axis=0
            )
            high, low = split(rows)
            value = dot(high, tx[0, ml]) + dot(low, tx[0, ml]) + dot(high, tx[1, ml])
            total = value if total is None else total + value
        high, low = split(total)
        for part in range(2):
            xh[part * 256 : (part + 1) * 256, p * 128 : (p + 1) * 128] = high[:, part * 128 : (part + 1) * 128]
            xl[part * 256 : (part + 1) * 256, p * 128 : (p + 1) * 128] = low[:, part * 128 : (part + 1) * 128]
    same = iota((MY, 8, 256), 1) == iota((MY, 8, 256), 2) // YL

    def spread(which):
        base = ty[gy, which]
        wide = jnp.where(same, jnp.broadcast_to(base[:, None, :], (MY, 8, 256)), 0.0)
        return wide.reshape(128, 256).astype(BF16)

    y_high = jnp.concatenate([spread(0), spread(2)], axis=1)
    y_low = jnp.concatenate([spread(1), spread(3)], axis=1)
    y_both = jnp.concatenate([y_high, y_low], axis=0)
    result = dot(y_both, xh[...]) + dot(y_both, xl[...])
    yout[...] = result[0:128] + result[128:256]
    block = iota((8, 128), 1) // 16 % 4
    for p in range(2):
        for q in range(4):
            quad = [
                yout[(q * 4 + ky) * 8 : (q * 4 + ky + 1) * 8, p * 128 : (p + 1) * 128]
                for ky in range(4)
            ]
            for kxb in range(4):
                out = moved(quad[0], 0 - kxb)
                for ky in range(1, 4):
                    out = jnp.where(block == ky, moved(quad[ky], ky - kxb), out)
                send1[q * 8 + p * 4 + kxb] = out

    pl.semaphore_wait(barrier, 15 + 6 + 31)

    def copy1(i):
        target, t = plane_peer(i)
        return pltpu.make_async_remote_copy(
            send1.at[t], recv1.at[me], s1, r1, device_id=target, device_id_type=MESH
        )

    def start1(i, carry):
        copy1(i).start()
        return carry

    lax.fori_loop(1, 32, start1, 0)
    own1 = pltpu.make_async_copy(send1.at[me], recv1.at[me], r1)
    own1.start()

    def copyf(i):
        return pltpu.make_async_remote_copy(
            ftile, fbuf.at[zc], sf, rf, device_id=(ring_peer(i), gy), device_id_type=MESH
        )

    def startf(i, carry):
        copyf(i).start()
        return carry

    def copy_row(dz, side):
        dy = 1 if side == 0 else -1
        slot = (1 - dz) * 2 + side
        return pltpu.make_async_remote_copy(
            edge.at[side], hrow.at[slot], sh, rh.at[0 if dz == 0 else 1],
            device_id=halo_peer(dz, dy), device_id_type=MESH,
        )

    def copy_plane(dz):
        return pltpu.make_async_remote_copy(
            field3, pad.at[1 - dz, :, 8:40, :], sz, rz.at[1 - dz],
            device_id=halo_peer(dz, 0), device_id_type=MESH,
        )

    for side in range(2):
        copy_row(0, side).start()
    for dz in (-1, 1):
        copy_plane(dz).start()
    for dz in (-1, 1):
        for side in range(2):
            copy_row(dz, side).start()
    lax.fori_loop(1, ZC, startf, 0)
    own_f = pltpu.make_async_copy(ftile, fbuf.at[zc], rf)
    own_f.start()

    def put_rows(plane, slot):
        pad[plane, :, 7, :] = hrow[slot]
        pad[plane, :, 40, :] = hrow[slot + 1]

    def conv(plane, first):
        def channel(c, carry):
            sums = [None, None, None]
            for b in range(3):
                window = pad[plane, c, 7 + b : 39 + b, :]
                for e in range(3):
                    term = depth_w[c, plane * 9 + b * 3 + e] * window
                    sums[e] = term if sums[e] is None else sums[e] + term
            value = sums[1] + pltpu.roll(sums[0], 1, 1) + pltpu.roll(sums[2], NX - 1, 1)
            depth[c] = value if first else depth[c] + value
            return carry

        lax.fori_loop(0, C, channel, 0)

    load_mid.wait()

    def wait_rows(index, count):
        part = hrow.at[0:count]
        pltpu.make_async_copy(part, part, rh.at[index]).wait()

    wait_rows(0, 2)
    put_rows(1, 2)
    conv(1, True)

    pltpu.make_async_copy(recv1, recv1, r1).wait()
    for k in range(W):
        tmp[k * 8 : (k + 1) * 8, :] = (recv1[k] + recv1[8 + k]) + (recv1[16 + k] + recv1[24 + k])
    for s in range(8):
        send2[:, s * 128 : (s + 1) * 128] = tmp[pl.ds(s, 8, stride=8), :]

    def far_first(k):
        return 8 + (k + 1) // 2 * (2 * (k % 2) - 1)

    def copy2(k):
        return pltpu.make_async_remote_copy(
            send2, agbuf.at[zc], s2, r2, device_id=(ring_peer(far_first(k)), gy), device_id_type=MESH
        )

    def start2(k, carry):
        copy2(k).start()
        return carry

    lax.fori_loop(0, ZC - 1, start2, 0)
    own2 = pltpu.make_async_copy(send2, agbuf.at[zc], r2)
    own2.start()

    pltpu.make_async_copy(fbuf, fbuf, rf).wait()
    raw = fbuf[...].reshape(128, 128)
    high = raw.astype(BF16)
    rest = raw - high.astype(F32)
    mid = rest.astype(BF16)
    low = (rest - mid.astype(F32)).astype(BF16)
    wide = dot(high, te[...]) + dot(mid, te[...]) + dot(low, te[...])
    lower = iota((8, 128), 1) < 64
    for part in range(2):
        for h in range(2):
            lanes = slice((part * 2 + h) * 128, (part * 2 + h + 1) * 128)
            for s in range(8):
                gains[part, h * 8 : (h + 1) * 8, s * 128 : (s + 1) * 128] = jnp.where(
                    lower, wide[s * 16 : s * 16 + 8, lanes], wide[s * 16 + 8 : s * 16 + 16, lanes]
                )

    wait_rows(1, 4)
    near = jnp.where(core == 0, 2, 0)
    far = 2 - near
    pltpu.make_async_copy(field3, pad.at[near, :, 8:40, :], rz.at[near]).wait()
    put_rows(near, near * 2)
    conv(near, False)

    pltpu.make_async_copy(agbuf, agbuf, r2).wait()
    a_high, a_low = split(agbuf[...].reshape(NZ, 1024))
    both = dot(tz[...], a_high) + dot(tz[...], a_low)
    modes = both[0:16] + both[32:48] + swapped(both[16:32] + both[48:64])
    filtered = modes * gains[0] - swapped(modes) * gains[1]
    stacked = jnp.concatenate([filtered, -swapped(filtered)], axis=0)
    f_high, f_low = split(stacked)
    table = tzi[zc].astype(BF16)
    both = dot(table, f_high) + dot(table, f_low)
    back = both[0:8] + both[8:16]
    for s in range(8):
        tmp3[pl.ds(s, 8, stride=8), :] = back[:, s * 128 : (s + 1) * 128]

    def copy3(i):
        target, t = plane_peer(i)
        return pltpu.make_async_remote_copy(
            tmp3.at[pl.ds(pl.multiple_of(t % W * 8, 8), 8), :], tiles_out.at[w * 4 + gy], s3, r3,
            device_id=target, device_id_type=MESH,
        )

    def start3(i, carry):
        copy3(i).start()
        return carry

    lax.fori_loop(1, 32, start3, 0)
    own3 = pltpu.make_async_copy(
        tmp3.at[pl.ds(pl.multiple_of(w * 8, 8), 8), :], tiles_out.at[w * 4 + gy], r3
    )
    own3.start()

    pltpu.make_async_copy(field3, pad.at[far, :, 8:40, :], rz.at[far]).wait()
    put_rows(far, far * 2)
    conv(far, False)

    grow = (iota((256, C), 0) // 8 == iota((256, C), 1)).astype(F32).astype(BF16)
    grow_t = (iota((C, 256), 1) // 8 == iota((C, 256), 0)).astype(F32).astype(BF16)
    diagonal = iota((256, 256), 0) % 8 == iota((256, 256), 1) % 8
    mixers = []
    for part in split(point_w[...]):
        tall = dot(grow, part).astype(BF16)
        mixers.append(jnp.where(diagonal, dot(tall, grow_t), 0.0).astype(BF16))
    for k in range(YL // 8):
        d_high, d_low = split(depth[:, k * 8 : (k + 1) * 8, :].reshape(256, NX))
        value = dot(mixers[0], d_high) + dot(mixers[0], d_low) + dot(mixers[1], d_high)
        pacc[:, k * 8 : (k + 1) * 8, :] = value.reshape(C, 8, NX)
    put = pltpu.make_async_copy(pacc, point_out, so)
    put.start()

    pltpu.make_async_copy(tiles_out, tiles_out, r3).wait()
    put.wait()

    def done1(i, carry):
        copy1(i).wait_send()
        copy3(i).wait_send()
        return carry

    def done2(k, carry):
        copy2(k).wait_send()
        return carry

    def donef(i, carry):
        copyf(i).wait_send()
        return carry

    lax.fori_loop(1, 32, done1, 0)
    lax.fori_loop(0, ZC - 1, done2, 0)
    lax.fori_loop(1, ZC, donef, 0)
    for dz in (-1, 0, 1):
        for side in range(2):
            copy_row(dz, side).wait_send()
    for dz in (-1, 1):
        copy_plane(dz).wait_send()


def last_kernel(tiles, point, bias, tyi, txi, out, yh, yl):
    step = pl.program_id(0)
    gy = lax.axis_index("gy")

    @pl.when(step == 0)
    def _():
        block = iota((8, 128), 1) // 16 % 4
        columns = []
        for p in range(2):
            rows = []
            for ky in range(MY):
                q, k4 = ky // 4, ky % 4
                value = moved(tiles[p * 16 + q], 0 - k4)
                for kxb in range(1, 4):
                    value = jnp.where(block == kxb, moved(tiles[(p * 4 + kxb) * 4 + q], kxb - k4), value)
                rows.append(value)
            columns.append(jnp.concatenate(rows, axis=0))
        r_high, r_low = split(jnp.concatenate(columns, axis=1))
        same = iota((8, YL, 128), 0) == iota((8, YL, 128), 2) % 8

        def spread(which):
            base = tyi[gy, which]
            wide = jnp.where(same, jnp.broadcast_to(base[None], (8, YL, 128)), 0.0)
            return wide.reshape(256, 128).astype(BF16)

        t_high = jnp.concatenate([spread(0), spread(2)], axis=0)
        t_low = jnp.concatenate([spread(1), spread(3)], axis=0)
        value = dot(t_high, r_high) + dot(t_high, r_low) + dot(t_low, r_high)
        high, low = split(value)
        yh[...] = high
        yl[...] = low

    def gathered(ref):
        start = pl.multiple_of(step * 64, 64)
        real = ref[pl.ds(start, 64), :]
        imag = ref[pl.ds(256 + start, 64), :]
        return jnp.concatenate(
            [
                jnp.concatenate([real[:, p * 128 : (p + 1) * 128], imag[:, p * 128 : (p + 1) * 128]], axis=1)
                for p in range(2)
            ],
            axis=0,
        )

    high, low = gathered(yh), gathered(yl)
    spectral = dot(high, txi[0]) + dot(low, txi[0]) + dot(high, txi[1])
    for p in range(2):
        for sl in range(2):
            for ml in range(2):
                ch = 4 * sl + 2 * ml + p
                value = spectral[p * 64 + sl * 32 : p * 64 + (sl + 1) * 32, ml * 256 : (ml + 1) * 256]
                value = value + point[ch] + bias[step * 8 + ch]
                out[ch] = 0.5 * value * (1.0 + lax.erf(value * (0.5**0.5)))


def body(field, spectral_filter, depth_weight, point_weight, bias_vector):
    field3 = field.reshape(C, YL, NX)
    filt = spectral_filter.reshape(128, 8)
    const = {name: jnp.asarray(value) for name, value in TABLES.items()}
    vmem = pl.BlockSpec(memory_space=pltpu.VMEM)
    smem = pl.BlockSpec(memory_space=pltpu.SMEM)
    hbm = pl.BlockSpec(memory_space=pl.ANY)
    tiles, point = pl.pallas_call(
        wide_kernel,
        name="wide",
        out_shape=(
            jax.ShapeDtypeStruct((32, 8, 128), F32),
            jax.ShapeDtypeStruct((C, YL, NX), F32),
        ),
        in_specs=[hbm, vmem, smem, vmem, vmem, vmem, vmem, vmem, vmem],
        out_specs=(hbm, hbm),
        scratch_shapes=[
            VMEM((C, YL, NX), F32),
            VMEM((3, C, 48, NX), F32),
            VMEM((2, C, NX), F32),
            VMEM((6, C, NX), F32),
            VMEM((512, 256), BF16),
            VMEM((512, 256), BF16),
            VMEM((128, 256), F32),
            VMEM((32, 8, 128), F32),
            VMEM((32, 8, 128), F32),
            VMEM((64, 128), F32),
            VMEM((8, 1024), F32),
            VMEM((ZC, 8, 1024), F32),
            VMEM((2, 16, 1024), F32),
            VMEM((128, 128), F32),
            VMEM((8, 128), F32),
            VMEM((ZC, 8, 128), F32),
            VMEM((64, 128), F32),
            VMEM((C, YL, NX), F32),
            VMEM((C, YL, NX), F32),
            DMA((2,)), DMA, DMA, DMA, DMA, DMA, DMA((2,)), DMA, DMA((3,)), DMA, DMA, DMA, DMA, DMA,
        ],
        compiler_params=pltpu.CompilerParams(
            collective_id=0, has_side_effects=True, vmem_limit_bytes=40 * 1024 * 1024
        ),
    )(
        field3, filt, depth_weight, point_weight,
        const["tx"], const["ty"], const["tz"], const["tzi"], const["te"],
    )
    out = pl.pallas_call(
        last_kernel,
        name="last",
        out_shape=jax.ShapeDtypeStruct((C, YL, NX), F32),
        grid=(4,),
        in_specs=[
            vmem,
            pl.BlockSpec((8, YL, NX), lambda i: (i, 0, 0)),
            smem,
            vmem,
            vmem,
        ],
        out_specs=pl.BlockSpec((8, YL, NX), lambda i: (i, 0, 0)),
        scratch_shapes=[VMEM((512, 256), BF16), VMEM((512, 256), BF16)],
        compiler_params=pltpu.CompilerParams(dimension_semantics=("arbitrary",)),
    )(tiles, point, bias_vector, const["tyi"], const["txi"])
    return out.reshape(C, 1, YL, NX)


def solution(mesh):
    in_specs = (P(None, "gz", "gy", None), P(None, None, "gy", "gz"), P(), P(), P())
    out_specs = P(None, "gz", "gy", None)
    return jax.shard_map(body, mesh=mesh, in_specs=in_specs, out_specs=out_specs, check_vma=False)
```

```python
import functools

import jax
import jax.numpy as jnp
import ml_dtypes
import numpy as np
from jax import lax
from jax.experimental import pallas as pl
from jax.experimental.pallas import tpu as pltpu
from jax.sharding import PartitionSpec as P

C = 32
NX = 256
NY = 128
NZ = 128
MX = 32
MY = 16
MZ = 16
GY = 4
ZC = 16
W = 8
YL = NY // GY
VMEM_ALL = 67043328
MESH = pl.DeviceIdType.MESH
F32 = jnp.float32
BF16 = jnp.bfloat16
VMEM = pltpu.VMEM
DMA = pltpu.SemaphoreType.DMA


def halves(table):
    high = table.astype(ml_dtypes.bfloat16)
    low = (table - high.astype(np.float64)).astype(ml_dtypes.bfloat16)
    return high, low


def kept(count, total):
    series = np.arange(count)
    return np.where(series < count // 2, series, total - count + series)


def make_tables():
    tables = {}
    angle = 2 * np.pi * (np.arange(NX)[:, None] * np.arange(MX)[None, :] % NX) / NX
    cos = np.cos(angle).reshape(NX, 4, 8)
    sin = np.sin(angle).reshape(NX, 4, 8)
    plain = np.stack([cos, -sin], axis=2).reshape(NX, 64)
    swapped = np.stack([-sin, -cos], axis=2).reshape(NX, 64)
    zero = np.zeros_like(plain)
    tx = np.stack(
        [
            np.concatenate([plain, zero, swapped, zero], axis=1),
            np.concatenate([zero, plain, zero, swapped], axis=1),
        ]
    )
    tables["tx"] = np.stack(halves(tx))
    places = np.arange(NY)
    angle = 2 * np.pi * (kept(MY, NY)[:, None] * places[None, :] % NY) / NY
    parts = []
    for value in (np.cos(angle), np.sin(angle)):
        parts.extend(part.astype(np.float32) for part in halves(value))
    stack = np.stack(parts)
    mine = stack.reshape(4, MY, GY, YL).transpose(2, 0, 1, 3)
    tables["ty"] = np.tile(mine, (1, 1, 1, 8))
    tables["tyi"] = np.repeat(mine.transpose(0, 1, 3, 2), 8, axis=3)
    angle = 2 * np.pi * (kept(MZ, NZ)[:, None] * np.arange(NZ)[None, :] % NZ) / NZ
    high, low = halves(np.concatenate([np.cos(angle), np.sin(angle)], axis=0))
    both = np.concatenate([high, low], axis=0).reshape(64, ZC, 2, 4)
    tables["tz"] = both.transpose(2, 0, 1, 3).reshape(128, 64)
    scale = (NX * NY * NZ) ** -0.5 * (2.0 * MX * MY * MZ) ** -0.5
    both = np.concatenate([np.cos(angle), np.sin(angle)], axis=0).T * scale
    both = both.reshape(ZC, 2, 4, 32).transpose(1, 0, 2, 3).reshape(128, 32)
    tables["tzi"] = np.concatenate(halves(both), axis=0)
    weight = np.where(np.arange(MX) == 0, 1.0, 2.0)[:, None]
    angle = 2 * np.pi * (np.arange(MX)[:, None] * np.arange(NX)[None, :] % NX) / NX
    cos = (weight * np.cos(angle)).reshape(4, 8, NX)
    sin = (weight * np.sin(angle)).reshape(4, 8, NX)
    from_c = np.stack([cos, -sin], axis=1).reshape(64, NX)
    from_s = np.stack([-sin, -cos], axis=1).reshape(64, NX)
    zero = np.zeros_like(from_c)
    txi = np.block([[from_c, zero], [zero, from_c], [from_s, zero], [zero, from_s]])
    tables["txi"] = np.stack(halves(txi))
    return tables


TABLES = make_tables()


def split(value):
    high = value.astype(BF16)
    return high, (value - high.astype(F32)).astype(BF16)


def dot(left, right):
    return jnp.dot(left, right, preferred_element_type=F32)


def iota(shape, dim):
    return lax.broadcasted_iota(jnp.int32, shape, dim)


def swapped(value):
    pieces = []
    for k in range(value.shape[1] // 128):
        piece = value[:, k * 128 : (k + 1) * 128]
        real_lane = iota(piece.shape, 1) % 16 < 8
        pieces.append(jnp.where(real_lane, pltpu.roll(piece, 120, 1), -pltpu.roll(piece, 8, 1)))
    return jnp.concatenate(pieces, axis=1)


def moved(value, blocks):
    return value if blocks % 8 == 0 else pltpu.roll(value, blocks % 8 * 16, 1)


def wide_kernel(
    field3, filt_in, depth_in, point_in, tx_in, ty_in, tz_in, tzi_in,
    tiles_out, point_out,
    fv, filt, depth_w, point_w, tx, ty, tz, tzi,
    pad, edge, hrow, xh, xl, yout, send1, recv1, tmp, send2, recv2, gains,
    send4, recv4, tmp4, tmp3, depth, pacc,
    ld_sem, s1, r1, sh, rh, sz, rz, s2, r2, s4, r4, s3, r3, so,
):
    gz = lax.axis_index("gz")
    gy = lax.axis_index("gy")
    zc = gz // W
    w = gz % W
    core = gz % 2
    me = gy * W + w

    def plane_peer(i):
        t = (me + i) % 32
        return (zc * W + t % W, t // W), t

    def ring_peer(i):
        return ((zc + i) % ZC) * W + w

    def halo_peer(dz, dy):
        return ((gz + NZ + dz) % NZ, (gy + GY + dy) % GY)

    barrier = pltpu.get_barrier_semaphore()

    def signal(target):
        pl.semaphore_signal(barrier, inc=1, device_id=target, device_id_type=MESH)

    def greet_ring(i, carry):
        signal((ring_peer(i), gy))
        return carry

    def greet_plane(i, carry):
        signal(plane_peer(i)[0])
        return carry

    lax.fori_loop(1, ZC, greet_ring, 0)
    for dz in (-1, 1):
        for dy in (-1, 0, 1):
            signal(halo_peer(dz, dy))
    lax.fori_loop(1, 32, greet_plane, 0)

    loads = [
        pltpu.make_async_copy(src, dst, ld_sem.at[k])
        for k, (src, dst) in enumerate(
            [
                (field3, fv),
                (tx_in, tx),
                (ty_in.at[gy], ty),
                (field3, pad.at[1, :, 8:40, :]),
                (filt_in, filt),
                (depth_in, depth_w),
                (point_in, point_w),
                (tz_in, tz),
                (tzi_in, tzi),
            ]
        )
    ]
    for load in loads:
        load.start()
    loads[0].wait()
    for side, row in ((0, YL - 1), (1, 0)):
        edge[side] = fv[:, row, :]

    loads[1].wait()
    loads[2].wait()
    for p in range(2):
        total = None
        for ml in range(2):
            g = 2 * ml + p
            rows = jnp.concatenate(
                [fv[4 * s + g] for s in range(8)], axis=0
            )
            high, low = split(rows)
            value = dot(high, tx[0, ml]) + dot(low, tx[0, ml]) + dot(high, tx[1, ml])
            total = value if total is None else total + value
        high, low = split(total)
        for part in range(2):
            xh[part * 256 : (part + 1) * 256, p * 128 : (p + 1) * 128] = high[:, part * 128 : (part + 1) * 128]
            xl[part * 256 : (part + 1) * 256, p * 128 : (p + 1) * 128] = low[:, part * 128 : (part + 1) * 128]
    same = iota((MY, 8, 256), 1) == iota((MY, 8, 256), 2) // YL

    def spread(which):
        base = ty[which]
        wide = jnp.where(same, jnp.broadcast_to(base[:, None, :], (MY, 8, 256)), 0.0)
        return wide.reshape(128, 256).astype(BF16)

    y_high = jnp.concatenate([spread(0), spread(2)], axis=1)
    y_low = jnp.concatenate([spread(1), spread(3)], axis=1)
    y_both = jnp.concatenate([y_high, y_low], axis=0)
    result = dot(y_both, xh[...]) + dot(y_both, xl[...])
    yout[...] = result[0:128] + result[128:256]
    block = iota((8, 128), 1) // 16 % 4
    for p in range(2):
        for q in range(4):
            quad = [
                yout[(q * 4 + ky) * 8 : (q * 4 + ky + 1) * 8, p * 128 : (p + 1) * 128]
                for ky in range(4)
            ]
            for kxb in range(4):
                out = moved(quad[0], 0 - kxb)
                for ky in range(1, 4):
                    out = jnp.where(block == ky, moved(quad[ky], ky - kxb), out)
                send1[q * 8 + p * 4 + kxb] = out

    pl.semaphore_wait(barrier, 15 + 6 + 31)

    def copy1(i):
        target, t = plane_peer(i)
        return pltpu.make_async_remote_copy(
            send1.at[t], recv1.at[me], s1, r1, device_id=target, device_id_type=MESH
        )

    def start1(i, carry):
        copy1(i).start()
        return carry

    lax.fori_loop(1, 32, start1, 0)
    own1 = pltpu.make_async_copy(send1.at[me], recv1.at[me], r1)
    own1.start()

    def copy_row(dz, side):
        dy = 1 if side == 0 else -1
        slot = (1 - dz) * 2 + side
        return pltpu.make_async_remote_copy(
            edge.at[side], hrow.at[slot], sh, rh.at[0 if dz == 0 else 1],
            device_id=halo_peer(dz, dy), device_id_type=MESH,
        )

    def copy_plane(dz):
        return pltpu.make_async_remote_copy(
            field3, pad.at[1 - dz, :, 8:40, :], sz, rz.at[1 - dz],
            device_id=halo_peer(dz, 0), device_id_type=MESH,
        )

    for side in range(2):
        copy_row(0, side).start()
    for dz in (-1, 1):
        copy_plane(dz).start()
    for dz in (-1, 1):
        for side in range(2):
            copy_row(dz, side).start()
    for load in loads[4:]:
        load.wait()
    gains[...] = jnp.zeros_like(gains)
    for part in range(2):
        for ky in range(4):
            for r in range(2):
                row = part * 64 + ky * 16 + r * 8
                gains[row : row + 8, 0:16] = filt[part * 32 + ky * 8 : part * 32 + ky * 8 + 8, :]

    def put_rows(plane, slot):
        pad[plane, :, 7, :] = hrow[slot]
        pad[plane, :, 40, :] = hrow[slot + 1]

    def conv(plane, first):
        def channels(step, carry):
            for k in range(4):
                c = step * 4 + k
                sums = [None, None, None]
                for b in range(3):
                    window = pad[plane, c, 7 + b : 39 + b, :]
                    for e in range(3):
                        term = depth_w[c, plane * 9 + b * 3 + e] * window
                        sums[e] = term if sums[e] is None else sums[e] + term
                value = sums[1] + pltpu.roll(sums[0], 1, 1) + pltpu.roll(sums[2], NX - 1, 1)
                depth[c] = value if first else depth[c] + value
            return carry

        lax.fori_loop(0, C // 4, channels, 0)

    loads[3].wait()

    def wait_rows(index, count):
        part = hrow.at[0:count]
        pltpu.make_async_copy(part, part, rh.at[index]).wait()

    wait_rows(0, 2)
    put_rows(1, 2)
    conv(1, True)

    pltpu.make_async_copy(recv1, recv1, r1).wait()
    for k in range(W):
        tmp[k * 8 : (k + 1) * 8, :] = (recv1[k] + recv1[8 + k]) + (recv1[16 + k] + recv1[24 + k])
    lower = iota((8, 128), 1) < 64
    for s in range(8):
        part = tmp[pl.ds(s, 8, stride=8), :]
        turned = pltpu.roll(part, 64, 1)
        send2[2 * s] = jnp.where(lower[0:4], part[0:4], turned[4:8])
        send2[2 * s + 1] = jnp.where(lower[0:4], turned[0:4], part[4:8])

    def far_first(k):
        return 8 + (k + 1) // 2 * (2 * (k % 2) - 1)

    def copy2(k, src, dst, ssem, rsem):
        i = far_first(k)
        return pltpu.make_async_remote_copy(
            src.at[(zc + i) % ZC], dst.at[zc], ssem, rsem,
            device_id=(ring_peer(i), gy), device_id_type=MESH,
        )

    def start2(k, carry):
        copy2(k, send2, recv2, s2, r2).start()
        return carry

    lax.fori_loop(0, ZC - 1, start2, 0)
    own2 = pltpu.make_async_copy(send2.at[zc], recv2.at[zc], r2)
    own2.start()

    wait_rows(1, 4)
    near = jnp.where(core == 0, 2, 0)
    far = 2 - near
    pltpu.make_async_copy(field3, pad.at[near, :, 8:40, :], rz.at[near]).wait()
    put_rows(near, near * 2)
    conv(near, False)

    pltpu.make_async_copy(recv2, recv2, r2).wait()
    a_high, a_low = split(recv2[...].reshape(64, 128))
    both = dot(tz[...], a_high) + dot(tz[...], a_low)
    both = both[0:64] + pltpu.roll(both[64:128], 64, 1)
    modes = both[0:16] + both[32:48] + swapped(both[16:32] + both[48:64])
    turned = jnp.transpose(gains[...])[0:16, :]
    filtered = modes * turned - swapped(modes) * pltpu.roll(turned, 64, 1)
    stacked = jnp.concatenate([filtered, -swapped(filtered)], axis=0)
    f_high, f_low = split(stacked)
    both = dot(tzi[...], f_high) + dot(tzi[...], f_low)
    both = both[0:128] + both[128:256]
    back = jnp.where(iota((64, 128), 1) < 64, both[0:64], pltpu.roll(both[64:128], 64, 1))
    send4[...] = back.reshape(ZC, 4, 128)

    def start4(k, carry):
        copy2(k, send4, recv4, s4, r4).start()
        return carry

    lax.fori_loop(0, ZC - 1, start4, 0)
    own4 = pltpu.make_async_copy(send4.at[zc], recv4.at[zc], r4)
    own4.start()

    pltpu.make_async_copy(field3, pad.at[far, :, 8:40, :], rz.at[far]).wait()
    put_rows(far, far * 2)
    conv(far, False)

    pltpu.make_async_copy(recv4, recv4, r4).wait()
    tmp4[...] = recv4[...].reshape(64, 128)
    for i in range(4):
        even = tmp4[pl.ds(i, 8, stride=8), :]
        odd = tmp4[pl.ds(4 + i, 8, stride=8), :]
        tmp3[i] = jnp.where(lower, even, pltpu.roll(odd, 64, 1))
        tmp3[4 + i] = jnp.where(lower, pltpu.roll(even, 64, 1), odd)

    def copy3(i):
        target, t = plane_peer(i)
        return pltpu.make_async_remote_copy(
            tmp3.at[t % W], tiles_out.at[w * 4 + gy], s3, r3,
            device_id=target, device_id_type=MESH,
        )

    def start3(i, carry):
        copy3(i).start()
        return carry

    lax.fori_loop(1, 32, start3, 0)
    own3 = pltpu.make_async_copy(
        tmp3.at[w], tiles_out.at[w * 4 + gy], r3
    )
    own3.start()

    grow = (iota((256, C), 0) // 8 == iota((256, C), 1)).astype(F32).astype(BF16)
    grow_t = (iota((C, 256), 1) // 8 == iota((C, 256), 0)).astype(F32).astype(BF16)
    diagonal = iota((256, 256), 0) % 8 == iota((256, 256), 1) % 8
    mixers = []
    for part in split(point_w[...]):
        tall = dot(grow, part).astype(BF16)
        mixers.append(jnp.where(diagonal, dot(tall, grow_t), 0.0).astype(BF16))
    for k in range(YL // 8):
        d_high, d_low = split(depth[:, k * 8 : (k + 1) * 8, :].reshape(256, NX))
        value = dot(mixers[0], d_high) + dot(mixers[0], d_low) + dot(mixers[1], d_high)
        pacc[:, k * 8 : (k + 1) * 8, :] = value.reshape(C, 8, NX)
    put = pltpu.make_async_copy(pacc, point_out, so)
    put.start()

    pltpu.make_async_copy(tiles_out, tiles_out, r3).wait()
    put.wait()

    def done1(i, carry):
        copy1(i).wait_send()
        copy3(i).wait_send()
        return carry

    def done2(k, carry):
        copy2(k, send2, recv2, s2, r2).wait_send()
        copy2(k, send4, recv4, s4, r4).wait_send()
        return carry

    lax.fori_loop(1, 32, done1, 0)
    lax.fori_loop(0, ZC - 1, done2, 0)
    for dz in (-1, 0, 1):
        for side in range(2):
            copy_row(dz, side).wait_send()
    for dz in (-1, 1):
        copy_plane(dz).wait_send()


def last_kernel(tiles, point, bias, tyi, txi, out, yh, yl):
    step = pl.program_id(0)
    gy = lax.axis_index("gy")

    @pl.when(step == 0)
    def _():
        block = iota((8, 128), 1) // 16 % 4
        columns = []
        for p in range(2):
            rows = []
            for ky in range(MY):
                q, k4 = ky // 4, ky % 4
                value = moved(tiles[p * 16 + q], 0 - k4)
                for kxb in range(1, 4):
                    value = jnp.where(block == kxb, moved(tiles[(p * 4 + kxb) * 4 + q], kxb - k4), value)
                rows.append(value)
            columns.append(jnp.concatenate(rows, axis=0))
        r_high, r_low = split(jnp.concatenate(columns, axis=1))
        same = iota((8, YL, 128), 0) == iota((8, YL, 128), 2) % 8

        def spread(which):
            base = tyi[gy, which]
            wide = jnp.where(same, jnp.broadcast_to(base[None], (8, YL, 128)), 0.0)
            return wide.reshape(256, 128).astype(BF16)

        t_high = jnp.concatenate([spread(0), spread(2)], axis=0)
        t_low = jnp.concatenate([spread(1), spread(3)], axis=0)
        value = dot(t_high, r_high) + dot(t_high, r_low) + dot(t_low, r_high)
        high, low = split(value)
        yh[...] = high
        yl[...] = low

    def gathered(ref):
        start = pl.multiple_of(step * 64, 64)
        real = ref[pl.ds(start, 64), :]
        imag = ref[pl.ds(256 + start, 64), :]
        return jnp.concatenate(
            [
                jnp.concatenate([real[:, p * 128 : (p + 1) * 128], imag[:, p * 128 : (p + 1) * 128]], axis=1)
                for p in range(2)
            ],
            axis=0,
        )

    high, low = gathered(yh), gathered(yl)
    spectral = dot(high, txi[0]) + dot(low, txi[0]) + dot(high, txi[1])
    for p in range(2):
        for sl in range(2):
            for ml in range(2):
                ch = 4 * sl + 2 * ml + p
                value = spectral[p * 64 + sl * 32 : p * 64 + (sl + 1) * 32, ml * 256 : (ml + 1) * 256]
                value = value + point[ch] + bias[step * 8 + ch]
                out[ch] = 0.5 * value * (1.0 + lax.erf(value * (0.5**0.5)))


def body(field, spectral_filter, depth_weight, point_weight, bias_vector):
    field3 = field.reshape(C, YL, NX)
    filt = spectral_filter.transpose(0, 2, 3, 1).reshape(64, 16)
    const = {name: jnp.asarray(value) for name, value in TABLES.items()}
    vmem = pl.BlockSpec(memory_space=pltpu.VMEM)
    smem = pl.BlockSpec(memory_space=pltpu.SMEM)
    hbm = pl.BlockSpec(memory_space=pltpu.HBM)
    tiles, point = pl.pallas_call(
        wide_kernel,
        name="wide",
        out_shape=(
            jax.ShapeDtypeStruct((32, 8, 128), F32),
            jax.ShapeDtypeStruct((C, YL, NX), F32),
        ),
        in_specs=[hbm] * 8,
        out_specs=(hbm, hbm),
        scratch_shapes=[
            VMEM((C, YL, NX), F32),
            VMEM((64, 16), F32),
            pltpu.SMEM((C, 27), F32),
            VMEM((C, C), F32),
            VMEM((2, 2, 256, 256), BF16),
            VMEM((4, MY, 256), F32),
            VMEM((128, 64), BF16),
            VMEM((256, 32), BF16),
            VMEM((3, C, 48, NX), F32),
            VMEM((2, C, NX), F32),
            VMEM((6, C, NX), F32),
            VMEM((512, 256), BF16),
            VMEM((512, 256), BF16),
            VMEM((128, 256), F32),
            VMEM((32, 8, 128), F32),
            VMEM((32, 8, 128), F32),
            VMEM((64, 128), F32),
            VMEM((ZC, 4, 128), F32),
            VMEM((ZC, 4, 128), F32),
            VMEM((128, 128), F32),
            VMEM((ZC, 4, 128), F32),
            VMEM((ZC, 4, 128), F32),
            VMEM((64, 128), F32),
            VMEM((W, 8, 128), F32),
            VMEM((C, YL, NX), F32),
            VMEM((C, YL, NX), F32),
            DMA((9,)), DMA, DMA, DMA, DMA((2,)), DMA, DMA((3,)), DMA, DMA, DMA, DMA, DMA, DMA, DMA,
        ],
        compiler_params=pltpu.CompilerParams(
            collective_id=0, has_side_effects=True, vmem_limit_bytes=VMEM_ALL
        ),
    )(
        field3, filt, depth_weight, point_weight,
        const["tx"], const["ty"], const["tz"], const["tzi"],
    )
    out = pl.pallas_call(
        last_kernel,
        name="last",
        out_shape=jax.ShapeDtypeStruct((C, YL, NX), F32),
        grid=(4,),
        in_specs=[
            vmem,
            pl.BlockSpec((8, YL, NX), lambda i: (i, 0, 0)),
            smem,
            vmem,
            vmem,
        ],
        out_specs=pl.BlockSpec((8, YL, NX), lambda i: (i, 0, 0)),
        scratch_shapes=[VMEM((512, 256), BF16), VMEM((512, 256), BF16)],
        compiler_params=pltpu.CompilerParams(dimension_semantics=("arbitrary",), vmem_limit_bytes=VMEM_ALL),
    )(tiles, point, bias_vector, const["tyi"], const["txi"])
    return out.reshape(C, 1, YL, NX)


def solution(mesh):
    in_specs = (P(None, "gz", "gy", None), P(None, None, "gy", "gz"), P(), P(), P())
    out_specs = P(None, "gz", "gy", None)
    return jax.shard_map(body, mesh=mesh, in_specs=in_specs, out_specs=out_specs, check_vma=False)
```

```python
import functools

import jax
import jax.numpy as jnp
import ml_dtypes
import numpy as np
from jax import lax
from jax.experimental import pallas as pl
from jax.experimental.pallas import tpu as pltpu
from jax.sharding import PartitionSpec as P

C = 32
NX = 256
NY = 128
NZ = 128
MX = 32
MY = 16
MZ = 16
GY = 4
ZC = 16
W = 8
YL = NY // GY
VMEM_ALL = 67043328
MESH = pl.DeviceIdType.MESH
F32 = jnp.float32
BF16 = jnp.bfloat16
VMEM = pltpu.VMEM
DMA = pltpu.SemaphoreType.DMA


def halves(table):
    high = table.astype(ml_dtypes.bfloat16)
    low = (table - high.astype(np.float64)).astype(ml_dtypes.bfloat16)
    return high, low


def kept(count, total):
    series = np.arange(count)
    return np.where(series < count // 2, series, total - count + series)


def make_tables():
    tables = {}
    angle = 2 * np.pi * (np.arange(NX)[:, None] * np.arange(MX)[None, :] % NX) / NX
    cos = np.cos(angle).reshape(NX, 4, 8)
    sin = np.sin(angle).reshape(NX, 4, 8)
    plain = np.stack([cos, -sin], axis=2).reshape(NX, 64)
    swapped = np.stack([-sin, -cos], axis=2).reshape(NX, 64)
    zero = np.zeros_like(plain)
    tx = np.stack(
        [
            np.concatenate([plain, zero, swapped, zero], axis=1),
            np.concatenate([zero, plain, zero, swapped], axis=1),
        ]
    )
    tables["tx"] = np.stack(halves(tx))
    places = np.arange(NY)
    angle = 2 * np.pi * (kept(MY, NY)[:, None] * places[None, :] % NY) / NY
    parts = []
    for value in (np.cos(angle), np.sin(angle)):
        parts.extend(part.astype(np.float32) for part in halves(value))
    stack = np.stack(parts)
    mine = stack.reshape(4, MY, GY, YL).transpose(2, 0, 1, 3)
    tables["ty"] = np.tile(mine, (1, 1, 1, 8))
    tables["tyi"] = np.repeat(mine.transpose(0, 1, 3, 2), 8, axis=3)
    angle = 2 * np.pi * (kept(MZ, NZ)[:, None] * np.arange(NZ)[None, :] % NZ) / NZ
    high, low = halves(np.concatenate([np.cos(angle), np.sin(angle)], axis=0))
    tables["tz"] = np.concatenate([high, low], axis=0)
    scale = (NX * NY * NZ) ** -0.5 * (2.0 * MX * MY * MZ) ** -0.5
    both = np.concatenate([np.cos(angle), np.sin(angle)], axis=0).T * scale
    tables["tzi"] = np.concatenate(halves(both), axis=0)
    weight = np.where(np.arange(MX) == 0, 1.0, 2.0)[:, None]
    angle = 2 * np.pi * (np.arange(MX)[:, None] * np.arange(NX)[None, :] % NX) / NX
    cos = (weight * np.cos(angle)).reshape(4, 8, NX)
    sin = (weight * np.sin(angle)).reshape(4, 8, NX)
    from_c = np.stack([cos, -sin], axis=1).reshape(64, NX)
    from_s = np.stack([-sin, -cos], axis=1).reshape(64, NX)
    zero = np.zeros_like(from_c)
    txi = np.block([[from_c, zero], [zero, from_c], [from_s, zero], [zero, from_s]])
    tables["txi"] = np.stack(halves(txi))
    return tables


TABLES = make_tables()


def split(value):
    high = value.astype(BF16)
    return high, (value - high.astype(F32)).astype(BF16)


def dot(left, right):
    return jnp.dot(left, right, preferred_element_type=F32)


def iota(shape, dim):
    return lax.broadcasted_iota(jnp.int32, shape, dim)


def swapped(value):
    pieces = []
    for k in range(value.shape[1] // 128):
        piece = value[:, k * 128 : (k + 1) * 128]
        real_lane = iota(piece.shape, 1) % 16 < 8
        pieces.append(jnp.where(real_lane, pltpu.roll(piece, 120, 1), -pltpu.roll(piece, 8, 1)))
    return jnp.concatenate(pieces, axis=1)


def moved(value, blocks):
    return value if blocks % 8 == 0 else pltpu.roll(value, blocks % 8 * 16, 1)


def wide_kernel(
    field3, filt_in, depth_in, point_in, tx_in, ty_in, tz_in, tzi_in,
    tiles_out, point_out,
    fv, filt, filt2, depth_w, point_w, tx, ty, tz, tzi,
    pad, edge, hrow, xh, xl, yout, send1, recv1, tmp, send2, recv2, gains,
    send4, recv4, tmp3, depth, pacc,
    ld_sem, s1, r1, sh, rh, sz, rz, s2, r2, s4, r4, s3, r3, so, sf, rf, tokens,
):
    gz = lax.axis_index("gz")
    gy = lax.axis_index("gy")
    zc = gz // W
    w = gz % W
    core = gz % 2
    me = gy * W + w

    def plane_peer(i):
        t = (me + i) % 32
        return (zc * W + t % W, t // W), t

    def ring_peer(i):
        return ((zc + i) % ZC) * W + w

    def halo_peer(dz, dy):
        return ((gz + NZ + dz) % NZ, (gy + GY + dy) % GY)

    barrier = pltpu.get_barrier_semaphore()

    def signal(target):
        pl.semaphore_signal(barrier, inc=1, device_id=target, device_id_type=MESH)

    def greet_plane(i, carry):
        signal(plane_peer(i)[0])
        return carry

    loads = [
        pltpu.make_async_copy(src, dst, ld_sem.at[k])
        for k, (src, dst) in enumerate(
            [
                (field3, fv),
                (tx_in, tx),
                (ty_in.at[gy], ty),
                (field3, pad.at[1, :, 8:40, :]),
                (filt_in, filt),
                (depth_in, depth_w),
                (point_in, point_w),
                (tz_in, tz),
                (tzi_in, tzi),
            ]
        )
    ]
    for load in loads[:3]:
        load.start()
    for i in (2, ZC - 2, 1, ZC - 1):
        signal((ring_peer(i), gy))
    for dz in (-1, 1):
        for dy in (-1, 0, 1):
            signal(halo_peer(dz, dy))
    lax.fori_loop(1, 32, greet_plane, 0)
    loads[0].wait()
    for load in loads[3:]:
        load.start()
    for side, row in ((0, YL - 1), (1, 0)):
        edge[side] = fv[:, row, :]

    loads[1].wait()
    loads[2].wait()
    for p in range(2):
        total = None
        for ml in range(2):
            g = 2 * ml + p
            rows = jnp.concatenate(
                [fv[4 * s + g] for s in range(8)], axis=0
            )
            high, low = split(rows)
            value = dot(high, tx[0, ml]) + dot(low, tx[0, ml]) + dot(high, tx[1, ml])
            total = value if total is None else total + value
        high, low = split(total)
        for part in range(2):
            xh[part * 256 : (part + 1) * 256, p * 128 : (p + 1) * 128] = high[:, part * 128 : (part + 1) * 128]
            xl[part * 256 : (part + 1) * 256, p * 128 : (p + 1) * 128] = low[:, part * 128 : (part + 1) * 128]
    same = iota((MY, 8, 256), 1) == iota((MY, 8, 256), 2) // YL

    def spread(which):
        base = ty[which]
        wide = jnp.where(same, jnp.broadcast_to(base[:, None, :], (MY, 8, 256)), 0.0)
        return wide.reshape(128, 256).astype(BF16)

    y_high = jnp.concatenate([spread(0), spread(2)], axis=1)
    y_low = jnp.concatenate([spread(1), spread(3)], axis=1)
    y_both = jnp.concatenate([y_high, y_low], axis=0)
    result = dot(y_both, xh[...]) + dot(y_both, xl[...])
    yout[...] = result[0:128] + result[128:256]
    block = iota((8, 128), 1) // 16 % 4
    for p in range(2):
        for q in range(4):
            quad = [
                yout[(q * 4 + ky) * 8 : (q * 4 + ky + 1) * 8, p * 128 : (p + 1) * 128]
                for ky in range(4)
            ]
            for kxb in range(4):
                out = moved(quad[0], 0 - kxb)
                for ky in range(1, 4):
                    out = jnp.where(block == ky, moved(quad[ky], ky - kxb), out)
                send1[q * 8 + p * 4 + kxb] = out

    pl.semaphore_wait(barrier, 4 + 6 + 31)

    def copy1(i):
        target, t = plane_peer(i)
        return pltpu.make_async_remote_copy(
            send1.at[t], recv1.at[me], s1, r1, device_id=target, device_id_type=MESH
        )

    def start1(i, carry):
        copy1(i).start()
        return carry

    lax.fori_loop(1, 32, start1, 0)
    own1 = pltpu.make_async_copy(send1.at[me], recv1.at[me], r1)
    own1.start()

    def copy_row(dz, side):
        dy = 1 if side == 0 else -1
        slot = (1 - dz) * 2 + side
        return pltpu.make_async_remote_copy(
            edge.at[side], hrow.at[slot], sh, rh.at[0 if dz == 0 else 1],
            device_id=halo_peer(dz, dy), device_id_type=MESH,
        )

    def copy_plane(dz):
        return pltpu.make_async_remote_copy(
            field3, pad.at[1 - dz, :, 8:40, :], sz, rz.at[1 - dz],
            device_id=halo_peer(dz, 0), device_id_type=MESH,
        )

    def send_tokens(which, reach):
        for i in (reach, ZC - reach):
            pl.semaphore_signal(
                tokens.at[which], inc=1, device_id=(ring_peer(i), gy), device_id_type=MESH
            )

    send_tokens(0, 2)
    for side in range(2):
        copy_row(0, side).start()
    for dz in (-1, 1):
        copy_plane(dz).start()
    for dz in (-1, 1):
        for side in range(2):
            copy_row(dz, side).start()
    def put_gains(source, pair):
        for part in range(2):
            for ky in range(4):
                for r in range(2):
                    row = pl.multiple_of(pair * 64 + ky * 16 + r * 8, 8)
                    gains[part, pl.ds(row, 8), 0:16] = source[part * 32 + ky * 8 : part * 32 + ky * 8 + 8, :]

    for load in loads[4:]:
        load.wait()
    gains[...] = jnp.zeros_like(gains)
    put_gains(filt, zc // 8)

    def put_rows(plane, slot):
        pad[plane, :, 7, :] = hrow[slot]
        pad[plane, :, 40, :] = hrow[slot + 1]

    def conv(plane, first):
        def channels(step, carry):
            for k in range(4):
                c = step * 4 + k
                sums = [None, None, None]
                for b in range(3):
                    window = pad[plane, c, 7 + b : 39 + b, :]
                    for e in range(3):
                        term = depth_w[c, plane * 9 + b * 3 + e] * window
                        sums[e] = term if sums[e] is None else sums[e] + term
                value = sums[1] + pltpu.roll(sums[0], 1, 1) + pltpu.roll(sums[2], NX - 1, 1)
                depth[c] = value if first else depth[c] + value
            return carry

        lax.fori_loop(0, C // 4, channels, 0)

    loads[3].wait()

    def wait_rows(index, count):
        part = hrow.at[0:count]
        pltpu.make_async_copy(part, part, rh.at[index]).wait()

    wait_rows(0, 2)
    pl.semaphore_wait(tokens.at[0], 2)
    send_tokens(1, 4)
    put_rows(1, 2)
    conv(1, True)

    pltpu.make_async_copy(recv1, recv1, r1).wait()
    for k in range(W):
        tmp[k * 8 : (k + 1) * 8, :] = (recv1[k] + recv1[8 + k]) + (recv1[16 + k] + recv1[24 + k])
    lower = iota((8, 128), 1) < 64
    for k in range(8):
        one = tmp[pl.ds(k // 2, 8, stride=8), :]
        two = tmp[pl.ds(k // 2 + 4, 8, stride=8), :]
        if k % 2 == 0:
            send2[k] = jnp.where(lower, one, pltpu.roll(two, 64, 1))
        else:
            send2[k] = jnp.where(lower, pltpu.roll(one, 64, 1), two)

    pl.semaphore_wait(tokens.at[1], 2)

    def copy2(k):
        i = 8 + (k + 1) // 2 * (2 * (k % 2) - 1)
        return pltpu.make_async_remote_copy(
            send2.at[(zc + i) % 8], recv2.at[zc], s2, r2,
            device_id=(ring_peer(i), gy), device_id_type=MESH,
        )

    def start2(k, carry):
        copy2(k).start()
        return carry

    copyf = pltpu.make_async_remote_copy(
        filt_in, filt2, sf, rf, device_id=(ring_peer(8), gy), device_id_type=MESH
    )
    copyf.start()
    lax.fori_loop(0, ZC - 1, start2, 0)
    own2 = pltpu.make_async_copy(send2.at[zc % 8], recv2.at[zc], r2)
    own2.start()

    wait_rows(1, 4)
    near = jnp.where(core == 0, 2, 0)
    far = 2 - near
    pltpu.make_async_copy(field3, pad.at[near, :, 8:40, :], rz.at[near]).wait()
    put_rows(near, near * 2)
    conv(near, False)

    copyf.wait_recv()
    put_gains(filt2, 1 - zc // 8)
    gain_re = jnp.transpose(gains[0])[0:16, :]
    gain_im = jnp.transpose(gains[1])[0:16, :]
    pltpu.make_async_copy(recv2, recv2, r2).wait()
    a_high, a_low = split(recv2[...].reshape(NZ, 128))
    both = dot(tz[...], a_high) + dot(tz[...], a_low)
    modes = both[0:16] + both[32:48] + swapped(both[16:32] + both[48:64])
    filtered = modes * gain_re - swapped(modes) * gain_im
    stacked = jnp.concatenate([filtered, -swapped(filtered)], axis=0)
    f_high, f_low = split(stacked)
    both = dot(tzi[...], f_high) + dot(tzi[...], f_low)
    send4[...] = (both[0:128] + both[128:256]).reshape(ZC, 8, 128)

    def copy4(i):
        return pltpu.make_async_remote_copy(
            send4.at[(zc + i) % ZC], recv4.at[pl.ds(pl.multiple_of(zc % 8 * 8, 8), 8), :], s4, r4,
            device_id=(ring_peer(i), gy), device_id_type=MESH,
        )

    nearer = (ZC - 4, 3, ZC - 3, 2, ZC - 2, 1, ZC - 1)
    for i in nearer:
        copy4(i).start()
    own4 = pltpu.make_async_copy(
        send4.at[zc], recv4.at[pl.ds(pl.multiple_of(zc % 8 * 8, 8), 8), :], r4
    )
    own4.start()

    pltpu.make_async_copy(field3, pad.at[far, :, 8:40, :], rz.at[far]).wait()
    put_rows(far, far * 2)
    conv(far, False)

    pltpu.make_async_copy(recv4, recv4, r4).wait()
    for k in range(W):
        even = recv4[pl.ds(k, 4, stride=16), :]
        odd = recv4[pl.ds(8 + k, 4, stride=16), :]
        tmp3[k, 0:4] = jnp.where(lower[0:4], even, pltpu.roll(odd, 64, 1))
        tmp3[k, 4:8] = jnp.where(lower[0:4], pltpu.roll(even, 64, 1), odd)

    def copy3(i):
        target, t = plane_peer(i)
        return pltpu.make_async_remote_copy(
            tmp3.at[t % W], tiles_out.at[w * 4 + gy], s3, r3,
            device_id=target, device_id_type=MESH,
        )

    def start3(i, carry):
        copy3(i).start()
        return carry

    lax.fori_loop(1, 32, start3, 0)
    own3 = pltpu.make_async_copy(
        tmp3.at[w], tiles_out.at[w * 4 + gy], r3
    )
    own3.start()

    grow = (iota((256, C), 0) // 8 == iota((256, C), 1)).astype(F32).astype(BF16)
    grow_t = (iota((C, 256), 1) // 8 == iota((C, 256), 0)).astype(F32).astype(BF16)
    diagonal = iota((256, 256), 0) % 8 == iota((256, 256), 1) % 8
    mixers = []
    for part in split(point_w[...]):
        tall = dot(grow, part).astype(BF16)
        mixers.append(jnp.where(diagonal, dot(tall, grow_t), 0.0).astype(BF16))
    for k in range(YL // 8):
        d_high, d_low = split(depth[:, k * 8 : (k + 1) * 8, :].reshape(256, NX))
        value = dot(mixers[0], d_high) + dot(mixers[0], d_low) + dot(mixers[1], d_high)
        pacc[:, k * 8 : (k + 1) * 8, :] = value.reshape(C, 8, NX)
    put = pltpu.make_async_copy(pacc, point_out, so)
    put.start()

    pltpu.make_async_copy(tiles_out, tiles_out, r3).wait()
    put.wait()

    def done1(i, carry):
        copy1(i).wait_send()
        copy3(i).wait_send()
        return carry

    def done2(k, carry):
        copy2(k).wait_send()
        return carry

    lax.fori_loop(1, 32, done1, 0)
    lax.fori_loop(0, ZC - 1, done2, 0)
    for i in nearer:
        copy4(i).wait_send()
    copyf.wait_send()
    for dz in (-1, 0, 1):
        for side in range(2):
            copy_row(dz, side).wait_send()
    for dz in (-1, 1):
        copy_plane(dz).wait_send()


def last_kernel(tiles, point, bias, tyi, txi, out, yh, yl):
    step = pl.program_id(0)
    gy = lax.axis_index("gy")

    @pl.when(step == 0)
    def _():
        block = iota((8, 128), 1) // 16 % 4
        columns = []
        for p in range(2):
            rows = []
            for ky in range(MY):
                q, k4 = ky // 4, ky % 4
                value = moved(tiles[p * 16 + q], 0 - k4)
                for kxb in range(1, 4):
                    value = jnp.where(block == kxb, moved(tiles[(p * 4 + kxb) * 4 + q], kxb - k4), value)
                rows.append(value)
            columns.append(jnp.concatenate(rows, axis=0))
        r_high, r_low = split(jnp.concatenate(columns, axis=1))
        same = iota((8, YL, 128), 0) == iota((8, YL, 128), 2) % 8

        def spread(which):
            base = tyi[gy, which]
            wide = jnp.where(same, jnp.broadcast_to(base[None], (8, YL, 128)), 0.0)
            return wide.reshape(256, 128).astype(BF16)

        t_high = jnp.concatenate([spread(0), spread(2)], axis=0)
        t_low = jnp.concatenate([spread(1), spread(3)], axis=0)
        value = dot(t_high, r_high) + dot(t_high, r_low) + dot(t_low, r_high)
        high, low = split(value)
        yh[...] = high
        yl[...] = low

    def gathered(ref):
        start = pl.multiple_of(step * 64, 64)
        real = ref[pl.ds(start, 64), :]
        imag = ref[pl.ds(256 + start, 64), :]
        return jnp.concatenate(
            [
                jnp.concatenate([real[:, p * 128 : (p + 1) * 128], imag[:, p * 128 : (p + 1) * 128]], axis=1)
                for p in range(2)
            ],
            axis=0,
        )

    high, low = gathered(yh), gathered(yl)
    spectral = dot(high, txi[0]) + dot(low, txi[0]) + dot(high, txi[1])
    for p in range(2):
        for sl in range(2):
            for ml in range(2):
                ch = 4 * sl + 2 * ml + p
                value = spectral[p * 64 + sl * 32 : p * 64 + (sl + 1) * 32, ml * 256 : (ml + 1) * 256]
                value = value + point[ch] + bias[step * 8 + ch]
                out[ch] = 0.5 * value * (1.0 + lax.erf(value * (0.5**0.5)))


def body(field, spectral_filter, depth_weight, point_weight, bias_vector):
    field3 = field.reshape(C, YL, NX)
    filt = spectral_filter.transpose(0, 2, 3, 1).reshape(64, 16)
    const = {name: jnp.asarray(value) for name, value in TABLES.items()}
    vmem = pl.BlockSpec(memory_space=pltpu.VMEM)
    smem = pl.BlockSpec(memory_space=pltpu.SMEM)
    hbm = pl.BlockSpec(memory_space=pltpu.HBM)
    tiles, point = pl.pallas_call(
        wide_kernel,
        name="wide",
        out_shape=(
            jax.ShapeDtypeStruct((32, 8, 128), F32),
            jax.ShapeDtypeStruct((C, YL, NX), F32),
        ),
        in_specs=[hbm] * 8,
        out_specs=(hbm, hbm),
        scratch_shapes=[
            VMEM((C, YL, NX), F32),
            VMEM((64, 16), F32),
            VMEM((64, 16), F32),
            pltpu.SMEM((C, 27), F32),
            VMEM((C, C), F32),
            VMEM((2, 2, 256, 256), BF16),
            VMEM((4, MY, 256), F32),
            VMEM((64, 128), BF16),
            VMEM((256, 32), BF16),
            VMEM((3, C, 48, NX), F32),
            VMEM((2, C, NX), F32),
            VMEM((6, C, NX), F32),
            VMEM((512, 256), BF16),
            VMEM((512, 256), BF16),
            VMEM((128, 256), F32),
            VMEM((32, 8, 128), F32),
            VMEM((32, 8, 128), F32),
            VMEM((64, 128), F32),
            VMEM((8, 8, 128), F32),
            VMEM((ZC, 8, 128), F32),
            VMEM((2, 128, 128), F32),
            VMEM((ZC, 8, 128), F32),
            VMEM((64, 128), F32),
            VMEM((W, 8, 128), F32),
            VMEM((C, YL, NX), F32),
            VMEM((C, YL, NX), F32),
            DMA((9,)), DMA, DMA, DMA, DMA((2,)), DMA, DMA((3,)), DMA, DMA, DMA, DMA, DMA, DMA, DMA, DMA, DMA,
            pltpu.SemaphoreType.REGULAR((2,)),
        ],
        compiler_params=pltpu.CompilerParams(
            collective_id=0, has_side_effects=True, vmem_limit_bytes=VMEM_ALL
        ),
    )(
        field3, filt, depth_weight, point_weight,
        const["tx"], const["ty"], const["tz"], const["tzi"],
    )
    out = pl.pallas_call(
        last_kernel,
        name="last",
        out_shape=jax.ShapeDtypeStruct((C, YL, NX), F32),
        grid=(4,),
        in_specs=[
            vmem,
            pl.BlockSpec((8, YL, NX), lambda i: (i, 0, 0)),
            smem,
            vmem,
            vmem,
        ],
        out_specs=pl.BlockSpec((8, YL, NX), lambda i: (i, 0, 0)),
        scratch_shapes=[VMEM((512, 256), BF16), VMEM((512, 256), BF16)],
        compiler_params=pltpu.CompilerParams(dimension_semantics=("arbitrary",), vmem_limit_bytes=VMEM_ALL),
    )(tiles, point, bias_vector, const["tyi"], const["txi"])
    return out.reshape(C, 1, YL, NX)


def solution(mesh):
    in_specs = (P(None, "gz", "gy", None), P(None, None, "gy", "gz"), P(), P(), P())
    out_specs = P(None, "gz", "gy", None)
    return jax.shard_map(body, mesh=mesh, in_specs=in_specs, out_specs=out_specs, check_vma=False)
```

```python
import functools

import jax
import jax.numpy as jnp
import ml_dtypes
import numpy as np
from jax import lax
from jax.experimental import pallas as pl
from jax.experimental.pallas import tpu as pltpu
from jax.sharding import PartitionSpec as P

C = 32
NX = 256
NY = 128
NZ = 128
MX = 32
MY = 16
MZ = 16
GY = 4
ZC = 16
W = 8
YL = NY // GY
VMEM_ALL = 67043328
CUTS = (8, 22)
MESH = pl.DeviceIdType.MESH
F32 = jnp.float32
BF16 = jnp.bfloat16
VMEM = pltpu.VMEM
DMA = pltpu.SemaphoreType.DMA


def halves(table):
    high = table.astype(ml_dtypes.bfloat16)
    low = (table - high.astype(np.float64)).astype(ml_dtypes.bfloat16)
    return high, low


def kept(count, total):
    series = np.arange(count)
    return np.where(series < count // 2, series, total - count + series)


def make_tables():
    tables = {}
    angle = 2 * np.pi * (np.arange(NX)[:, None] * np.arange(MX)[None, :] % NX) / NX
    cos = np.cos(angle).reshape(NX, 4, 8)
    sin = np.sin(angle).reshape(NX, 4, 8)
    plain = np.stack([cos, -sin], axis=2).reshape(NX, 64)
    swapped = np.stack([-sin, -cos], axis=2).reshape(NX, 64)
    zero = np.zeros_like(plain)
    tx = np.stack(
        [
            np.concatenate([plain, zero, swapped, zero], axis=1),
            np.concatenate([zero, plain, zero, swapped], axis=1),
        ]
    )
    tables["tx"] = np.stack(halves(tx))
    places = np.arange(NY)
    angle = 2 * np.pi * (kept(MY, NY)[:, None] * places[None, :] % NY) / NY
    parts = []
    for value in (np.cos(angle), np.sin(angle)):
        parts.extend(part.astype(np.float32) for part in halves(value))
    stack = np.stack(parts)
    mine = stack.reshape(4, MY, GY, YL).transpose(2, 0, 1, 3)
    tables["ty"] = np.tile(mine, (1, 1, 1, 8))
    tables["tyi"] = np.repeat(mine.transpose(0, 1, 3, 2), 8, axis=3)
    angle = 2 * np.pi * (kept(MZ, NZ)[:, None] * np.arange(NZ)[None, :] % NZ) / NZ
    high, low = halves(np.concatenate([np.cos(angle), np.sin(angle)], axis=0))
    tables["tz"] = np.concatenate([high, low], axis=0)
    scale = (NX * NY * NZ) ** -0.5 * (2.0 * MX * MY * MZ) ** -0.5
    both = np.concatenate([np.cos(angle), np.sin(angle)], axis=0).T * scale
    tables["tzi"] = np.concatenate(halves(both), axis=0)
    weight = np.where(np.arange(MX) == 0, 1.0, 2.0)[:, None]
    angle = 2 * np.pi * (np.arange(MX)[:, None] * np.arange(NX)[None, :] % NX) / NX
    cos = (weight * np.cos(angle)).reshape(4, 8, NX)
    sin = (weight * np.sin(angle)).reshape(4, 8, NX)
    from_c = np.stack([cos, -sin], axis=1).reshape(64, NX)
    from_s = np.stack([-sin, -cos], axis=1).reshape(64, NX)
    zero = np.zeros_like(from_c)
    txi = np.block([[from_c, zero], [zero, from_c], [from_s, zero], [zero, from_s]])
    tables["txi"] = np.stack(halves(txi))
    return tables


TABLES = make_tables()


def split(value):
    high = value.astype(BF16)
    return high, (value - high.astype(F32)).astype(BF16)


def dot(left, right):
    return jnp.dot(left, right, preferred_element_type=F32)


def iota(shape, dim):
    return lax.broadcasted_iota(jnp.int32, shape, dim)


def swapped(value):
    pieces = []
    for k in range(value.shape[1] // 128):
        piece = value[:, k * 128 : (k + 1) * 128]
        real_lane = iota(piece.shape, 1) % 16 < 8
        pieces.append(jnp.where(real_lane, pltpu.roll(piece, 120, 1), -pltpu.roll(piece, 8, 1)))
    return jnp.concatenate(pieces, axis=1)


def moved(value, blocks):
    return value if blocks % 8 == 0 else pltpu.roll(value, blocks % 8 * 16, 1)


def wide_kernel(
    field3, filt_in, depth_in, point_in, tx_in, ty_in, tz_in, tzi_in,
    tiles_out, point_out,
    fv, filt, filt2, depth_w, point_w, tx, ty, tz, tzi,
    pad, edge, hrow, xh, xl, yout, send1, recv1, tmp, send2, recv2, gains,
    send4, recv4, tmp3, depth, pacc,
    ld_sem, s1, r1, sh, rh, sz, rz, s2, r2, s4, r4, s3, r3, so, sf, rf, tokens,
):
    gz = lax.axis_index("gz")
    gy = lax.axis_index("gy")
    zc = gz // W
    w = gz % W
    core = gz % 2
    me = gy * W + w

    def plane_peer(i):
        t = (me + i) % 32
        return (zc * W + t % W, t // W), t

    def ring_peer(i):
        return ((zc + i) % ZC) * W + w

    def halo_peer(dz, dy):
        return ((gz + NZ + dz) % NZ, (gy + GY + dy) % GY)

    barrier = pltpu.get_barrier_semaphore()

    def signal(target):
        pl.semaphore_signal(barrier, inc=1, device_id=target, device_id_type=MESH)

    def greet_plane(i, carry):
        signal(plane_peer(i)[0])
        return carry

    loads = [
        pltpu.make_async_copy(src, dst, ld_sem.at[k])
        for k, (src, dst) in enumerate(
            [
                (field3, fv),
                (tx_in, tx),
                (ty_in.at[gy], ty),
                (field3, pad.at[1, :, 8:40, :]),
                (filt_in, filt),
                (depth_in, depth_w),
                (point_in, point_w),
                (tz_in, tz),
                (tzi_in, tzi),
            ]
        )
    ]
    for load in loads[:3]:
        load.start()
    for i in (2, ZC - 2, 1, ZC - 1):
        signal((ring_peer(i), gy))
    for dz in (-1, 1):
        for dy in (-1, 0, 1):
            signal(halo_peer(dz, dy))
    lax.fori_loop(1, 32, greet_plane, 0)
    loads[0].wait()
    for load in loads[3:]:
        load.start()
    for side, row in ((0, YL - 1), (1, 0)):
        edge[side] = fv[:, row, :]

    loads[1].wait()
    loads[2].wait()
    for p in range(2):
        total = None
        for ml in range(2):
            g = 2 * ml + p
            rows = jnp.concatenate(
                [fv[4 * s + g] for s in range(8)], axis=0
            )
            high, low = split(rows)
            value = dot(high, tx[0, ml]) + dot(low, tx[0, ml]) + dot(high, tx[1, ml])
            total = value if total is None else total + value
        high, low = split(total)
        for part in range(2):
            xh[part * 256 : (part + 1) * 256, p * 128 : (p + 1) * 128] = high[:, part * 128 : (part + 1) * 128]
            xl[part * 256 : (part + 1) * 256, p * 128 : (p + 1) * 128] = low[:, part * 128 : (part + 1) * 128]
    same = iota((MY, 8, 256), 1) == iota((MY, 8, 256), 2) // YL

    def spread(which):
        base = ty[which]
        wide = jnp.where(same, jnp.broadcast_to(base[:, None, :], (MY, 8, 256)), 0.0)
        return wide.reshape(128, 256).astype(BF16)

    y_high = jnp.concatenate([spread(0), spread(2)], axis=1)
    y_low = jnp.concatenate([spread(1), spread(3)], axis=1)
    y_both = jnp.concatenate([y_high, y_low], axis=0)
    result = dot(y_both, xh[...]) + dot(y_both, xl[...])
    yout[...] = result[0:128] + result[128:256]
    block = iota((8, 128), 1) // 16 % 4
    for p in range(2):
        for q in range(4):
            quad = [
                yout[(q * 4 + ky) * 8 : (q * 4 + ky + 1) * 8, p * 128 : (p + 1) * 128]
                for ky in range(4)
            ]
            for kxb in range(4):
                out = moved(quad[0], 0 - kxb)
                for ky in range(1, 4):
                    out = jnp.where(block == ky, moved(quad[ky], ky - kxb), out)
                send1[q * 8 + p * 4 + kxb] = out

    pl.semaphore_wait(barrier, 4 + 6 + 31)

    def copy1(i):
        target, t = plane_peer(i)
        return pltpu.make_async_remote_copy(
            send1.at[t], recv1.at[me], s1, r1, device_id=target, device_id_type=MESH
        )

    def start1(i, carry):
        copy1(i).start()
        return carry

    lax.fori_loop(1, 32, start1, 0)
    own1 = pltpu.make_async_copy(send1.at[me], recv1.at[me], r1)
    own1.start()

    def copy_row(dz, side):
        dy = 1 if side == 0 else -1
        slot = (1 - dz) * 2 + side
        return pltpu.make_async_remote_copy(
            edge.at[side], hrow.at[slot], sh, rh.at[0 if dz == 0 else 1],
            device_id=halo_peer(dz, dy), device_id_type=MESH,
        )

    to_near = 1 - 2 * core

    def copy_plane(dz, chans):
        return pltpu.make_async_remote_copy(
            field3.at[chans[0] : chans[1]], pad.at[1 - dz, chans[0] : chans[1], 8:40, :], sz, rz.at[1 - dz],
            device_id=halo_peer(dz, 0), device_id_type=MESH,
        )

    parts = ((0, CUTS[0]), (CUTS[0], CUTS[1]), (CUTS[1], C))
    crossing = jnp.logical_or(w == 0, w == W - 1)

    def cross(part):
        @pl.when(crossing)
        def _():
            copy_plane(-to_near, parts[part]).start()

    def send_tokens(which, reach):
        for i in (reach, ZC - reach):
            pl.semaphore_signal(
                tokens.at[which], inc=1, device_id=(ring_peer(i), gy), device_id_type=MESH
            )

    send_tokens(0, 2)
    for side in range(2):
        copy_row(0, side).start()
    copy_plane(to_near, (0, C)).start()
    cross(0)

    @pl.when(jnp.logical_not(crossing))
    def _():
        for part in parts:
            copy_plane(-to_near, part).start()

    for dz in (-1, 1):
        for side in range(2):
            copy_row(dz, side).start()
    def put_gains(source, pair):
        for part in range(2):
            for ky in range(4):
                for r in range(2):
                    row = pl.multiple_of(pair * 64 + ky * 16 + r * 8, 8)
                    gains[part, pl.ds(row, 8), 0:16] = source[part * 32 + ky * 8 : part * 32 + ky * 8 + 8, :]

    for load in loads[4:]:
        load.wait()
    gains[...] = jnp.zeros_like(gains)
    put_gains(filt, zc // 8)

    def put_rows(plane, slot):
        pad[plane, :, 7, :] = hrow[slot]
        pad[plane, :, 40, :] = hrow[slot + 1]

    def conv(plane, first):
        def channels(step, carry):
            for k in range(4):
                c = step * 4 + k
                sums = [None, None, None]
                for b in range(3):
                    window = pad[plane, c, 7 + b : 39 + b, :]
                    for e in range(3):
                        term = depth_w[c, plane * 9 + b * 3 + e] * window
                        sums[e] = term if sums[e] is None else sums[e] + term
                value = sums[1] + pltpu.roll(sums[0], 1, 1) + pltpu.roll(sums[2], NX - 1, 1)
                depth[c] = value if first else depth[c] + value
            return carry

        lax.fori_loop(0, C // 4, channels, 0)

    pl.semaphore_wait(tokens.at[0], 2)
    send_tokens(1, 4)

    pltpu.make_async_copy(recv1, recv1, r1).wait()
    for k in range(W):
        tmp[k * 8 : (k + 1) * 8, :] = (recv1[k] + recv1[8 + k]) + (recv1[16 + k] + recv1[24 + k])
    lower = iota((8, 128), 1) < 64
    for k in range(8):
        one = tmp[pl.ds(k // 2, 8, stride=8), :]
        two = tmp[pl.ds(k // 2 + 4, 8, stride=8), :]
        if k % 2 == 0:
            send2[k] = jnp.where(lower, one, pltpu.roll(two, 64, 1))
        else:
            send2[k] = jnp.where(lower, pltpu.roll(one, 64, 1), two)

    pl.semaphore_wait(tokens.at[1], 2)

    def copy2(k):
        i = 8 + (k + 1) // 2 * (2 * (k % 2) - 1)
        return pltpu.make_async_remote_copy(
            send2.at[(zc + i) % 8], recv2.at[zc], s2, r2,
            device_id=(ring_peer(i), gy), device_id_type=MESH,
        )

    def start2(k, carry):
        copy2(k).start()
        return carry

    copyf = pltpu.make_async_remote_copy(
        filt_in, filt2, sf, rf, device_id=(ring_peer(8), gy), device_id_type=MESH
    )
    copyf.start()
    lax.fori_loop(0, ZC - 1, start2, 0)
    own2 = pltpu.make_async_copy(send2.at[zc % 8], recv2.at[zc], r2)
    own2.start()

    cross(1)
    loads[3].wait()

    def wait_rows(index, count):
        part = hrow.at[0:count]
        pltpu.make_async_copy(part, part, rh.at[index]).wait()

    wait_rows(0, 2)
    put_rows(1, 2)
    conv(1, True)

    wait_rows(1, 4)
    near = jnp.where(core == 0, 2, 0)
    far = 2 - near
    pltpu.make_async_copy(field3, pad.at[near, :, 8:40, :], rz.at[near]).wait()
    put_rows(near, near * 2)
    conv(near, False)

    copyf.wait_recv()
    put_gains(filt2, 1 - zc // 8)
    gain_re = jnp.transpose(gains[0])[0:16, :]
    gain_im = jnp.transpose(gains[1])[0:16, :]
    pltpu.make_async_copy(recv2, recv2, r2).wait()
    a_high, a_low = split(recv2[...].reshape(NZ, 128))
    both = dot(tz[...], a_high) + dot(tz[...], a_low)
    modes = both[0:16] + both[32:48] + swapped(both[16:32] + both[48:64])
    filtered = modes * gain_re - swapped(modes) * gain_im
    stacked = jnp.concatenate([filtered, -swapped(filtered)], axis=0)
    f_high, f_low = split(stacked)
    both = dot(tzi[...], f_high) + dot(tzi[...], f_low)
    send4[...] = (both[0:128] + both[128:256]).reshape(ZC, 8, 128)

    def copy4(i):
        return pltpu.make_async_remote_copy(
            send4.at[(zc + i) % ZC], recv4.at[pl.ds(pl.multiple_of(zc % 8 * 8, 8), 8), :], s4, r4,
            device_id=(ring_peer(i), gy), device_id_type=MESH,
        )

    nearer = (ZC - 4, 3, ZC - 3, 2, ZC - 2, 1, ZC - 1)
    for i in nearer:
        copy4(i).start()
    own4 = pltpu.make_async_copy(
        send4.at[zc], recv4.at[pl.ds(pl.multiple_of(zc % 8 * 8, 8), 8), :], r4
    )
    own4.start()

    cross(2)
    pltpu.make_async_copy(recv4, recv4, r4).wait()
    for k in range(W):
        even = recv4[pl.ds(k, 4, stride=16), :]
        odd = recv4[pl.ds(8 + k, 4, stride=16), :]
        tmp3[k, 0:4] = jnp.where(lower[0:4], even, pltpu.roll(odd, 64, 1))
        tmp3[k, 4:8] = jnp.where(lower[0:4], pltpu.roll(even, 64, 1), odd)

    def copy3(i):
        target, t = plane_peer(i)
        return pltpu.make_async_remote_copy(
            tmp3.at[t % W], tiles_out.at[w * 4 + gy], s3, r3,
            device_id=target, device_id_type=MESH,
        )

    def start3(i, carry):
        copy3(i).start()
        return carry

    lax.fori_loop(1, 32, start3, 0)
    own3 = pltpu.make_async_copy(
        tmp3.at[w], tiles_out.at[w * 4 + gy], r3
    )
    own3.start()

    pltpu.make_async_copy(field3, pad.at[far, :, 8:40, :], rz.at[far]).wait()
    put_rows(far, far * 2)
    conv(far, False)

    grow = (iota((256, C), 0) // 8 == iota((256, C), 1)).astype(F32).astype(BF16)
    grow_t = (iota((C, 256), 1) // 8 == iota((C, 256), 0)).astype(F32).astype(BF16)
    diagonal = iota((256, 256), 0) % 8 == iota((256, 256), 1) % 8
    mixers = []
    for part in split(point_w[...]):
        tall = dot(grow, part).astype(BF16)
        mixers.append(jnp.where(diagonal, dot(tall, grow_t), 0.0).astype(BF16))
    for k in range(YL // 8):
        d_high, d_low = split(depth[:, k * 8 : (k + 1) * 8, :].reshape(256, NX))
        value = dot(mixers[0], d_high) + dot(mixers[0], d_low) + dot(mixers[1], d_high)
        pacc[:, k * 8 : (k + 1) * 8, :] = value.reshape(C, 8, NX)
    put = pltpu.make_async_copy(pacc, point_out, so)
    put.start()

    pltpu.make_async_copy(tiles_out, tiles_out, r3).wait()
    put.wait()

    def done1(i, carry):
        copy1(i).wait_send()
        copy3(i).wait_send()
        return carry

    def done2(k, carry):
        copy2(k).wait_send()
        return carry

    lax.fori_loop(1, 32, done1, 0)
    lax.fori_loop(0, ZC - 1, done2, 0)
    for i in nearer:
        copy4(i).wait_send()
    copyf.wait_send()
    for dz in (-1, 0, 1):
        for side in range(2):
            copy_row(dz, side).wait_send()
    copy_plane(to_near, (0, C)).wait_send()
    for part in parts:
        copy_plane(-to_near, part).wait_send()


def last_kernel(tiles, point, bias, tyi, txi, out, yh, yl):
    step = pl.program_id(0)
    gy = lax.axis_index("gy")

    @pl.when(step == 0)
    def _():
        block = iota((8, 128), 1) // 16 % 4
        columns = []
        for p in range(2):
            rows = []
            for ky in range(MY):
                q, k4 = ky // 4, ky % 4
                value = moved(tiles[p * 16 + q], 0 - k4)
                for kxb in range(1, 4):
                    value = jnp.where(block == kxb, moved(tiles[(p * 4 + kxb) * 4 + q], kxb - k4), value)
                rows.append(value)
            columns.append(jnp.concatenate(rows, axis=0))
        r_high, r_low = split(jnp.concatenate(columns, axis=1))
        same = iota((8, YL, 128), 0) == iota((8, YL, 128), 2) % 8

        def spread(which):
            base = tyi[gy, which]
            wide = jnp.where(same, jnp.broadcast_to(base[None], (8, YL, 128)), 0.0)
            return wide.reshape(256, 128).astype(BF16)

        t_high = jnp.concatenate([spread(0), spread(2)], axis=0)
        t_low = jnp.concatenate([spread(1), spread(3)], axis=0)
        value = dot(t_high, r_high) + dot(t_high, r_low) + dot(t_low, r_high)
        high, low = split(value)
        yh[...] = high
        yl[...] = low

    def gathered(ref):
        start = pl.multiple_of(step * 64, 64)
        real = ref[pl.ds(start, 64), :]
        imag = ref[pl.ds(256 + start, 64), :]
        return jnp.concatenate(
            [
                jnp.concatenate([real[:, p * 128 : (p + 1) * 128], imag[:, p * 128 : (p + 1) * 128]], axis=1)
                for p in range(2)
            ],
            axis=0,
        )

    high, low = gathered(yh), gathered(yl)
    spectral = dot(high, txi[0]) + dot(low, txi[0]) + dot(high, txi[1])
    for p in range(2):
        for sl in range(2):
            for ml in range(2):
                ch = 4 * sl + 2 * ml + p
                value = spectral[p * 64 + sl * 32 : p * 64 + (sl + 1) * 32, ml * 256 : (ml + 1) * 256]
                value = value + point[ch] + bias[step * 8 + ch]
                out[ch] = 0.5 * value * (1.0 + lax.erf(value * (0.5**0.5)))


def body(field, spectral_filter, depth_weight, point_weight, bias_vector):
    field3 = field.reshape(C, YL, NX)
    filt = spectral_filter.transpose(0, 2, 3, 1).reshape(64, 16)
    const = {name: jnp.asarray(value) for name, value in TABLES.items()}
    vmem = pl.BlockSpec(memory_space=pltpu.VMEM)
    smem = pl.BlockSpec(memory_space=pltpu.SMEM)
    hbm = pl.BlockSpec(memory_space=pltpu.HBM)
    tiles, point = pl.pallas_call(
        wide_kernel,
        name="wide",
        out_shape=(
            jax.ShapeDtypeStruct((32, 8, 128), F32),
            jax.ShapeDtypeStruct((C, YL, NX), F32),
        ),
        in_specs=[hbm] * 8,
        out_specs=(hbm, hbm),
        scratch_shapes=[
            VMEM((C, YL, NX), F32),
            VMEM((64, 16), F32),
            VMEM((64, 16), F32),
            pltpu.SMEM((C, 27), F32),
            VMEM((C, C), F32),
            VMEM((2, 2, 256, 256), BF16),
            VMEM((4, MY, 256), F32),
            VMEM((64, 128), BF16),
            VMEM((256, 32), BF16),
            VMEM((3, C, 48, NX), F32),
            VMEM((2, C, NX), F32),
            VMEM((6, C, NX), F32),
            VMEM((512, 256), BF16),
            VMEM((512, 256), BF16),
            VMEM((128, 256), F32),
            VMEM((32, 8, 128), F32),
            VMEM((32, 8, 128), F32),
            VMEM((64, 128), F32),
            VMEM((8, 8, 128), F32),
            VMEM((ZC, 8, 128), F32),
            VMEM((2, 128, 128), F32),
            VMEM((ZC, 8, 128), F32),
            VMEM((64, 128), F32),
            VMEM((W, 8, 128), F32),
            VMEM((C, YL, NX), F32),
            VMEM((C, YL, NX), F32),
            DMA((9,)), DMA, DMA, DMA, DMA((2,)), DMA, DMA((3,)), DMA, DMA, DMA, DMA, DMA, DMA, DMA, DMA, DMA,
            pltpu.SemaphoreType.REGULAR((2,)),
        ],
        compiler_params=pltpu.CompilerParams(
            collective_id=0, has_side_effects=True, vmem_limit_bytes=VMEM_ALL
        ),
    )(
        field3, filt, depth_weight, point_weight,
        const["tx"], const["ty"], const["tz"], const["tzi"],
    )
    out = pl.pallas_call(
        last_kernel,
        name="last",
        out_shape=jax.ShapeDtypeStruct((C, YL, NX), F32),
        grid=(4,),
        in_specs=[
            vmem,
            pl.BlockSpec((8, YL, NX), lambda i: (i, 0, 0)),
            smem,
            vmem,
            vmem,
        ],
        out_specs=pl.BlockSpec((8, YL, NX), lambda i: (i, 0, 0)),
        scratch_shapes=[VMEM((512, 256), BF16), VMEM((512, 256), BF16)],
        compiler_params=pltpu.CompilerParams(dimension_semantics=("arbitrary",), vmem_limit_bytes=VMEM_ALL),
    )(tiles, point, bias_vector, const["tyi"], const["txi"])
    return out.reshape(C, 1, YL, NX)


def solution(mesh):
    in_specs = (P(None, "gz", "gy", None), P(None, None, "gy", "gz"), P(), P(), P())
    out_specs = P(None, "gz", "gy", None)
    return jax.shard_map(body, mesh=mesh, in_specs=in_specs, out_specs=out_specs, check_vma=False)
```

```python
import functools

import jax
import jax.numpy as jnp
import ml_dtypes
import numpy as np
from jax import lax
from jax.experimental import pallas as pl
from jax.experimental.pallas import tpu as pltpu
from jax.sharding import PartitionSpec as P

C = 32
NX = 256
NY = 128
NZ = 128
MX = 32
MY = 16
MZ = 16
GY = 4
ZC = 16
W = 8
YL = NY // GY
VMEM_ALL = 67043328
CUTS = (12, 24)
MESH = pl.DeviceIdType.MESH
F32 = jnp.float32
BF16 = jnp.bfloat16
VMEM = pltpu.VMEM
DMA = pltpu.SemaphoreType.DMA


def halves(table):
    high = table.astype(ml_dtypes.bfloat16)
    low = (table - high.astype(np.float64)).astype(ml_dtypes.bfloat16)
    return high, low


def kept(count, total):
    series = np.arange(count)
    return np.where(series < count // 2, series, total - count + series)


def make_tables():
    tables = {}
    angle = 2 * np.pi * (np.arange(NX)[:, None] * np.arange(MX)[None, :] % NX) / NX
    cos = np.cos(angle).reshape(NX, 4, 8)
    sin = np.sin(angle).reshape(NX, 4, 8)
    plain = np.stack([cos, -sin], axis=2).reshape(NX, 64)
    swapped = np.stack([-sin, -cos], axis=2).reshape(NX, 64)
    zero = np.zeros_like(plain)
    tx = np.stack(
        [
            np.concatenate([plain, zero, swapped, zero], axis=1),
            np.concatenate([zero, plain, zero, swapped], axis=1),
        ]
    )
    high, low = halves(tx)
    tables["tx"] = np.concatenate([high, high, low], axis=1)
    places = np.arange(NY)
    angle = 2 * np.pi * (kept(MY, NY)[:, None] * places[None, :] % NY) / NY
    parts = []
    for value in (np.cos(angle), np.sin(angle)):
        parts.extend(part.astype(np.float32) for part in halves(value))
    stack = np.stack(parts)
    mine = stack.reshape(4, MY, GY, YL).transpose(2, 0, 1, 3)
    tables["ty"] = np.tile(mine, (1, 1, 1, 8))
    tables["tyi"] = np.repeat(mine.transpose(0, 1, 3, 2), 8, axis=3)
    angle = 2 * np.pi * (kept(MZ, NZ)[:, None] * np.arange(NZ)[None, :] % NZ) / NZ
    high, low = halves(np.concatenate([np.cos(angle), np.sin(angle)], axis=0))
    tables["tz"] = np.concatenate([high, low], axis=0)
    scale = (NX * NY * NZ) ** -0.5 * (2.0 * MX * MY * MZ) ** -0.5
    both = np.concatenate([np.cos(angle), np.sin(angle)], axis=0).T * scale
    tables["tzi"] = np.concatenate(halves(both), axis=0)
    weight = np.where(np.arange(MX) == 0, 1.0, 2.0)[:, None]
    angle = 2 * np.pi * (np.arange(MX)[:, None] * np.arange(NX)[None, :] % NX) / NX
    cos = (weight * np.cos(angle)).reshape(4, 8, NX)
    sin = (weight * np.sin(angle)).reshape(4, 8, NX)
    from_c = np.stack([cos, -sin], axis=1).reshape(64, NX)
    from_s = np.stack([-sin, -cos], axis=1).reshape(64, NX)
    zero = np.zeros_like(from_c)
    txi = np.block([[from_c, zero], [zero, from_c], [from_s, zero], [zero, from_s]])
    high, low = halves(txi)
    tables["txi"] = np.concatenate([high, high, low], axis=0)
    return tables


TABLES = make_tables()


def split(value):
    high = value.astype(BF16)
    return high, (value - high.astype(F32)).astype(BF16)


def dot(left, right):
    return jnp.dot(left, right, preferred_element_type=F32)


def iota(shape, dim):
    return lax.broadcasted_iota(jnp.int32, shape, dim)


def swapped(value):
    pieces = []
    for k in range(value.shape[1] // 128):
        piece = value[:, k * 128 : (k + 1) * 128]
        real_lane = iota(piece.shape, 1) % 16 < 8
        pieces.append(jnp.where(real_lane, pltpu.roll(piece, 120, 1), -pltpu.roll(piece, 8, 1)))
    return jnp.concatenate(pieces, axis=1)


def moved(value, blocks):
    return value if blocks % 8 == 0 else pltpu.roll(value, blocks % 8 * 16, 1)


def wide_kernel(
    field3, filt_in, depth_in, point_in, tx_in, ty_in, tz_in, tzi_in, tyi_in, txi_in,
    done_out,
    fv, filt, filt2, depth_w, point_w, tx, ty, tz, tzi, tyi, txi, wide_yi, recv3,
    pad, edge, hrow, xh, xl, yout, send1, recv1, tmp, send2, recv2, gains,
    send4, recv4, tmp3, depth, pacc,
    ld_sem, s1, r1, sh, rh, sz, rz, s2, r2, s4, r4, s3, r3, so, sf, rf, tokens,
):
    gz = lax.axis_index("gz")
    gy = lax.axis_index("gy")
    zc = gz // W
    w = gz % W
    core = gz % 2
    me = gy * W + w

    def plane_peer(i):
        t = (me + i) % 32
        return (zc * W + t % W, t // W), t

    def plane_loop(step):
        lax.fori_loop(0, 16, lambda k, carry: step(23 - k, carry), 0)
        lax.fori_loop(24, 32, step, 0)
        lax.fori_loop(1, 8, step, 0)

    def ring_peer(i):
        return ((zc + i) % ZC) * W + w

    def halo_peer(dz, dy):
        return ((gz + NZ + dz) % NZ, (gy + GY + dy) % GY)

    barrier = pltpu.get_barrier_semaphore()

    def signal(target):
        pl.semaphore_signal(barrier, inc=1, device_id=target, device_id_type=MESH)

    def greet_plane(i, carry):
        signal(plane_peer(i)[0])
        return carry

    loads = [
        pltpu.make_async_copy(src, dst, ld_sem.at[k])
        for k, (src, dst) in enumerate(
            [
                (field3, fv),
                (tx_in, tx),
                (ty_in.at[gy], ty),
                (field3, pad.at[1, :, 8:40, :]),
                (filt_in, filt),
                (depth_in, depth_w),
                (point_in, point_w),
                (tz_in, tz),
                (tzi_in, tzi),
                (tyi_in.at[gy], tyi),
                (txi_in, txi),
            ]
        )
    ]
    for load in loads[:3]:
        load.start()
    for i in (2, ZC - 2, 1, ZC - 1):
        signal((ring_peer(i), gy))
    for dz in (-1, 1):
        for dy in (-1, 0, 1):
            signal(halo_peer(dz, dy))
    plane_loop(greet_plane)
    loads[0].wait()
    for load in loads[3:]:
        load.start()
    for side, row in ((0, YL - 1), (1, 0)):
        edge[side] = fv[:, row, :]

    loads[1].wait()
    loads[2].wait()
    for p in range(2):
        total = None
        for ml in range(2):
            g = 2 * ml + p
            rows = jnp.concatenate(
                [fv[4 * s + g] for s in range(8)], axis=0
            )
            high, low = split(rows)
            value = dot(jnp.concatenate([high, low, high], axis=1), tx[ml])
            total = value if total is None else total + value
        high, low = split(total)
        for part in range(2):
            xh[part * 256 : (part + 1) * 256, p * 128 : (p + 1) * 128] = high[:, part * 128 : (part + 1) * 128]
            xl[part * 256 : (part + 1) * 256, p * 128 : (p + 1) * 128] = low[:, part * 128 : (part + 1) * 128]
    same = iota((MY, 8, 256), 1) == iota((MY, 8, 256), 2) // YL

    def spread(which):
        base = ty[which]
        wide = jnp.where(same, jnp.broadcast_to(base[:, None, :], (MY, 8, 256)), 0.0)
        return wide.reshape(128, 256).astype(BF16)

    y_high = jnp.concatenate([spread(0), spread(2)], axis=1)
    y_low = jnp.concatenate([spread(1), spread(3)], axis=1)
    y_both = jnp.concatenate([y_high, y_low], axis=0)
    result = dot(y_both, xh[...]) + dot(y_both, xl[...])
    yout[...] = result[0:128] + result[128:256]
    block = iota((8, 128), 1) // 16 % 4
    for p in range(2):
        for q in range(4):
            quad = [
                yout[(q * 4 + ky) * 8 : (q * 4 + ky + 1) * 8, p * 128 : (p + 1) * 128]
                for ky in range(4)
            ]
            for kxb in range(4):
                out = moved(quad[0], 0 - kxb)
                for ky in range(1, 4):
                    out = jnp.where(block == ky, moved(quad[ky], ky - kxb), out)
                send1[q * 8 + p * 4 + kxb] = out

    pl.semaphore_wait(barrier, 4 + 6 + 31)

    def copy1(i):
        target, t = plane_peer(i)
        return pltpu.make_async_remote_copy(
            send1.at[t], recv1.at[me], s1, r1, device_id=target, device_id_type=MESH
        )

    def start1(i, carry):
        copy1(i).start()
        return carry

    plane_loop(start1)
    own1 = pltpu.make_async_copy(send1.at[me], recv1.at[me], r1)
    own1.start()

    def copy_row(dz, side):
        dy = 1 if side == 0 else -1
        slot = (1 - dz) * 2 + side
        return pltpu.make_async_remote_copy(
            edge.at[side], hrow.at[slot], sh, rh.at[0 if dz == 0 else 1],
            device_id=halo_peer(dz, dy), device_id_type=MESH,
        )

    to_near = 1 - 2 * core

    def copy_plane(dz, chans):
        landed = 1 if chans[0] == CUTS[1] else 1 - dz
        return pltpu.make_async_remote_copy(
            field3.at[chans[0] : chans[1]], pad.at[1 - dz, chans[0] : chans[1], 8:40, :], sz, rz.at[landed],
            device_id=halo_peer(dz, 0), device_id_type=MESH,
        )

    parts = ((0, CUTS[0]), (CUTS[0], CUTS[1]), (CUTS[1], C))
    crossing = jnp.logical_or(w == 0, w == W - 1)

    def cross(part):
        @pl.when(crossing)
        def _():
            copy_plane(-to_near, parts[part]).start()

    def send_tokens(which, reach):
        for i in (reach, ZC - reach):
            pl.semaphore_signal(
                tokens.at[which], inc=1, device_id=(ring_peer(i), gy), device_id_type=MESH
            )

    send_tokens(0, 2)
    for side in range(2):
        copy_row(0, side).start()
    copy_plane(to_near, (0, C)).start()
    cross(0)

    @pl.when(jnp.logical_not(crossing))
    def _():
        for part in parts:
            copy_plane(-to_near, part).start()

    for dz in (-1, 1):
        for side in range(2):
            copy_row(dz, side).start()
    def put_gains(source, pair):
        for part in range(2):
            for ky in range(4):
                for r in range(2):
                    row = pl.multiple_of(pair * 64 + ky * 16 + r * 8, 8)
                    gains[part, pl.ds(row, 8), 0:16] = source[part * 32 + ky * 8 : part * 32 + ky * 8 + 8, :]

    for load in loads[4:]:
        load.wait()
    gains[...] = jnp.zeros_like(gains)
    put_gains(filt, zc // 8)

    def put_rows(plane, slot):
        pad[plane, :, 7, :] = hrow[slot]
        pad[plane, :, 40, :] = hrow[slot + 1]

    def conv(plane, first, chans=(0, C)):
        def channels(step, carry):
            for k in range(4):
                c = step * 4 + k
                sums = [None, None, None]
                for b in range(3):
                    window = pad[plane, c, 7 + b : 39 + b, :]
                    for e in range(3):
                        term = depth_w[c, plane * 9 + b * 3 + e] * window
                        sums[e] = term if sums[e] is None else sums[e] + term
                value = sums[1] + pltpu.roll(sums[0], 1, 1) + pltpu.roll(sums[2], NX - 1, 1)
                depth[c] = value if first else depth[c] + value
            return carry

        lax.fori_loop(chans[0] // 4, chans[1] // 4, channels, 0)

    pl.semaphore_wait(tokens.at[0], 2)
    send_tokens(1, 4)

    pltpu.make_async_copy(recv1, recv1, r1).wait()
    for k in range(W):
        tmp[k * 8 : (k + 1) * 8, :] = (recv1[k] + recv1[8 + k]) + (recv1[16 + k] + recv1[24 + k])
    lower = iota((8, 128), 1) < 64
    for k in range(8):
        one = tmp[pl.ds(k // 2, 8, stride=8), :]
        two = tmp[pl.ds(k // 2 + 4, 8, stride=8), :]
        if k % 2 == 0:
            send2[k] = jnp.where(lower, one, pltpu.roll(two, 64, 1))
        else:
            send2[k] = jnp.where(lower, pltpu.roll(one, 64, 1), two)

    pl.semaphore_wait(tokens.at[1], 2)

    def copy2(k):
        i = 8 + (k + 1) // 2 * (2 * (k % 2) - 1)
        return pltpu.make_async_remote_copy(
            send2.at[(zc + i) % 8], recv2.at[zc], s2, r2,
            device_id=(ring_peer(i), gy), device_id_type=MESH,
        )

    def start2(k, carry):
        copy2(k).start()
        return carry

    copyf = pltpu.make_async_remote_copy(
        filt_in, filt2, sf, rf, device_id=(ring_peer(8), gy), device_id_type=MESH
    )
    copyf.start()
    lax.fori_loop(0, ZC - 1, start2, 0)
    own2 = pltpu.make_async_copy(send2.at[zc % 8], recv2.at[zc], r2)
    own2.start()

    cross(1)
    loads[3].wait()

    def wait_rows(index, count):
        part = hrow.at[0:count]
        pltpu.make_async_copy(part, part, rh.at[index]).wait()

    wait_rows(0, 2)
    put_rows(1, 2)
    conv(1, True)

    wait_rows(1, 4)
    near = jnp.where(core == 0, 2, 0)
    far = 2 - near
    pltpu.make_async_copy(field3, pad.at[near, :, 8:40, :], rz.at[near]).wait()
    put_rows(near, near * 2)
    conv(near, False)

    grow = (iota((256, C), 0) // 8 == iota((256, C), 1)).astype(F32).astype(BF16)
    grow_t = (iota((C, 256), 1) // 8 == iota((C, 256), 0)).astype(F32).astype(BF16)
    diagonal = iota((256, 256), 0) % 8 == iota((256, 256), 1) % 8
    mixers = []
    for part in split(point_w[...]):
        tall = dot(grow, part).astype(BF16)
        mixers.append(jnp.where(diagonal, dot(tall, grow_t), 0.0).astype(BF16))
    same_i = iota((8, YL, 128), 0) == iota((8, YL, 128), 2) % 8
    for which in range(4):
        base = tyi[which]
        filled = jnp.where(same_i, jnp.broadcast_to(base[None], (8, YL, 128)), 0.0)
        row = which // 2 * 256
        filled = filled.reshape(256, 128).astype(BF16)
        for k in (0, 1) if which % 2 == 0 else (2,):
            wide_yi[row : row + 256, k * 128 : (k + 1) * 128] = filled

    copyf.wait_recv()
    put_gains(filt2, 1 - zc // 8)
    gain_re = jnp.transpose(gains[0])[0:16, :]
    gain_im = jnp.transpose(gains[1])[0:16, :]
    pltpu.make_async_copy(recv2, recv2, r2).wait()
    a_high, a_low = split(recv2[...].reshape(NZ, 128))
    both = dot(tz[...], a_high) + dot(tz[...], a_low)
    modes = both[0:16] + both[32:48] + swapped(both[16:32] + both[48:64])
    filtered = modes * gain_re - swapped(modes) * gain_im
    stacked = jnp.concatenate([filtered, -swapped(filtered)], axis=0)
    f_high, f_low = split(stacked)
    both = dot(tzi[...], f_high) + dot(tzi[...], f_low)
    send4[...] = (both[0:128] + both[128:256]).reshape(ZC, 8, 128)

    def copy4(i):
        return pltpu.make_async_remote_copy(
            send4.at[(zc + i) % ZC], recv4.at[pl.ds(pl.multiple_of(zc % 8 * 8, 8), 8), :], s4, r4,
            device_id=(ring_peer(i), gy), device_id_type=MESH,
        )

    nearer = (ZC - 4, 3, ZC - 3, 2, ZC - 2, 1, ZC - 1)
    for i in nearer:
        copy4(i).start()
    own4 = pltpu.make_async_copy(
        send4.at[zc], recv4.at[pl.ds(pl.multiple_of(zc % 8 * 8, 8), 8), :], r4
    )
    own4.start()

    cross(2)
    def wait_plane(plane, chans, landed):
        part = pad.at[plane, chans[0] : chans[1], 8:40, :]
        pltpu.make_async_copy(part, part, rz.at[landed]).wait()

    wait_plane(far, (0, CUTS[1]), far)
    put_rows(far, far * 2)
    conv(far, False, (0, CUTS[1]))
    pltpu.make_async_copy(recv4, recv4, r4).wait()
    for k in range(W):
        even = recv4[pl.ds(k, 4, stride=16), :]
        odd = recv4[pl.ds(8 + k, 4, stride=16), :]
        tmp3[k, 0:4] = jnp.where(lower[0:4], even, pltpu.roll(odd, 64, 1))
        tmp3[k, 4:8] = jnp.where(lower[0:4], pltpu.roll(even, 64, 1), odd)

    def copy3(i):
        target, t = plane_peer(i)
        return pltpu.make_async_remote_copy(
            tmp3.at[t % W], recv3.at[w * 4 + gy], s3, r3,
            device_id=target, device_id_type=MESH,
        )

    def start3(i, carry):
        copy3(i).start()
        return carry

    plane_loop(start3)
    own3 = pltpu.make_async_copy(
        tmp3.at[w], recv3.at[w * 4 + gy], r3
    )
    own3.start()

    wait_plane(far, parts[2], 1)
    conv(far, False, parts[2])

    for k in range(YL // 8):
        d_high, d_low = split(depth[:, k * 8 : (k + 1) * 8, :].reshape(256, NX))
        value = dot(mixers[0], d_high) + dot(mixers[0], d_low) + dot(mixers[1], d_high)
        pacc[:, k * 8 : (k + 1) * 8, :] = value.reshape(C, 8, NX)

    def done1(i, carry):
        copy1(i).wait_send()
        copy3(i).wait_send()
        return carry

    def done2(k, carry):
        copy2(k).wait_send()
        return carry

    lax.fori_loop(1, 32, done1, 0)
    lax.fori_loop(0, ZC - 1, done2, 0)
    for i in nearer:
        copy4(i).wait_send()
    copyf.wait_send()
    for dz in (-1, 0, 1):
        for side in range(2):
            copy_row(dz, side).wait_send()
    copy_plane(to_near, (0, C)).wait_send()
    for part in parts:
        copy_plane(-to_near, part).wait_send()

    pltpu.make_async_copy(recv3, recv3, r3).wait()
    columns = []
    for p in range(2):
        rows = []
        for ky in range(MY):
            q, k4 = ky // 4, ky % 4
            value = moved(recv3[p * 16 + q], 0 - k4)
            for kxb in range(1, 4):
                value = jnp.where(block == kxb, moved(recv3[(p * 4 + kxb) * 4 + q], kxb - k4), value)
            rows.append(value)
        columns.append(jnp.concatenate(rows, axis=0))
    r_high, r_low = split(jnp.concatenate(columns, axis=1))
    value = dot(wide_yi[...], jnp.concatenate([r_high, r_low, r_high], axis=0))
    y_halves = split(value)
    puts = []
    for step in range(4):

        def gathered(half):
            real = half[step * 64 : (step + 1) * 64]
            imag = half[256 + step * 64 : 256 + (step + 1) * 64]
            return jnp.concatenate(
                [
                    jnp.concatenate(
                        [real[:, p * 128 : (p + 1) * 128], imag[:, p * 128 : (p + 1) * 128]], axis=1
                    )
                    for p in range(2)
                ],
                axis=0,
            )

        high, low = gathered(y_halves[0]), gathered(y_halves[1])
        spectral = dot(jnp.concatenate([high, low, high], axis=1), txi[...])
        for p in range(2):
            for sl in range(2):
                for ml in range(2):
                    ch = step * 8 + 4 * sl + 2 * ml + p
                    row = p * 64 + sl * 32
                    pacc[ch] = pacc[ch] + spectral[row : row + 32, ml * 256 : (ml + 1) * 256]
        chans = pl.ds(step * 8, 8)
        put = pltpu.make_async_copy(pacc.at[chans], done_out.at[chans], so.at[step])
        put.start()
        puts.append(put)
    for put in puts:
        put.wait()


def body(field, spectral_filter, depth_weight, point_weight, bias_vector):
    field3 = field.reshape(C, YL, NX)
    filt = spectral_filter.transpose(0, 2, 3, 1).reshape(64, 16)
    const = {name: jnp.asarray(value) for name, value in TABLES.items()}
    hbm = pl.BlockSpec(memory_space=pltpu.HBM)
    value = pl.pallas_call(
        wide_kernel,
        name="wide",
        out_shape=jax.ShapeDtypeStruct((C, YL, NX), F32),
        in_specs=[hbm] * 10,
        out_specs=hbm,
        scratch_shapes=[
            VMEM((C, YL, NX), F32),
            VMEM((64, 16), F32),
            VMEM((64, 16), F32),
            pltpu.SMEM((C, 27), F32),
            VMEM((C, C), F32),
            VMEM((2, 768, 256), BF16),
            VMEM((4, MY, 256), F32),
            VMEM((64, 128), BF16),
            VMEM((256, 32), BF16),
            VMEM((4, YL, 128), F32),
            VMEM((768, 512), BF16),
            VMEM((512, 384), BF16),
            VMEM((32, 8, 128), F32),
            VMEM((3, C, 48, NX), F32),
            VMEM((2, C, NX), F32),
            VMEM((6, C, NX), F32),
            VMEM((512, 256), BF16),
            VMEM((512, 256), BF16),
            VMEM((128, 256), F32),
            VMEM((32, 8, 128), F32),
            VMEM((32, 8, 128), F32),
            VMEM((64, 128), F32),
            VMEM((8, 8, 128), F32),
            VMEM((ZC, 8, 128), F32),
            VMEM((2, 128, 128), F32),
            VMEM((ZC, 8, 128), F32),
            VMEM((64, 128), F32),
            VMEM((W, 8, 128), F32),
            VMEM((C, YL, NX), F32),
            VMEM((C, YL, NX), F32),
            DMA((11,)), DMA, DMA, DMA, DMA((2,)), DMA, DMA((3,)), DMA, DMA, DMA, DMA, DMA, DMA, DMA((4,)), DMA, DMA,
            pltpu.SemaphoreType.REGULAR((2,)),
        ],
        compiler_params=pltpu.CompilerParams(
            collective_id=0, has_side_effects=True, vmem_limit_bytes=VMEM_ALL
        ),
    )(
        field3, filt, depth_weight, point_weight,
        const["tx"], const["ty"], const["tz"], const["tzi"], const["tyi"], const["txi"],
    )
    value = value.reshape(C, 1, YL, NX) + bias_vector[:, None, None, None]
    return 0.5 * value * (1.0 + lax.erf(value * (0.5**0.5)))


def solution(mesh):
    in_specs = (P(None, "gz", "gy", None), P(None, None, "gy", "gz"), P(), P(), P())
    out_specs = P(None, "gz", "gy", None)
    return jax.shard_map(body, mesh=mesh, in_specs=in_specs, out_specs=out_specs, check_vma=False)
```

```python
import functools

import jax
import jax.numpy as jnp
import ml_dtypes
import numpy as np
from jax import lax
from jax.experimental import pallas as pl
from jax.experimental.pallas import tpu as pltpu
from jax.sharding import PartitionSpec as P

C = 32
NX = 256
NY = 128
NZ = 128
MX = 32
MY = 16
MZ = 16
GY = 4
ZC = 16
W = 8
YL = NY // GY
VMEM_ALL = 67043328
CUTS = (12, 24)
MESH = pl.DeviceIdType.MESH
F32 = jnp.float32
BF16 = jnp.bfloat16
VMEM = pltpu.VMEM
DMA = pltpu.SemaphoreType.DMA


def halves(table):
    high = table.astype(ml_dtypes.bfloat16)
    low = (table - high.astype(np.float64)).astype(ml_dtypes.bfloat16)
    return high, low


def kept(count, total):
    series = np.arange(count)
    return np.where(series < count // 2, series, total - count + series)


def make_tables():
    tables = {}
    angle = 2 * np.pi * (np.arange(NX)[:, None] * np.arange(MX)[None, :] % NX) / NX
    cos = np.cos(angle).reshape(NX, 4, 8)
    sin = np.sin(angle).reshape(NX, 4, 8)
    plain = np.stack([cos, -sin], axis=2).reshape(NX, 64)
    swapped = np.stack([-sin, -cos], axis=2).reshape(NX, 64)
    zero = np.zeros_like(plain)
    tx = np.stack(
        [
            np.concatenate([plain, zero, swapped, zero], axis=1),
            np.concatenate([zero, plain, zero, swapped], axis=1),
        ]
    )
    high, low = halves(tx)
    tables["tx"] = np.concatenate([high, high, low], axis=1)
    places = np.arange(NY)
    angle = 2 * np.pi * (kept(MY, NY)[:, None] * places[None, :] % NY) / NY
    parts = []
    for value in (np.cos(angle), np.sin(angle)):
        parts.extend(part.astype(np.float32) for part in halves(value))
    stack = np.stack(parts)
    mine = stack.reshape(4, MY, GY, YL).transpose(2, 0, 1, 3)
    tables["ty"] = np.tile(mine, (1, 1, 1, 8))
    tables["tyi"] = np.repeat(mine.transpose(0, 1, 3, 2), 8, axis=3)
    angle = 2 * np.pi * (kept(MZ, NZ)[:, None] * np.arange(NZ)[None, :] % NZ) / NZ
    high, low = halves(np.concatenate([np.cos(angle), np.sin(angle)], axis=0))
    both = np.concatenate([high, low], axis=0)
    tables["tz"] = np.concatenate([both, both], axis=1)
    scale = (NX * NY * NZ) ** -0.5 * (2.0 * MX * MY * MZ) ** -0.5
    both = np.concatenate([np.cos(angle), np.sin(angle)], axis=0).T * scale
    both = np.concatenate(halves(both), axis=0)
    tables["tzi"] = np.concatenate([both, both], axis=1)
    weight = np.where(np.arange(MX) == 0, 1.0, 2.0)[:, None]
    angle = 2 * np.pi * (np.arange(MX)[:, None] * np.arange(NX)[None, :] % NX) / NX
    cos = (weight * np.cos(angle)).reshape(4, 8, NX)
    sin = (weight * np.sin(angle)).reshape(4, 8, NX)
    from_c = np.stack([cos, -sin], axis=1).reshape(64, NX)
    from_s = np.stack([-sin, -cos], axis=1).reshape(64, NX)
    zero = np.zeros_like(from_c)
    txi = np.block([[from_c, zero], [zero, from_c], [from_s, zero], [zero, from_s]])
    high, low = halves(txi)
    tables["txi"] = np.concatenate([high, high, low], axis=0)
    return tables


TABLES = make_tables()


def split(value):
    high = value.astype(BF16)
    return high, (value - high.astype(F32)).astype(BF16)


def dot(left, right):
    return jnp.dot(left, right, preferred_element_type=F32)


def iota(shape, dim):
    return lax.broadcasted_iota(jnp.int32, shape, dim)


def swapped(value):
    pieces = []
    for k in range(value.shape[1] // 128):
        piece = value[:, k * 128 : (k + 1) * 128]
        real_lane = iota(piece.shape, 1) % 16 < 8
        pieces.append(jnp.where(real_lane, pltpu.roll(piece, 120, 1), -pltpu.roll(piece, 8, 1)))
    return jnp.concatenate(pieces, axis=1)


def moved(value, blocks):
    return value if blocks % 8 == 0 else pltpu.roll(value, blocks % 8 * 16, 1)


def wide_kernel(
    field3, filt_in, depth_in, point_in, tx_in, ty_in, tz_in, tzi_in,
    recv3, point_out,
    fv, filt, filt2, depth_w, point_w, tx, ty, tz, tzi,
    pad, edge, hrow, xh, xl, yout, send1, recv1, tmp, send2, recv2, gains,
    send4, recv4, tmp3, depth, pacc,
    ld_sem, s1, r1, sh, rh, sz, rz, s2, r2, s4, r4, s3, r3, so, sf, rf, tokens,
):
    gz = lax.axis_index("gz")
    gy = lax.axis_index("gy")
    zc = lax.div(gz, W)
    w = lax.rem(gz, W)
    core = lax.rem(gz, 2)
    me = gy * W + w

    ws = [w] + [lax.rem(w + k, W) for k in range(1, W)]
    gys = [gy] + [lax.rem(gy + k, GY) for k in range(1, GY)]
    zs = [zc] + [lax.rem(zc + k, ZC) for k in range(1, ZC)]
    first_gz = gz - w
    plane_peers = [(dx, dw) for dx in (2, 1, 3, 0) for dw in (4, 3, 5, 2, 6, 1, 7, 0) if dx or dw]

    def plane_peer(peer):
        dx, dw = peer
        return (first_gz + ws[dw], gys[dx]), gys[dx] * W + ws[dw]

    def ring_peer(i):
        return zs[i] * W + w

    def halo_peer(dz, dy):
        return (lax.rem(gz + (NZ + dz), NZ), gys[dy % GY])

    barrier = pltpu.get_barrier_semaphore()

    def signal(target):
        pl.semaphore_signal(barrier, inc=1, device_id=target, device_id_type=MESH)

    loads = [
        pltpu.make_async_copy(src, dst, ld_sem.at[k])
        for k, (src, dst) in enumerate(
            [
                (field3, fv),
                (tx_in, tx),
                (ty_in.at[gy], ty),
                (field3, pad.at[1, :, 8:40, :]),
                (filt_in, filt),
                (depth_in, depth_w),
                (point_in, point_w),
                (tz_in, tz),
                (tzi_in, tzi),
            ]
        )
    ]
    for load in loads[:3]:
        load.start()
    for i in (2, ZC - 2, 1, ZC - 1):
        signal((ring_peer(i), gy))
    for dz in (-1, 1):
        for dy in (-1, 0, 1):
            signal(halo_peer(dz, dy))
    for peer in plane_peers:
        signal(plane_peer(peer)[0])
    loads[0].wait()
    for load in loads[3:]:
        load.start()
    for side, row in ((0, YL - 1), (1, 0)):
        edge[side] = fv[:, row, :]

    loads[1].wait()
    loads[2].wait()
    for p in range(2):
        total = None
        for ml in range(2):
            g = 2 * ml + p
            rows = jnp.concatenate(
                [fv[4 * s + g] for s in range(8)], axis=0
            )
            high, low = split(rows)
            value = dot(jnp.concatenate([high, low, high], axis=1), tx[ml])
            total = value if total is None else total + value
        high, low = split(total)
        for part in range(2):
            xh[part * 256 : (part + 1) * 256, p * 128 : (p + 1) * 128] = high[:, part * 128 : (part + 1) * 128]
            xl[part * 256 : (part + 1) * 256, p * 128 : (p + 1) * 128] = low[:, part * 128 : (part + 1) * 128]
    same = iota((MY, 8, 256), 1) == iota((MY, 8, 256), 2) // YL

    def spread(which):
        base = ty[which]
        wide = jnp.where(same, jnp.broadcast_to(base[:, None, :], (MY, 8, 256)), 0.0)
        return wide.reshape(128, 256).astype(BF16)

    y_high = jnp.concatenate([spread(0), spread(2)], axis=1)
    y_low = jnp.concatenate([spread(1), spread(3)], axis=1)
    y_both = jnp.concatenate([y_high, y_low], axis=0)
    result = dot(y_both, xh[...]) + dot(y_both, xl[...])
    yout[...] = result[0:128] + result[128:256]
    block = iota((8, 128), 1) // 16 % 4
    for p in range(2):
        for q in range(4):
            quad = [
                yout[(q * 4 + ky) * 8 : (q * 4 + ky + 1) * 8, p * 128 : (p + 1) * 128]
                for ky in range(4)
            ]
            for kxb in range(4):
                out = moved(quad[0], 0 - kxb)
                for ky in range(1, 4):
                    out = jnp.where(block == ky, moved(quad[ky], ky - kxb), out)
                send1[q * 8 + p * 4 + kxb] = out

    pl.semaphore_wait(barrier, 4 + 6 + 31)

    def copy1(i):
        target, t = plane_peer(i)
        return pltpu.make_async_remote_copy(
            send1.at[t], recv1.at[me], s1, r1, device_id=target, device_id_type=MESH
        )

    for peer in plane_peers:
        copy1(peer).start()
    own1 = pltpu.make_async_copy(send1.at[me], recv1.at[me], r1)
    own1.start()

    def copy_row(dz, side):
        dy = 1 if side == 0 else -1
        slot = (1 - dz) * 2 + side
        return pltpu.make_async_remote_copy(
            edge.at[side], hrow.at[slot], sh, rh.at[0 if dz == 0 else 1],
            device_id=halo_peer(dz, dy), device_id_type=MESH,
        )

    to_near = 1 - 2 * core

    def copy_plane(dz, chans):
        landed = 1 - dz if chans[0] == 0 else 1
        return pltpu.make_async_remote_copy(
            field3.at[chans[0] : chans[1]], pad.at[1 - dz, chans[0] : chans[1], 8:40, :], sz, rz.at[landed],
            device_id=halo_peer(dz, 0), device_id_type=MESH,
        )

    parts = ((0, CUTS[0]), (CUTS[0], CUTS[1]), (CUTS[1], C))
    crossing = jnp.logical_or(w == 0, w == W - 1)

    def cross(part):
        @pl.when(crossing)
        def _():
            copy_plane(-to_near, parts[part]).start()

    def send_tokens(which, reach):
        for i in (reach, ZC - reach):
            pl.semaphore_signal(
                tokens.at[which], inc=1, device_id=(ring_peer(i), gy), device_id_type=MESH
            )

    send_tokens(0, 2)
    for side in range(2):
        copy_row(0, side).start()
    copy_plane(to_near, (0, C)).start()
    cross(0)

    @pl.when(jnp.logical_not(crossing))
    def _():
        for part in parts:
            copy_plane(-to_near, part).start()

    for dz in (-1, 1):
        for side in range(2):
            copy_row(dz, side).start()
    def put_gains(source, pair):
        for part in range(2):
            for ky in range(4):
                for r in range(2):
                    row = pl.multiple_of(pair * 64 + ky * 16 + r * 8, 8)
                    gains[part, pl.ds(row, 8), 0:16] = source[part * 32 + ky * 8 : part * 32 + ky * 8 + 8, :]

    for load in loads[4:]:
        load.wait()
    gains[...] = jnp.zeros_like(gains)
    put_gains(filt, lax.div(zc, 8))

    def put_rows(plane, slot):
        pad[plane, :, 7, :] = hrow[slot]
        pad[plane, :, 40, :] = hrow[slot + 1]

    def conv(plane, first, chans=(0, C)):
        def channels(step, carry):
            for k in range(4):
                c = step * 4 + k
                sums = [None, None, None]
                for b in range(3):
                    window = pad[plane, c, 7 + b : 39 + b, :]
                    for e in range(3):
                        term = depth_w[c, plane * 9 + b * 3 + e] * window
                        sums[e] = term if sums[e] is None else sums[e] + term
                value = sums[1] + pltpu.roll(sums[0], 1, 1) + pltpu.roll(sums[2], NX - 1, 1)
                depth[c] = value if first else depth[c] + value
            return carry

        lax.fori_loop(chans[0] // 4, chans[1] // 4, channels, 0)

    pl.semaphore_wait(tokens.at[0], 2)
    send_tokens(1, 4)

    pltpu.make_async_copy(recv1, recv1, r1).wait()
    for k in range(W):
        tmp[k * 8 : (k + 1) * 8, :] = (recv1[k] + recv1[8 + k]) + (recv1[16 + k] + recv1[24 + k])
    lower = iota((8, 128), 1) < 64
    for k in range(8):
        one = tmp[pl.ds(k // 2, 8, stride=8), :]
        two = tmp[pl.ds(k // 2 + 4, 8, stride=8), :]
        if k % 2 == 0:
            send2[k] = jnp.where(lower, one, pltpu.roll(two, 64, 1))
        else:
            send2[k] = jnp.where(lower, pltpu.roll(one, 64, 1), two)

    far_first = (8, 7, 9, 6, 10, 5, 11, 4, 12, 3, 13, 2, 14, 1, 15)
    pl.semaphore_wait(tokens.at[1], 2)

    def copy2(i):
        return pltpu.make_async_remote_copy(
            send2.at[lax.rem(zs[i], 8)], recv2.at[zc], s2, r2,
            device_id=(ring_peer(i), gy), device_id_type=MESH,
        )

    copyf = pltpu.make_async_remote_copy(
        filt_in, filt2, sf, rf, device_id=(ring_peer(8), gy), device_id_type=MESH
    )
    copyf.start()
    for i in far_first:
        copy2(i).start()
    own2 = pltpu.make_async_copy(send2.at[lax.rem(zc, 8)], recv2.at[zc], r2)
    own2.start()

    cross(1)
    loads[3].wait()

    def wait_rows(index, count):
        part = hrow.at[0:count]
        pltpu.make_async_copy(part, part, rh.at[index]).wait()

    wait_rows(0, 2)
    put_rows(1, 2)
    conv(1, True)

    wait_rows(1, 4)
    near = jnp.where(core == 0, 2, 0)
    far = 2 - near
    pltpu.make_async_copy(field3, pad.at[near, :, 8:40, :], rz.at[near]).wait()
    put_rows(near, near * 2)
    conv(near, False)

    grow = (iota((256, C), 0) // 8 == iota((256, C), 1)).astype(F32).astype(BF16)
    grow_t = (iota((C, 256), 1) // 8 == iota((C, 256), 0)).astype(F32).astype(BF16)
    diagonal = iota((256, 256), 0) % 8 == iota((256, 256), 1) % 8
    mixers = []
    for part in split(point_w[...]):
        tall = dot(grow, part).astype(BF16)
        mixers.append(jnp.where(diagonal, dot(tall, grow_t), 0.0).astype(BF16))
    copyf.wait_recv()
    put_gains(filt2, 1 - lax.div(zc, 8))
    gain_re = jnp.transpose(gains[0])[0:16, :]
    gain_im = jnp.transpose(gains[1])[0:16, :]
    pltpu.make_async_copy(recv2, recv2, r2).wait()
    a_high, a_low = split(recv2[...].reshape(NZ, 128))
    both = dot(tz[...], jnp.concatenate([a_high, a_low], axis=0))
    modes = both[0:16] + both[32:48] + swapped(both[16:32] + both[48:64])
    filtered = modes * gain_re - swapped(modes) * gain_im
    stacked = jnp.concatenate([filtered, -swapped(filtered)], axis=0)
    f_high, f_low = split(stacked)
    both = dot(tzi[...], jnp.concatenate([f_high, f_low], axis=0))
    send4[...] = (both[0:128] + both[128:256]).reshape(ZC, 8, 128)

    def copy4(i):
        return pltpu.make_async_remote_copy(
            send4.at[zs[i]], recv4.at[pl.ds(pl.multiple_of(lax.rem(zc, 8) * 8, 8), 8), :], s4, r4,
            device_id=(ring_peer(i), gy), device_id_type=MESH,
        )

    nearer = (ZC - 4, 3, ZC - 3, 2, ZC - 2, 1, ZC - 1)
    for i in nearer:
        copy4(i).start()
    own4 = pltpu.make_async_copy(
        send4.at[zc], recv4.at[pl.ds(pl.multiple_of(lax.rem(zc, 8) * 8, 8), 8), :], r4
    )
    own4.start()

    cross(2)
    def wait_plane(plane, chans, landed):
        part = pad.at[plane, chans[0] : chans[1], 8:40, :]
        pltpu.make_async_copy(part, part, rz.at[landed]).wait()

    wait_plane(far, parts[0], far)
    put_rows(far, far * 2)
    conv(far, False, parts[0])
    pltpu.make_async_copy(recv4, recv4, r4).wait()
    for k in range(W):
        even = recv4[pl.ds(k, 4, stride=16), :]
        odd = recv4[pl.ds(8 + k, 4, stride=16), :]
        tmp3[k, 0:4] = jnp.where(lower[0:4], even, pltpu.roll(odd, 64, 1))
        tmp3[k, 4:8] = jnp.where(lower[0:4], pltpu.roll(even, 64, 1), odd)

    def copy3(i):
        target, t = plane_peer(i)
        return pltpu.make_async_remote_copy(
            tmp3.at[ws[i[1]]], recv3.at[w * 4 + gy], s3, r3,
            device_id=target, device_id_type=MESH,
        )

    for peer in plane_peers:
        copy3(peer).start()
    own3 = pltpu.make_async_copy(
        tmp3.at[w], recv3.at[w * 4 + gy], r3
    )
    own3.start()

    wait_plane(far, (CUTS[0], C), 1)
    conv(far, False, (CUTS[0], C))

    for k in range(YL // 8):
        d_high, d_low = split(depth[:, k * 8 : (k + 1) * 8, :].reshape(256, NX))
        value = dot(mixers[0], d_high) + dot(mixers[0], d_low) + dot(mixers[1], d_high)
        pacc[:, k * 8 : (k + 1) * 8, :] = value.reshape(C, 8, NX)
    put = pltpu.make_async_copy(pacc, point_out, so)
    put.start()

    for peer in plane_peers:
        copy1(peer).wait_send()
        copy3(peer).wait_send()
    for i in far_first:
        copy2(i).wait_send()
    for i in nearer:
        copy4(i).wait_send()
    copyf.wait_send()
    for dz in (-1, 0, 1):
        for side in range(2):
            copy_row(dz, side).wait_send()
    copy_plane(to_near, (0, C)).wait_send()
    for part in parts:
        copy_plane(-to_near, part).wait_send()

    pltpu.make_async_copy(recv3, recv3, r3).wait()
    put.wait()


def last_kernel(
    tiles_in, point_in, tyi_in, txi_in, bias_in, done_out,
    tiles, point, tyi, txi, bias, wide_yi, ld_sem, pt_sem, so,
):
    gy = lax.axis_index("gy")
    loads = [
        pltpu.make_async_copy(src, dst, ld_sem.at[k])
        for k, (src, dst) in enumerate(
            [(tyi_in.at[gy], tyi), (tiles_in, tiles), (bias_in, bias), (txi_in, txi)]
        )
    ]
    quarters = [pl.ds(k * 8, 8) for k in range(4)]
    points = [
        pltpu.make_async_copy(point_in.at[q], point.at[q], pt_sem.at[k]) for k, q in enumerate(quarters)
    ]
    for load in loads + points:
        load.start()
    block = iota((8, 128), 1) // 16 % 4
    same_i = iota((8, YL, 128), 0) == iota((8, YL, 128), 2) % 8
    loads[0].wait()
    for which in range(4):
        base = tyi[which]
        filled = jnp.where(same_i, jnp.broadcast_to(base[None], (8, YL, 128)), 0.0)
        row = which // 2 * 256
        filled = filled.reshape(256, 128).astype(BF16)
        for k in (0, 1) if which % 2 == 0 else (2,):
            wide_yi[row : row + 256, k * 128 : (k + 1) * 128] = filled
    loads[1].wait()
    loads[2].wait()
    columns = []
    for p in range(2):
        rows = []
        for ky in range(MY):
            q, k4 = ky // 4, ky % 4
            value = moved(tiles[p * 16 + q], 0 - k4)
            for kxb in range(1, 4):
                value = jnp.where(block == kxb, moved(tiles[(p * 4 + kxb) * 4 + q], kxb - k4), value)
            rows.append(value)
        columns.append(jnp.concatenate(rows, axis=0))
    r_high, r_low = split(jnp.concatenate(columns, axis=1))
    value = dot(wide_yi[...], jnp.concatenate([r_high, r_low, r_high], axis=0))
    y_halves = split(value)
    loads[3].wait()
    puts = []
    for step in range(4):
        points[step].wait()

        def gathered(half):
            real = half[step * 64 : (step + 1) * 64]
            imag = half[256 + step * 64 : 256 + (step + 1) * 64]
            return jnp.concatenate(
                [
                    jnp.concatenate(
                        [real[:, p * 128 : (p + 1) * 128], imag[:, p * 128 : (p + 1) * 128]], axis=1
                    )
                    for p in range(2)
                ],
                axis=0,
            )

        high, low = gathered(y_halves[0]), gathered(y_halves[1])
        spectral = dot(jnp.concatenate([high, low, high], axis=1), txi[...])
        for p in range(2):
            for sl in range(2):
                for ml in range(2):
                    ch = step * 8 + 4 * sl + 2 * ml + p
                    row = p * 64 + sl * 32
                    value = point[ch] + spectral[row : row + 32, ml * 256 : (ml + 1) * 256] + bias[0, ch]
                    point[ch] = 0.5 * value * (1.0 + lax.erf(value * (0.5**0.5)))
        chans = pl.ds(step * 8, 8)
        put = pltpu.make_async_copy(point.at[chans], done_out.at[chans], so.at[step])
        put.start()
        puts.append(put)
    for put in puts:
        put.wait()


def body(field, spectral_filter, depth_weight, point_weight, bias_vector):
    field3 = field.reshape(C, YL, NX)
    filt = spectral_filter.transpose(0, 2, 3, 1).reshape(64, 16)
    const = {name: jnp.asarray(value) for name, value in TABLES.items()}
    hbm = pl.BlockSpec(memory_space=pltpu.HBM)
    tiles, point = pl.pallas_call(
        wide_kernel,
        name="wide",
        out_shape=(
            jax.ShapeDtypeStruct((32, 8, 128), F32),
            jax.ShapeDtypeStruct((C, YL, NX), F32),
        ),
        in_specs=[hbm] * 8,
        out_specs=(hbm, hbm),
        scratch_shapes=[
            VMEM((C, YL, NX), F32),
            VMEM((64, 16), F32),
            VMEM((64, 16), F32),
            pltpu.SMEM((C, 27), F32),
            VMEM((C, C), F32),
            VMEM((2, 768, 256), BF16),
            VMEM((4, MY, 256), F32),
            VMEM((64, 256), BF16),
            VMEM((256, 64), BF16),
            VMEM((3, C, 48, NX), F32),
            VMEM((2, C, NX), F32),
            VMEM((6, C, NX), F32),
            VMEM((512, 256), BF16),
            VMEM((512, 256), BF16),
            VMEM((128, 256), F32),
            VMEM((32, 8, 128), F32),
            VMEM((32, 8, 128), F32),
            VMEM((64, 128), F32),
            VMEM((8, 8, 128), F32),
            VMEM((ZC, 8, 128), F32),
            VMEM((2, 128, 128), F32),
            VMEM((ZC, 8, 128), F32),
            VMEM((64, 128), F32),
            VMEM((W, 8, 128), F32),
            VMEM((C, YL, NX), F32),
            VMEM((C, YL, NX), F32),
            DMA((9,)), DMA, DMA, DMA, DMA((2,)), DMA, DMA((3,)), DMA, DMA, DMA, DMA, DMA, DMA, DMA, DMA, DMA,
            pltpu.SemaphoreType.REGULAR((2,)),
        ],
        compiler_params=pltpu.CompilerParams(
            collective_id=0, has_side_effects=True, vmem_limit_bytes=VMEM_ALL
        ),
    )(
        field3, filt, depth_weight, point_weight,
        const["tx"], const["ty"], const["tz"], const["tzi"],
    )
    value = pl.pallas_call(
        last_kernel,
        name="last",
        out_shape=jax.ShapeDtypeStruct((C, YL, NX), F32),
        in_specs=[hbm] * 5,
        out_specs=hbm,
        scratch_shapes=[
            VMEM((32, 8, 128), F32),
            VMEM((C, YL, NX), F32),
            VMEM((4, YL, 128), F32),
            VMEM((768, 512), BF16),
            pltpu.SMEM((1, C), F32),
            VMEM((512, 384), BF16),
            DMA((4,)), DMA((4,)), DMA((4,)),
        ],
        compiler_params=pltpu.CompilerParams(vmem_limit_bytes=VMEM_ALL),
    )(tiles, point, const["tyi"], const["txi"], bias_vector.reshape(1, C))
    return value.reshape(C, 1, YL, NX)


def solution(mesh):
    in_specs = (P(None, "gz", "gy", None), P(None, None, "gy", "gz"), P(), P(), P())
    out_specs = P(None, "gz", "gy", None)
    return jax.shard_map(body, mesh=mesh, in_specs=in_specs, out_specs=out_specs, check_vma=False)
```

```python
import functools

import jax
import jax.numpy as jnp
import ml_dtypes
import numpy as np
from jax import lax
from jax.experimental import pallas as pl
from jax.experimental.pallas import tpu as pltpu
from jax.sharding import PartitionSpec as P

C = 32
NX = 256
NY = 128
NZ = 128
MX = 32
MY = 16
MZ = 16
GY = 4
ZC = 16
W = 8
YL = NY // GY
VMEM_ALL = 67043328
CUTS = (8, 24)
MESH = pl.DeviceIdType.MESH
F32 = jnp.float32
BF16 = jnp.bfloat16
VMEM = pltpu.VMEM
DMA = pltpu.SemaphoreType.DMA


def halves(table):
    high = table.astype(ml_dtypes.bfloat16)
    low = (table - high.astype(np.float64)).astype(ml_dtypes.bfloat16)
    return high, low


def kept(count, total):
    series = np.arange(count)
    return np.where(series < count // 2, series, total - count + series)


def make_tables():
    tables = {}
    angle = 2 * np.pi * (np.arange(NX)[:, None] * np.arange(MX)[None, :] % NX) / NX
    cos = np.cos(angle).reshape(NX, 4, 8)
    sin = np.sin(angle).reshape(NX, 4, 8)
    plain = np.stack([cos, -sin], axis=2).reshape(NX, 64)
    swapped = np.stack([-sin, -cos], axis=2).reshape(NX, 64)
    zero = np.zeros_like(plain)
    tx = np.stack(
        [
            np.concatenate([plain, zero, swapped, zero], axis=1),
            np.concatenate([zero, plain, zero, swapped], axis=1),
        ]
    )
    high, low = halves(tx)
    tables["tx"] = np.concatenate([high, high, low], axis=1)
    places = np.arange(NY)
    angle = 2 * np.pi * (kept(MY, NY)[:, None] * places[None, :] % NY) / NY
    parts = []
    for value in (np.cos(angle), np.sin(angle)):
        parts.extend(part.astype(np.float32) for part in halves(value))
    stack = np.stack(parts)
    mine = stack.reshape(4, MY, GY, YL).transpose(2, 0, 1, 3)
    tables["ty"] = np.tile(mine, (1, 1, 1, 8))
    tables["tyi"] = np.repeat(mine.transpose(0, 1, 3, 2), 8, axis=3)
    angle = 2 * np.pi * (kept(MZ, NZ)[:, None] * np.arange(NZ)[None, :] % NZ) / NZ
    high, low = halves(np.concatenate([np.cos(angle), np.sin(angle)], axis=0))
    both = np.concatenate([high, low], axis=0)
    tables["tz"] = np.concatenate([both, both], axis=1)
    scale = (NX * NY * NZ) ** -0.5 * (2.0 * MX * MY * MZ) ** -0.5
    both = np.concatenate([np.cos(angle), np.sin(angle)], axis=0).T * scale
    both = np.concatenate(halves(both), axis=0)
    tables["tzi"] = np.concatenate([both, both], axis=1)
    weight = np.where(np.arange(MX) == 0, 1.0, 2.0)[:, None]
    angle = 2 * np.pi * (np.arange(MX)[:, None] * np.arange(NX)[None, :] % NX) / NX
    cos = (weight * np.cos(angle)).reshape(4, 8, NX)
    sin = (weight * np.sin(angle)).reshape(4, 8, NX)
    from_c = np.stack([cos, -sin], axis=1).reshape(64, NX)
    from_s = np.stack([-sin, -cos], axis=1).reshape(64, NX)
    zero = np.zeros_like(from_c)
    txi = np.block([[from_c, zero], [zero, from_c], [from_s, zero], [zero, from_s]])
    high, low = halves(txi)
    tables["txi"] = np.concatenate([high, high, low], axis=0)
    return tables


TABLES = make_tables()


def split(value):
    high = value.astype(BF16)
    return high, (value - high.astype(F32)).astype(BF16)


def dot(left, right):
    return jnp.dot(left, right, preferred_element_type=F32)


def iota(shape, dim):
    return lax.broadcasted_iota(jnp.int32, shape, dim)


def swapped(value):
    pieces = []
    for k in range(value.shape[1] // 128):
        piece = value[:, k * 128 : (k + 1) * 128]
        real_lane = iota(piece.shape, 1) % 16 < 8
        pieces.append(jnp.where(real_lane, pltpu.roll(piece, 120, 1), -pltpu.roll(piece, 8, 1)))
    return jnp.concatenate(pieces, axis=1)


def moved(value, blocks):
    return value if blocks % 8 == 0 else pltpu.roll(value, blocks % 8 * 16, 1)


def wide_kernel(
    field3, filt_in, depth_in, point_in, tx_in, ty_in, tz_in, tzi_in,
    recv3, point_out,
    fv, filt, fwide, ftile, ftile2, depth_w, point_w, tx, ty, tz, tzi,
    pad, edge, hrow, xh, xl, yout, send1, recv1, tmp, send2, recv2, gains,
    send4, recv4, tmp3, depth, pacc,
    ld_sem, s1, r1, sh, rh, sz, rz, s2, r2, s4, r4, s3, r3, so, sf, rf, tokens,
):
    gz = lax.axis_index("gz")
    gy = lax.axis_index("gy")
    zc = lax.div(gz, W)
    w = lax.rem(gz, W)
    core = lax.rem(gz, 2)
    me = gy * W + w

    ws = [w] + [lax.rem(w + k, W) for k in range(1, W)]
    gys = [gy] + [lax.rem(gy + k, GY) for k in range(1, GY)]
    zs = [zc] + [lax.rem(zc + k, ZC) for k in range(1, ZC)]
    first_gz = gz - w
    plane_peers = [(dx, dw) for dx in (2, 1, 3, 0) for dw in (4, 3, 5, 2, 6, 1, 7, 0) if dx or dw]

    def plane_peer(peer):
        dx, dw = peer
        return (first_gz + ws[dw], gys[dx]), gys[dx] * W + ws[dw]

    def ring_peer(i):
        return zs[i] * W + w

    def halo_peer(dz, dy):
        return (lax.rem(gz + (NZ + dz), NZ), gys[dy % GY])

    barrier = pltpu.get_barrier_semaphore()

    def signal(target):
        pl.semaphore_signal(barrier, inc=1, device_id=target, device_id_type=MESH)

    loads = [
        pltpu.make_async_copy(src, dst, ld_sem.at[k])
        for k, (src, dst) in enumerate(
            [
                (field3, fv),
                (tx_in, tx),
                (ty_in.at[gy], ty),
                (field3, pad.at[1, :, 8:40, :]),
                (filt_in, filt),
                (depth_in, depth_w),
                (point_in, point_w),
                (tz_in, tz),
                (tzi_in, tzi),
            ]
        )
    ]
    for load in loads[:3]:
        load.start()
    for i in (2, ZC - 2, 1, ZC - 1):
        signal((ring_peer(i), gy))
    for dz in (-1, 1):
        for dy in (-1, 0, 1):
            signal(halo_peer(dz, dy))
    for peer in plane_peers:
        signal(plane_peer(peer)[0])
    loads[0].wait()
    for load in loads[3:]:
        load.start()
    for side, row in ((0, YL - 1), (1, 0)):
        edge[side] = fv[:, row, :]

    loads[1].wait()
    loads[2].wait()
    for p in range(2):
        total = None
        for ml in range(2):
            g = 2 * ml + p
            rows = jnp.concatenate(
                [fv[4 * s + g] for s in range(8)], axis=0
            )
            high, low = split(rows)
            value = dot(jnp.concatenate([high, low, high], axis=1), tx[ml])
            total = value if total is None else total + value
        high, low = split(total)
        for part in range(2):
            xh[part * 256 : (part + 1) * 256, p * 128 : (p + 1) * 128] = high[:, part * 128 : (part + 1) * 128]
            xl[part * 256 : (part + 1) * 256, p * 128 : (p + 1) * 128] = low[:, part * 128 : (part + 1) * 128]
    same = iota((MY, 8, 256), 1) == iota((MY, 8, 256), 2) // YL

    def spread(which):
        base = ty[which]
        wide = jnp.where(same, jnp.broadcast_to(base[:, None, :], (MY, 8, 256)), 0.0)
        return wide.reshape(128, 256).astype(BF16)

    y_high = jnp.concatenate([spread(0), spread(2)], axis=1)
    y_low = jnp.concatenate([spread(1), spread(3)], axis=1)
    y_both = jnp.concatenate([y_high, y_low], axis=0)
    result = dot(y_both, xh[...]) + dot(y_both, xl[...])
    yout[...] = result[0:128] + result[128:256]
    block = iota((8, 128), 1) // 16 % 4
    for p in range(2):
        for q in range(4):
            quad = [
                yout[(q * 4 + ky) * 8 : (q * 4 + ky + 1) * 8, p * 128 : (p + 1) * 128]
                for ky in range(4)
            ]
            for kxb in range(4):
                out = moved(quad[0], 0 - kxb)
                for ky in range(1, 4):
                    out = jnp.where(block == ky, moved(quad[ky], ky - kxb), out)
                send1[q * 8 + p * 4 + kxb] = out

    pl.semaphore_wait(barrier, 4 + 6 + 31)

    def copy1(i):
        target, t = plane_peer(i)
        return pltpu.make_async_remote_copy(
            send1.at[t], recv1.at[me], s1, r1, device_id=target, device_id_type=MESH
        )

    for peer in plane_peers:
        copy1(peer).start()
    own1 = pltpu.make_async_copy(send1.at[me], recv1.at[me], r1)
    own1.start()

    def copy_row(dz, side):
        dy = 1 if side == 0 else -1
        slot = (1 - dz) * 2 + side
        return pltpu.make_async_remote_copy(
            edge.at[side], hrow.at[slot], sh, rh.at[0 if dz == 0 else 1],
            device_id=halo_peer(dz, dy), device_id_type=MESH,
        )

    to_near = 1 - 2 * core

    def copy_plane(dz, chans):
        landed = 1 - dz if chans[0] == 0 else 1
        return pltpu.make_async_remote_copy(
            field3.at[chans[0] : chans[1]], pad.at[1 - dz, chans[0] : chans[1], 8:40, :], sz, rz.at[landed],
            device_id=halo_peer(dz, 0), device_id_type=MESH,
        )

    parts = ((0, CUTS[0]), (CUTS[0], CUTS[1]), (CUTS[1], C))
    crossing = jnp.logical_or(w == 0, w == W - 1)

    def cross(part):
        @pl.when(crossing)
        def _():
            copy_plane(-to_near, parts[part]).start()

    def send_tokens(which, reach):
        for i in (reach, ZC - reach):
            pl.semaphore_signal(
                tokens.at[which], inc=1, device_id=(ring_peer(i), gy), device_id_type=MESH
            )

    send_tokens(0, 2)
    for side in range(2):
        copy_row(0, side).start()
    copy_plane(to_near, (0, C)).start()
    cross(0)

    @pl.when(jnp.logical_not(crossing))
    def _():
        for part in parts:
            copy_plane(-to_near, part).start()

    for dz in (-1, 1):
        for side in range(2):
            copy_row(dz, side).start()
    def put_gains(tile, pair):
        for part in range(2):
            for ky in range(4):
                k = part * 4 + ky
                value = tile if k == 0 else pltpu.roll(tile, 128 - k * 16, 1)
                for r in range(2):
                    row = pl.multiple_of(pair * 64 + ky * 16 + r * 8, 8)
                    gains[part, pl.ds(row, 8), :] = value

    for load in loads[4:]:
        load.wait()
    fwide[:, 0:16] = filt[...]
    tile = fwide[0:8, :]
    for k in range(1, 8):
        moved_in = pltpu.roll(fwide[k * 8 : k * 8 + 8, :], k * 16, 1)
        tile = jnp.where(iota((8, 128), 1) // 16 == k, moved_in, tile)
    ftile[...] = tile
    put_gains(tile, lax.div(zc, 8))

    def put_rows(plane, slot):
        pad[plane, :, 7, :] = hrow[slot]
        pad[plane, :, 40, :] = hrow[slot + 1]

    def conv(plane, first, chans=(0, C)):
        def channels(step, carry):
            for k in range(4):
                c = step * 4 + k
                sums = [None, None, None]
                for b in range(3):
                    window = pad[plane, c, 7 + b : 39 + b, :]
                    for e in range(3):
                        term = depth_w[c, plane * 9 + b * 3 + e] * window
                        sums[e] = term if sums[e] is None else sums[e] + term
                value = sums[1] + pltpu.roll(sums[0], 1, 1) + pltpu.roll(sums[2], NX - 1, 1)
                depth[c] = value if first else depth[c] + value
            return carry

        lax.fori_loop(chans[0] // 4, chans[1] // 4, channels, 0)

    pl.semaphore_wait(tokens.at[0], 2)
    send_tokens(1, 4)

    pltpu.make_async_copy(recv1, recv1, r1).wait()
    for k in range(W):
        tmp[k * 8 : (k + 1) * 8, :] = (recv1[k] + recv1[8 + k]) + (recv1[16 + k] + recv1[24 + k])
    lower = iota((8, 128), 1) < 64
    for k in range(8):
        one = tmp[pl.ds(k // 2, 8, stride=8), :]
        two = tmp[pl.ds(k // 2 + 4, 8, stride=8), :]
        if k % 2 == 0:
            send2[k] = jnp.where(lower, one, pltpu.roll(two, 64, 1))
        else:
            send2[k] = jnp.where(lower, pltpu.roll(one, 64, 1), two)

    far_first = (8, 7, 9, 6, 10, 5, 11, 4, 12, 3, 13, 2, 14, 1, 15)
    pl.semaphore_wait(tokens.at[1], 2)

    def copy2(i):
        return pltpu.make_async_remote_copy(
            send2.at[lax.rem(zs[i], 8)], recv2.at[zc], s2, r2,
            device_id=(ring_peer(i), gy), device_id_type=MESH,
        )

    copyf = pltpu.make_async_remote_copy(
        ftile, ftile2, sf, rf, device_id=(ring_peer(8), gy), device_id_type=MESH
    )
    copyf.start()
    for i in far_first:
        copy2(i).start()
    own2 = pltpu.make_async_copy(send2.at[lax.rem(zc, 8)], recv2.at[zc], r2)
    own2.start()

    cross(1)
    loads[3].wait()

    def wait_rows(index, count):
        part = hrow.at[0:count]
        pltpu.make_async_copy(part, part, rh.at[index]).wait()

    wait_rows(0, 2)
    put_rows(1, 2)
    conv(1, True)

    wait_rows(1, 4)
    near = jnp.where(core == 0, 2, 0)
    far = 2 - near
    pltpu.make_async_copy(field3, pad.at[near, :, 8:40, :], rz.at[near]).wait()
    put_rows(near, near * 2)
    conv(near, False)

    grow = (iota((256, C), 0) // 8 == iota((256, C), 1)).astype(F32).astype(BF16)
    grow_t = (iota((C, 256), 1) // 8 == iota((C, 256), 0)).astype(F32).astype(BF16)
    diagonal = iota((256, 256), 0) % 8 == iota((256, 256), 1) % 8
    mixers = []
    for part in split(point_w[...]):
        tall = dot(grow, part).astype(BF16)
        mixers.append(jnp.where(diagonal, dot(tall, grow_t), 0.0).astype(BF16))
    copyf.wait_recv()
    put_gains(ftile2[...], 1 - lax.div(zc, 8))
    gain_re = jnp.transpose(gains[0])[0:16, :]
    gain_im = jnp.transpose(gains[1])[0:16, :]
    pltpu.make_async_copy(recv2, recv2, r2).wait()
    a_high, a_low = split(recv2[...].reshape(NZ, 128))
    both = dot(tz[...], jnp.concatenate([a_high, a_low], axis=0))
    modes = both[0:16] + both[32:48] + swapped(both[16:32] + both[48:64])
    filtered = modes * gain_re - swapped(modes) * gain_im
    stacked = jnp.concatenate([filtered, -swapped(filtered)], axis=0)
    f_high, f_low = split(stacked)
    both = dot(tzi[...], jnp.concatenate([f_high, f_low], axis=0))
    send4[...] = (both[0:128] + both[128:256]).reshape(ZC, 8, 128)

    def copy4(i):
        return pltpu.make_async_remote_copy(
            send4.at[zs[i]], recv4.at[pl.ds(pl.multiple_of(lax.rem(zc, 8) * 8, 8), 8), :], s4, r4,
            device_id=(ring_peer(i), gy), device_id_type=MESH,
        )

    nearer = (ZC - 4, 3, ZC - 3, 2, ZC - 2, 1, ZC - 1)
    for i in nearer:
        copy4(i).start()
    own4 = pltpu.make_async_copy(
        send4.at[zc], recv4.at[pl.ds(pl.multiple_of(lax.rem(zc, 8) * 8, 8), 8), :], r4
    )
    own4.start()

    cross(2)
    def wait_plane(plane, chans, landed):
        part = pad.at[plane, chans[0] : chans[1], 8:40, :]
        pltpu.make_async_copy(part, part, rz.at[landed]).wait()

    wait_plane(far, parts[0], far)
    put_rows(far, far * 2)
    conv(far, False, parts[0])
    pltpu.make_async_copy(recv4, recv4, r4).wait()
    for k in range(W):
        even = recv4[pl.ds(k, 4, stride=16), :]
        odd = recv4[pl.ds(8 + k, 4, stride=16), :]
        tmp3[k, 0:4] = jnp.where(lower[0:4], even, pltpu.roll(odd, 64, 1))
        tmp3[k, 4:8] = jnp.where(lower[0:4], pltpu.roll(even, 64, 1), odd)

    def copy3(i):
        target, t = plane_peer(i)
        return pltpu.make_async_remote_copy(
            tmp3.at[ws[i[1]]], recv3.at[w * 4 + gy], s3, r3,
            device_id=target, device_id_type=MESH,
        )

    for peer in plane_peers:
        copy3(peer).start()
    own3 = pltpu.make_async_copy(
        tmp3.at[w], recv3.at[w * 4 + gy], r3
    )
    own3.start()

    wait_plane(far, (CUTS[0], C), 1)
    conv(far, False, (CUTS[0], C))

    for k in range(YL // 8):
        d_high, d_low = split(depth[:, k * 8 : (k + 1) * 8, :].reshape(256, NX))
        value = dot(mixers[0], d_high) + dot(mixers[0], d_low) + dot(mixers[1], d_high)
        pacc[:, k * 8 : (k + 1) * 8, :] = value.reshape(C, 8, NX)
    put = pltpu.make_async_copy(pacc, point_out, so)
    put.start()

    for peer in plane_peers:
        copy1(peer).wait_send()
        copy3(peer).wait_send()
    for i in far_first:
        copy2(i).wait_send()
    for i in nearer:
        copy4(i).wait_send()
    copyf.wait_send()
    for dz in (-1, 0, 1):
        for side in range(2):
            copy_row(dz, side).wait_send()
    copy_plane(to_near, (0, C)).wait_send()
    for part in parts:
        copy_plane(-to_near, part).wait_send()

    pltpu.make_async_copy(recv3, recv3, r3).wait()
    put.wait()


def last_kernel(
    tiles_in, point_in, tyi_in, txi_in, bias_in, done_out,
    tiles, point, tyi, txi, bias, wide_yi, ld_sem, pt_sem, so,
):
    gy = lax.axis_index("gy")
    loads = [
        pltpu.make_async_copy(src, dst, ld_sem.at[k])
        for k, (src, dst) in enumerate(
            [(tyi_in.at[gy], tyi), (tiles_in, tiles), (bias_in, bias), (txi_in, txi)]
        )
    ]
    quarters = [pl.ds(k * 8, 8) for k in range(4)]
    points = [
        pltpu.make_async_copy(point_in.at[q], point.at[q], pt_sem.at[k]) for k, q in enumerate(quarters)
    ]
    for load in loads + points:
        load.start()
    block = iota((8, 128), 1) // 16 % 4
    same_i = iota((8, YL, 128), 0) == iota((8, YL, 128), 2) % 8
    loads[0].wait()
    for which in range(4):
        base = tyi[which]
        filled = jnp.where(same_i, jnp.broadcast_to(base[None], (8, YL, 128)), 0.0)
        row = which // 2 * 256
        filled = filled.reshape(256, 128).astype(BF16)
        for k in (0, 1) if which % 2 == 0 else (2,):
            wide_yi[row : row + 256, k * 128 : (k + 1) * 128] = filled
    loads[1].wait()
    loads[2].wait()
    columns = []
    for p in range(2):
        rows = []
        for ky in range(MY):
            q, k4 = ky // 4, ky % 4
            value = moved(tiles[p * 16 + q], 0 - k4)
            for kxb in range(1, 4):
                value = jnp.where(block == kxb, moved(tiles[(p * 4 + kxb) * 4 + q], kxb - k4), value)
            rows.append(value)
        columns.append(jnp.concatenate(rows, axis=0))
    r_high, r_low = split(jnp.concatenate(columns, axis=1))
    value = dot(wide_yi[...], jnp.concatenate([r_high, r_low, r_high], axis=0))
    y_halves = split(value)
    loads[3].wait()
    puts = []
    for step in range(4):
        points[step].wait()

        def gathered(half):
            real = half[step * 64 : (step + 1) * 64]
            imag = half[256 + step * 64 : 256 + (step + 1) * 64]
            return jnp.concatenate(
                [
                    jnp.concatenate(
                        [real[:, p * 128 : (p + 1) * 128], imag[:, p * 128 : (p + 1) * 128]], axis=1
                    )
                    for p in range(2)
                ],
                axis=0,
            )

        high, low = gathered(y_halves[0]), gathered(y_halves[1])
        spectral = dot(jnp.concatenate([high, low, high], axis=1), txi[...])
        for p in range(2):
            for sl in range(2):
                for ml in range(2):
                    ch = step * 8 + 4 * sl + 2 * ml + p
                    row = p * 64 + sl * 32
                    value = point[ch] + spectral[row : row + 32, ml * 256 : (ml + 1) * 256] + bias[0, ch]
                    point[ch] = 0.5 * value * (1.0 + lax.erf(value * (0.5**0.5)))
        chans = pl.ds(step * 8, 8)
        put = pltpu.make_async_copy(point.at[chans], done_out.at[chans], so.at[step])
        put.start()
        puts.append(put)
    for put in puts:
        put.wait()


def body(field, spectral_filter, depth_weight, point_weight, bias_vector):
    field3 = field.reshape(C, YL, NX)
    filt = spectral_filter.transpose(0, 2, 3, 1).reshape(64, 16)
    const = {name: jnp.asarray(value) for name, value in TABLES.items()}
    hbm = pl.BlockSpec(memory_space=pltpu.HBM)
    tiles, point = pl.pallas_call(
        wide_kernel,
        name="wide",
        out_shape=(
            jax.ShapeDtypeStruct((32, 8, 128), F32),
            jax.ShapeDtypeStruct((C, YL, NX), F32),
        ),
        in_specs=[hbm] * 8,
        out_specs=(hbm, hbm),
        scratch_shapes=[
            VMEM((C, YL, NX), F32),
            VMEM((64, 16), F32),
            VMEM((64, 128), F32),
            VMEM((8, 128), F32),
            VMEM((8, 128), F32),
            pltpu.SMEM((C, 27), F32),
            VMEM((C, C), F32),
            VMEM((2, 768, 256), BF16),
            VMEM((4, MY, 256), F32),
            VMEM((64, 256), BF16),
            VMEM((256, 64), BF16),
            VMEM((3, C, 48, NX), F32),
            VMEM((2, C, NX), F32),
            VMEM((6, C, NX), F32),
            VMEM((512, 256), BF16),
            VMEM((512, 256), BF16),
            VMEM((128, 256), F32),
            VMEM((32, 8, 128), F32),
            VMEM((32, 8, 128), F32),
            VMEM((64, 128), F32),
            VMEM((8, 8, 128), F32),
            VMEM((ZC, 8, 128), F32),
            VMEM((2, 128, 128), F32),
            VMEM((ZC, 8, 128), F32),
            VMEM((64, 128), F32),
            VMEM((W, 8, 128), F32),
            VMEM((C, YL, NX), F32),
            VMEM((C, YL, NX), F32),
            DMA((9,)), DMA, DMA, DMA, DMA((2,)), DMA, DMA((3,)), DMA, DMA, DMA, DMA, DMA, DMA, DMA, DMA, DMA,
            pltpu.SemaphoreType.REGULAR((2,)),
        ],
        compiler_params=pltpu.CompilerParams(
            collective_id=0, has_side_effects=True, vmem_limit_bytes=VMEM_ALL
        ),
    )(
        field3, filt, depth_weight, point_weight,
        const["tx"], const["ty"], const["tz"], const["tzi"],
    )
    value = pl.pallas_call(
        last_kernel,
        name="last",
        out_shape=jax.ShapeDtypeStruct((C, YL, NX), F32),
        in_specs=[hbm] * 5,
        out_specs=hbm,
        scratch_shapes=[
            VMEM((32, 8, 128), F32),
            VMEM((C, YL, NX), F32),
            VMEM((4, YL, 128), F32),
            VMEM((768, 512), BF16),
            pltpu.SMEM((1, C), F32),
            VMEM((512, 384), BF16),
            DMA((4,)), DMA((4,)), DMA((4,)),
        ],
        compiler_params=pltpu.CompilerParams(vmem_limit_bytes=VMEM_ALL),
    )(tiles, point, const["tyi"], const["txi"], bias_vector.reshape(1, C))
    return value.reshape(C, 1, YL, NX)


def solution(mesh):
    in_specs = (P(None, "gz", "gy", None), P(None, None, "gy", "gz"), P(), P(), P())
    out_specs = P(None, "gz", "gy", None)
    return jax.shard_map(body, mesh=mesh, in_specs=in_specs, out_specs=out_specs, check_vma=False)
```

```python
import functools

import jax
import jax.numpy as jnp
import ml_dtypes
import numpy as np
from jax import lax
from jax.experimental import pallas as pl
from jax.experimental.pallas import tpu as pltpu
from jax.sharding import PartitionSpec as P

C = 32
NX = 256
NY = 128
NZ = 128
MX = 32
MY = 16
MZ = 16
GY = 4
ZC = 16
W = 8
YL = NY // GY
VMEM_ALL = 67043328
CUTS = (8, 24)
MESH = pl.DeviceIdType.MESH
F32 = jnp.float32
BF16 = jnp.bfloat16
VMEM = pltpu.VMEM
DMA = pltpu.SemaphoreType.DMA


def halves(table):
    high = table.astype(ml_dtypes.bfloat16)
    low = (table - high.astype(np.float64)).astype(ml_dtypes.bfloat16)
    return high, low


def kept(count, total):
    series = np.arange(count)
    return np.where(series < count // 2, series, total - count + series)


def make_tables():
    tables = {}
    angle = 2 * np.pi * (np.arange(NX)[:, None] * np.arange(MX)[None, :] % NX) / NX
    cos = np.cos(angle).reshape(NX, 4, 8)
    sin = np.sin(angle).reshape(NX, 4, 8)
    plain = np.stack([cos, -sin], axis=2).reshape(NX, 64)
    swapped = np.stack([-sin, -cos], axis=2).reshape(NX, 64)
    zero = np.zeros_like(plain)
    tx = np.stack(
        [
            np.concatenate([plain, zero, swapped, zero], axis=1),
            np.concatenate([zero, plain, zero, swapped], axis=1),
        ]
    )
    high, low = halves(tx)
    tables["tx"] = np.concatenate([high, high, low], axis=1)
    places = np.arange(NY)
    angle = 2 * np.pi * (kept(MY, NY)[:, None] * places[None, :] % NY) / NY
    parts = []
    for value in (np.cos(angle), np.sin(angle)):
        parts.extend(part.astype(np.float32) for part in halves(value))
    stack = np.stack(parts)
    mine = stack.reshape(4, MY, GY, YL).transpose(2, 0, 1, 3)
    tables["ty"] = np.tile(mine, (1, 1, 1, 8))
    tables["tyi"] = np.repeat(mine.transpose(0, 1, 3, 2), 8, axis=3)
    angle = 2 * np.pi * (kept(MZ, NZ)[:, None] * np.arange(NZ)[None, :] % NZ) / NZ
    high, low = halves(np.concatenate([np.cos(angle), np.sin(angle)], axis=0))
    both = np.concatenate([high, low], axis=0)
    tables["tz"] = np.concatenate([both, both], axis=1)
    scale = (NX * NY * NZ) ** -0.5 * (2.0 * MX * MY * MZ) ** -0.5
    both = np.concatenate([np.cos(angle), np.sin(angle)], axis=0).T * scale
    both = np.concatenate(halves(both), axis=0)
    tables["tzi"] = np.concatenate([both, both], axis=1)
    weight = np.where(np.arange(MX) == 0, 1.0, 2.0)[:, None]
    angle = 2 * np.pi * (np.arange(MX)[:, None] * np.arange(NX)[None, :] % NX) / NX
    cos = (weight * np.cos(angle)).reshape(4, 8, NX)
    sin = (weight * np.sin(angle)).reshape(4, 8, NX)
    from_c = np.stack([cos, -sin], axis=1).reshape(64, NX)
    from_s = np.stack([-sin, -cos], axis=1).reshape(64, NX)
    zero = np.zeros_like(from_c)
    txi = np.block([[from_c, zero], [zero, from_c], [from_s, zero], [zero, from_s]])
    high, low = halves(txi)
    tables["txi"] = np.concatenate([high, high, low], axis=0)
    return tables


TABLES = make_tables()


def split(value):
    high = value.astype(BF16)
    return high, (value - high.astype(F32)).astype(BF16)


def dot(left, right):
    return jnp.dot(left, right, preferred_element_type=F32)


def iota(shape, dim):
    return lax.broadcasted_iota(jnp.int32, shape, dim)


def swapped(value):
    pieces = []
    for k in range(value.shape[1] // 128):
        piece = value[:, k * 128 : (k + 1) * 128]
        real_lane = iota(piece.shape, 1) % 16 < 8
        pieces.append(jnp.where(real_lane, pltpu.roll(piece, 120, 1), -pltpu.roll(piece, 8, 1)))
    return jnp.concatenate(pieces, axis=1)


def moved(value, blocks):
    return value if blocks % 8 == 0 else pltpu.roll(value, blocks % 8 * 16, 1)


def wide_kernel(
    field3, filt_in, depth_in, point_in, tx_in, ty_in, tz_in, tzi_in,
    recv3, point_out,
    fv, filt, fwide, ftile, ftile2, depth_w, point_w, tx, ty, tz, tzi,
    pad, edge, hrow, xh, xl, yout, send1, recv1, tmp, send2, recv2, gains,
    send4, recv4, tmp3, depth, pacc,
    ld_sem, s1, r1, sh, rh, sz, rz, s2, r2, s4, r4, s3, r3, so, sf, rf, tokens,
):
    gz = lax.axis_index("gz")
    gy = lax.axis_index("gy")
    zc = lax.div(gz, W)
    w = lax.rem(gz, W)
    core = lax.rem(gz, 2)
    me = gy * W + w

    ws = [w] + [lax.rem(w + k, W) for k in range(1, W)]
    gys = [gy] + [lax.rem(gy + k, GY) for k in range(1, GY)]
    zs = [zc] + [lax.rem(zc + k, ZC) for k in range(1, ZC)]
    first_gz = gz - w
    plane_peers = [(dx, dw) for dx in (2, 1, 3, 0) for dw in (4, 3, 5, 2, 6, 1, 7, 0) if dx or dw]

    def plane_peer(peer):
        dx, dw = peer
        return (first_gz + ws[dw], gys[dx]), gys[dx] * W + ws[dw]

    def ring_peer(i):
        return zs[i] * W + w

    def halo_peer(dz, dy):
        return (lax.rem(gz + (NZ + dz), NZ), gys[dy % GY])

    barrier = pltpu.get_barrier_semaphore()

    def signal(target):
        pl.semaphore_signal(barrier, inc=1, device_id=target, device_id_type=MESH)

    loads = [
        pltpu.make_async_copy(src, dst, ld_sem.at[k])
        for k, (src, dst) in enumerate(
            [
                (field3, fv),
                (tx_in, tx),
                (ty_in.at[gy], ty),
                (field3, pad.at[1, :, 8:40, :]),
                (filt_in, filt),
                (depth_in, depth_w),
                (point_in, point_w),
                (tz_in, tz),
                (tzi_in, tzi),
            ]
        )
    ]
    for load in loads[:3]:
        load.start()
    for i in (2, ZC - 2, 1, ZC - 1):
        signal((ring_peer(i), gy))
    for dz in (-1, 1):
        for dy in (-1, 0, 1):
            signal(halo_peer(dz, dy))
    for peer in plane_peers:
        signal(plane_peer(peer)[0])
    loads[0].wait()
    for load in loads[3:]:
        load.start()
    for side, row in ((0, YL - 1), (1, 0)):
        edge[side] = fv[:, row, :]

    loads[1].wait()
    loads[2].wait()
    for p in range(2):
        total = None
        for ml in range(2):
            g = 2 * ml + p
            rows = jnp.concatenate(
                [fv[4 * s + g] for s in range(8)], axis=0
            )
            high, low = split(rows)
            value = dot(jnp.concatenate([high, low, high], axis=1), tx[ml])
            total = value if total is None else total + value
        high, low = split(total)
        for part in range(2):
            xh[part * 256 : (part + 1) * 256, p * 128 : (p + 1) * 128] = high[:, part * 128 : (part + 1) * 128]
            xl[part * 256 : (part + 1) * 256, p * 128 : (p + 1) * 128] = low[:, part * 128 : (part + 1) * 128]
    same = iota((MY, 8, 256), 1) == iota((MY, 8, 256), 2) // YL

    def spread(which):
        base = ty[which]
        wide = jnp.where(same, jnp.broadcast_to(base[:, None, :], (MY, 8, 256)), 0.0)
        return wide.reshape(128, 256).astype(BF16)

    y_high = jnp.concatenate([spread(0), spread(2)], axis=1)
    y_low = jnp.concatenate([spread(1), spread(3)], axis=1)
    y_both = jnp.concatenate([y_high, y_low], axis=0)
    result = dot(y_both, xh[...]) + dot(y_both, xl[...])
    yout[...] = result[0:128] + result[128:256]
    block = iota((8, 128), 1) // 16 % 4
    for p in range(2):
        for q in range(4):
            quad = [
                yout[(q * 4 + ky) * 8 : (q * 4 + ky + 1) * 8, p * 128 : (p + 1) * 128]
                for ky in range(4)
            ]
            for kxb in range(4):
                out = moved(quad[0], 0 - kxb)
                for ky in range(1, 4):
                    out = jnp.where(block == ky, moved(quad[ky], ky - kxb), out)
                send1[q * 8 + p * 4 + kxb] = out

    pl.semaphore_wait(barrier, 4 + 6 + 31)

    def copy1(i):
        target, t = plane_peer(i)
        return pltpu.make_async_remote_copy(
            send1.at[t], recv1.at[me], s1, r1, device_id=target, device_id_type=MESH
        )

    for peer in plane_peers:
        copy1(peer).start()
    own1 = pltpu.make_async_copy(send1.at[me], recv1.at[me], r1)
    own1.start()

    def copy_row(dz, side):
        dy = 1 if side == 0 else -1
        slot = (1 - dz) * 2 + side
        return pltpu.make_async_remote_copy(
            edge.at[side], hrow.at[slot], sh, rh.at[0 if dz == 0 else 1],
            device_id=halo_peer(dz, dy), device_id_type=MESH,
        )

    to_near = 1 - 2 * core

    def copy_plane(dz, chans):
        landed = {0: 1 - dz, CUTS[0]: 3, CUTS[1]: 1}[chans[0]]
        return pltpu.make_async_remote_copy(
            field3.at[chans[0] : chans[1]], pad.at[1 - dz, chans[0] : chans[1], 8:40, :], sz, rz.at[landed],
            device_id=halo_peer(dz, 0), device_id_type=MESH,
        )

    parts = ((0, CUTS[0]), (CUTS[0], CUTS[1]), (CUTS[1], C))
    crossing = jnp.logical_or(w == 0, w == W - 1)

    def cross(part):
        @pl.when(crossing)
        def _():
            copy_plane(-to_near, parts[part]).start()

    def send_tokens(which, reach):
        for i in (reach, ZC - reach):
            pl.semaphore_signal(
                tokens.at[which], inc=1, device_id=(ring_peer(i), gy), device_id_type=MESH
            )

    send_tokens(0, 2)
    for side in range(2):
        copy_row(0, side).start()
    copy_plane(to_near, (0, C)).start()
    cross(0)

    @pl.when(jnp.logical_not(crossing))
    def _():
        for part in parts:
            copy_plane(-to_near, part).start()

    for dz in (-1, 1):
        for side in range(2):
            copy_row(dz, side).start()
    def put_gains(tile, pair):
        for part in range(2):
            for ky in range(4):
                k = part * 4 + ky
                value = tile if k == 0 else pltpu.roll(tile, 128 - k * 16, 1)
                for r in range(2):
                    row = pl.multiple_of(pair * 64 + ky * 16 + r * 8, 8)
                    gains[part, pl.ds(row, 8), :] = value

    for load in loads[4:]:
        load.wait()
    fwide[:, 0:16] = filt[...]
    tile = fwide[0:8, :]
    for k in range(1, 8):
        moved_in = pltpu.roll(fwide[k * 8 : k * 8 + 8, :], k * 16, 1)
        tile = jnp.where(iota((8, 128), 1) // 16 == k, moved_in, tile)
    ftile[...] = tile
    put_gains(tile, lax.div(zc, 8))

    def put_rows(plane, slot):
        pad[plane, :, 7, :] = hrow[slot]
        pad[plane, :, 40, :] = hrow[slot + 1]

    def conv(plane, first, chans=(0, C)):
        def channels(step, carry):
            for k in range(4):
                c = step * 4 + k
                sums = [None, None, None]
                for b in range(3):
                    window = pad[plane, c, 7 + b : 39 + b, :]
                    for e in range(3):
                        term = depth_w[c, plane * 9 + b * 3 + e] * window
                        sums[e] = term if sums[e] is None else sums[e] + term
                value = sums[1] + pltpu.roll(sums[0], 1, 1) + pltpu.roll(sums[2], NX - 1, 1)
                depth[c] = value if first else depth[c] + value
            return carry

        lax.fori_loop(chans[0] // 4, chans[1] // 4, channels, 0)

    pl.semaphore_wait(tokens.at[0], 2)
    send_tokens(1, 4)

    pltpu.make_async_copy(recv1, recv1, r1).wait()
    for k in range(W):
        tmp[k * 8 : (k + 1) * 8, :] = (recv1[k] + recv1[8 + k]) + (recv1[16 + k] + recv1[24 + k])
    lower = iota((8, 128), 1) < 64
    for k in range(8):
        one = tmp[pl.ds(k // 2, 8, stride=8), :]
        two = tmp[pl.ds(k // 2 + 4, 8, stride=8), :]
        if k % 2 == 0:
            send2[k] = jnp.where(lower, one, pltpu.roll(two, 64, 1))
        else:
            send2[k] = jnp.where(lower, pltpu.roll(one, 64, 1), two)

    far_first = (8, 7, 9, 6, 10, 5, 11, 4, 12, 3, 13, 2, 14, 1, 15)
    pl.semaphore_wait(tokens.at[1], 2)

    def copy2(i):
        return pltpu.make_async_remote_copy(
            send2.at[lax.rem(zs[i], 8)], recv2.at[zc], s2, r2,
            device_id=(ring_peer(i), gy), device_id_type=MESH,
        )

    copyf = pltpu.make_async_remote_copy(
        ftile, ftile2, sf, rf, device_id=(ring_peer(8), gy), device_id_type=MESH
    )
    copyf.start()
    for i in far_first:
        copy2(i).start()
    own2 = pltpu.make_async_copy(send2.at[lax.rem(zc, 8)], recv2.at[zc], r2)
    own2.start()

    cross(1)
    loads[3].wait()

    def wait_rows(index, count):
        part = hrow.at[0:count]
        pltpu.make_async_copy(part, part, rh.at[index]).wait()

    wait_rows(0, 2)
    put_rows(1, 2)
    conv(1, True)

    wait_rows(1, 4)
    near = jnp.where(core == 0, 2, 0)
    far = 2 - near
    pltpu.make_async_copy(field3, pad.at[near, :, 8:40, :], rz.at[near]).wait()
    put_rows(near, near * 2)
    conv(near, False)

    grow = (iota((256, C), 0) // 8 == iota((256, C), 1)).astype(F32).astype(BF16)
    grow_t = (iota((C, 256), 1) // 8 == iota((C, 256), 0)).astype(F32).astype(BF16)
    diagonal = iota((256, 256), 0) % 8 == iota((256, 256), 1) % 8
    mixers = []
    for part in split(point_w[...]):
        tall = dot(grow, part).astype(BF16)
        mixers.append(jnp.where(diagonal, dot(tall, grow_t), 0.0).astype(BF16))
    copyf.wait_recv()
    put_gains(ftile2[...], 1 - lax.div(zc, 8))
    gain_re = jnp.transpose(gains[0])[0:16, :]
    gain_im = jnp.transpose(gains[1])[0:16, :]
    pltpu.make_async_copy(recv2, recv2, r2).wait()
    a_high, a_low = split(recv2[...].reshape(NZ, 128))
    both = dot(tz[...], jnp.concatenate([a_high, a_low], axis=0))
    modes = both[0:16] + both[32:48] + swapped(both[16:32] + both[48:64])
    filtered = modes * gain_re - swapped(modes) * gain_im
    stacked = jnp.concatenate([filtered, -swapped(filtered)], axis=0)
    f_high, f_low = split(stacked)
    both = dot(tzi[...], jnp.concatenate([f_high, f_low], axis=0))
    send4[...] = (both[0:128] + both[128:256]).reshape(ZC, 8, 128)

    def copy4(i):
        return pltpu.make_async_remote_copy(
            send4.at[zs[i]], recv4.at[pl.ds(pl.multiple_of(lax.rem(zc, 8) * 8, 8), 8), :], s4, r4,
            device_id=(ring_peer(i), gy), device_id_type=MESH,
        )

    nearer = (ZC - 4, 3, ZC - 3, 2, ZC - 2, 1, ZC - 1)
    for i in nearer:
        copy4(i).start()
    own4 = pltpu.make_async_copy(
        send4.at[zc], recv4.at[pl.ds(pl.multiple_of(lax.rem(zc, 8) * 8, 8), 8), :], r4
    )
    own4.start()

    cross(2)
    def wait_plane(plane, chans, landed):
        part = pad.at[plane, chans[0] : chans[1], 8:40, :]
        pltpu.make_async_copy(part, part, rz.at[landed]).wait()

    wait_plane(far, parts[0], far)
    put_rows(far, far * 2)
    conv(far, False, parts[0])
    pltpu.make_async_copy(recv4, recv4, r4).wait()
    for k in range(W):
        even = recv4[pl.ds(k, 4, stride=16), :]
        odd = recv4[pl.ds(8 + k, 4, stride=16), :]
        tmp3[k, 0:4] = jnp.where(lower[0:4], even, pltpu.roll(odd, 64, 1))
        tmp3[k, 4:8] = jnp.where(lower[0:4], pltpu.roll(even, 64, 1), odd)

    def copy3(i):
        target, t = plane_peer(i)
        return pltpu.make_async_remote_copy(
            tmp3.at[ws[i[1]]], recv3.at[w * 4 + gy], s3, r3,
            device_id=target, device_id_type=MESH,
        )

    for peer in plane_peers:
        copy3(peer).start()
    own3 = pltpu.make_async_copy(
        tmp3.at[w], recv3.at[w * 4 + gy], r3
    )
    own3.start()

    wait_plane(far, parts[1], 3)
    conv(far, False, parts[1])
    wait_plane(far, parts[2], 1)
    conv(far, False, parts[2])

    for k in range(YL // 8):
        d_high, d_low = split(depth[:, k * 8 : (k + 1) * 8, :].reshape(256, NX))
        value = dot(mixers[0], d_high) + dot(mixers[0], d_low) + dot(mixers[1], d_high)
        pacc[:, k * 8 : (k + 1) * 8, :] = value.reshape(C, 8, NX)
    put = pltpu.make_async_copy(pacc, point_out, so)
    put.start()

    for peer in plane_peers:
        copy1(peer).wait_send()
        copy3(peer).wait_send()
    for i in far_first:
        copy2(i).wait_send()
    for i in nearer:
        copy4(i).wait_send()
    copyf.wait_send()
    for dz in (-1, 0, 1):
        for side in range(2):
            copy_row(dz, side).wait_send()
    copy_plane(to_near, (0, C)).wait_send()
    for part in parts:
        copy_plane(-to_near, part).wait_send()

    pltpu.make_async_copy(recv3, recv3, r3).wait()
    put.wait()


def last_kernel(
    tiles_in, point_in, tyi_in, txi_in, bias_in, done_out,
    tiles, point, tyi, txi, bias, wide_yi, ld_sem, pt_sem, so,
):
    gy = lax.axis_index("gy")
    loads = [
        pltpu.make_async_copy(src, dst, ld_sem.at[k])
        for k, (src, dst) in enumerate(
            [(tyi_in.at[gy], tyi), (tiles_in, tiles), (bias_in, bias), (txi_in, txi)]
        )
    ]
    quarters = [pl.ds(k * 8, 8) for k in range(4)]
    points = [
        pltpu.make_async_copy(point_in.at[q], point.at[q], pt_sem.at[k]) for k, q in enumerate(quarters)
    ]
    for load in loads + points:
        load.start()
    block = iota((8, 128), 1) // 16 % 4
    same_i = iota((8, YL, 128), 0) == iota((8, YL, 128), 2) % 8
    loads[0].wait()
    for which in range(4):
        base = tyi[which]
        filled = jnp.where(same_i, jnp.broadcast_to(base[None], (8, YL, 128)), 0.0)
        row = which // 2 * 256
        filled = filled.reshape(256, 128).astype(BF16)
        for k in (0, 1) if which % 2 == 0 else (2,):
            wide_yi[row : row + 256, k * 128 : (k + 1) * 128] = filled
    loads[1].wait()
    loads[2].wait()
    columns = []
    for p in range(2):
        rows = []
        for ky in range(MY):
            q, k4 = ky // 4, ky % 4
            value = moved(tiles[p * 16 + q], 0 - k4)
            for kxb in range(1, 4):
                value = jnp.where(block == kxb, moved(tiles[(p * 4 + kxb) * 4 + q], kxb - k4), value)
            rows.append(value)
        columns.append(jnp.concatenate(rows, axis=0))
    r_high, r_low = split(jnp.concatenate(columns, axis=1))
    value = dot(wide_yi[...], jnp.concatenate([r_high, r_low, r_high], axis=0))
    y_halves = split(value)
    loads[3].wait()
    puts = []
    for step in range(4):
        points[step].wait()

        def gathered(half):
            real = half[step * 64 : (step + 1) * 64]
            imag = half[256 + step * 64 : 256 + (step + 1) * 64]
            return jnp.concatenate(
                [
                    jnp.concatenate(
                        [real[:, p * 128 : (p + 1) * 128], imag[:, p * 128 : (p + 1) * 128]], axis=1
                    )
                    for p in range(2)
                ],
                axis=0,
            )

        high, low = gathered(y_halves[0]), gathered(y_halves[1])
        spectral = dot(jnp.concatenate([high, low, high], axis=1), txi[...])
        for p in range(2):
            for sl in range(2):
                for ml in range(2):
                    ch = step * 8 + 4 * sl + 2 * ml + p
                    row = p * 64 + sl * 32
                    value = point[ch] + spectral[row : row + 32, ml * 256 : (ml + 1) * 256] + bias[0, ch]
                    point[ch] = 0.5 * value * (1.0 + lax.erf(value * (0.5**0.5)))
        chans = pl.ds(step * 8, 8)
        put = pltpu.make_async_copy(point.at[chans], done_out.at[chans], so.at[step])
        put.start()
        puts.append(put)
    for put in puts:
        put.wait()


def body(field, spectral_filter, depth_weight, point_weight, bias_vector):
    field3 = field.reshape(C, YL, NX)
    filt = spectral_filter.transpose(0, 2, 3, 1).reshape(64, 16)
    const = {name: jnp.asarray(value) for name, value in TABLES.items()}
    hbm = pl.BlockSpec(memory_space=pltpu.HBM)
    tiles, point = pl.pallas_call(
        wide_kernel,
        name="wide",
        out_shape=(
            jax.ShapeDtypeStruct((32, 8, 128), F32),
            jax.ShapeDtypeStruct((C, YL, NX), F32),
        ),
        in_specs=[hbm] * 8,
        out_specs=(hbm, hbm),
        scratch_shapes=[
            VMEM((C, YL, NX), F32),
            VMEM((64, 16), F32),
            VMEM((64, 128), F32),
            VMEM((8, 128), F32),
            VMEM((8, 128), F32),
            pltpu.SMEM((C, 27), F32),
            VMEM((C, C), F32),
            VMEM((2, 768, 256), BF16),
            VMEM((4, MY, 256), F32),
            VMEM((64, 256), BF16),
            VMEM((256, 64), BF16),
            VMEM((3, C, 48, NX), F32),
            VMEM((2, C, NX), F32),
            VMEM((6, C, NX), F32),
            VMEM((512, 256), BF16),
            VMEM((512, 256), BF16),
            VMEM((128, 256), F32),
            VMEM((32, 8, 128), F32),
            VMEM((32, 8, 128), F32),
            VMEM((64, 128), F32),
            VMEM((8, 8, 128), F32),
            VMEM((ZC, 8, 128), F32),
            VMEM((2, 128, 128), F32),
            VMEM((ZC, 8, 128), F32),
            VMEM((64, 128), F32),
            VMEM((W, 8, 128), F32),
            VMEM((C, YL, NX), F32),
            VMEM((C, YL, NX), F32),
            DMA((9,)), DMA, DMA, DMA, DMA((2,)), DMA, DMA((4,)), DMA, DMA, DMA, DMA, DMA, DMA, DMA, DMA, DMA,
            pltpu.SemaphoreType.REGULAR((2,)),
        ],
        compiler_params=pltpu.CompilerParams(
            collective_id=0, has_side_effects=True, vmem_limit_bytes=VMEM_ALL
        ),
    )(
        field3, filt, depth_weight, point_weight,
        const["tx"], const["ty"], const["tz"], const["tzi"],
    )
    value = pl.pallas_call(
        last_kernel,
        name="last",
        out_shape=jax.ShapeDtypeStruct((C, YL, NX), F32),
        in_specs=[hbm] * 5,
        out_specs=hbm,
        scratch_shapes=[
            VMEM((32, 8, 128), F32),
            VMEM((C, YL, NX), F32),
            VMEM((4, YL, 128), F32),
            VMEM((768, 512), BF16),
            pltpu.SMEM((1, C), F32),
            VMEM((512, 384), BF16),
            DMA((4,)), DMA((4,)), DMA((4,)),
        ],
        compiler_params=pltpu.CompilerParams(vmem_limit_bytes=VMEM_ALL),
    )(tiles, point, const["tyi"], const["txi"], bias_vector.reshape(1, C))
    return value.reshape(C, 1, YL, NX)


def solution(mesh):
    in_specs = (P(None, "gz", "gy", None), P(None, None, "gy", "gz"), P(), P(), P())
    out_specs = P(None, "gz", "gy", None)
    return jax.shard_map(body, mesh=mesh, in_specs=in_specs, out_specs=out_specs, check_vma=False)
```

```python
import functools

import jax
import jax.numpy as jnp
import ml_dtypes
import numpy as np
from jax import lax
from jax.experimental import pallas as pl
from jax.experimental.pallas import tpu as pltpu
from jax.sharding import PartitionSpec as P

C = 32
NX = 256
NY = 128
NZ = 128
MX = 32
MY = 16
MZ = 16
GY = 4
ZC = 16
W = 8
YL = NY // GY
VMEM_ALL = 67043328
CUTS = (8, 24)
MESH = pl.DeviceIdType.MESH
F32 = jnp.float32
BF16 = jnp.bfloat16
VMEM = pltpu.VMEM
DMA = pltpu.SemaphoreType.DMA


def halves(table):
    high = table.astype(ml_dtypes.bfloat16)
    low = (table - high.astype(np.float64)).astype(ml_dtypes.bfloat16)
    return high, low


def kept(count, total):
    series = np.arange(count)
    return np.where(series < count // 2, series, total - count + series)


def make_tables():
    tables = {}
    angle = 2 * np.pi * (np.arange(NX)[:, None] * np.arange(MX)[None, :] % NX) / NX
    cos = np.cos(angle).reshape(NX, 4, 8)
    sin = np.sin(angle).reshape(NX, 4, 8)
    plain = np.stack([cos, -sin], axis=2).reshape(NX, 64)
    swapped = np.stack([-sin, -cos], axis=2).reshape(NX, 64)
    zero = np.zeros_like(plain)
    tx = np.stack(
        [
            np.concatenate([plain, zero, swapped, zero], axis=1),
            np.concatenate([zero, plain, zero, swapped], axis=1),
        ]
    )
    high, low = halves(tx)
    tables["tx"] = np.concatenate([high, high, low], axis=1)
    places = np.arange(NY)
    angle = 2 * np.pi * (kept(MY, NY)[:, None] * places[None, :] % NY) / NY
    parts = []
    for value in (np.cos(angle), np.sin(angle)):
        parts.extend(part.astype(np.float32) for part in halves(value))
    stack = np.stack(parts)
    mine = stack.reshape(4, MY, GY, YL).transpose(2, 0, 1, 3)
    tables["ty"] = np.tile(mine, (1, 1, 1, 8))
    tables["tyi"] = np.repeat(mine.transpose(0, 1, 3, 2), 8, axis=3)
    angle = 2 * np.pi * (kept(MZ, NZ)[:, None] * np.arange(NZ)[None, :] % NZ) / NZ
    high, low = halves(np.concatenate([np.cos(angle), np.sin(angle)], axis=0))
    both = np.concatenate([high, low], axis=0)
    tables["tz"] = np.concatenate([both, both], axis=1)
    scale = (NX * NY * NZ) ** -0.5 * (2.0 * MX * MY * MZ) ** -0.5
    both = np.concatenate([np.cos(angle), np.sin(angle)], axis=0).T * scale
    both = np.concatenate(halves(both), axis=0)
    tables["tzi"] = np.concatenate([both, both], axis=1)
    weight = np.where(np.arange(MX) == 0, 1.0, 2.0)[:, None]
    angle = 2 * np.pi * (np.arange(MX)[:, None] * np.arange(NX)[None, :] % NX) / NX
    cos = (weight * np.cos(angle)).reshape(4, 8, NX)
    sin = (weight * np.sin(angle)).reshape(4, 8, NX)
    from_c = np.stack([cos, -sin], axis=1).reshape(64, NX)
    from_s = np.stack([-sin, -cos], axis=1).reshape(64, NX)
    zero = np.zeros_like(from_c)
    txi = np.block([[from_c, zero], [zero, from_c], [from_s, zero], [zero, from_s]])
    high, low = halves(txi)
    tables["txi"] = np.concatenate([high, high, low], axis=0)
    return tables


TABLES = make_tables()


def split(value):
    high = value.astype(BF16)
    return high, (value - high.astype(F32)).astype(BF16)


def dot(left, right):
    return jnp.dot(left, right, preferred_element_type=F32)


def iota(shape, dim):
    return lax.broadcasted_iota(jnp.int32, shape, dim)


def swapped(value):
    pieces = []
    for k in range(value.shape[1] // 128):
        piece = value[:, k * 128 : (k + 1) * 128]
        real_lane = iota(piece.shape, 1) % 16 < 8
        pieces.append(jnp.where(real_lane, pltpu.roll(piece, 120, 1), -pltpu.roll(piece, 8, 1)))
    return jnp.concatenate(pieces, axis=1)


def moved(value, blocks):
    return value if blocks % 8 == 0 else pltpu.roll(value, blocks % 8 * 16, 1)


def wide_kernel(
    field3, filt_in, depth_in, point_in, tx_in, ty_in, tz_in, tzi_in,
    recv3, point_out,
    fv, filt, fwide, ftile, ftile2, depth_w, point_w, tx, ty, tz, tzi,
    pad, edge, hrow, xh, xl, yout, send1, recv1, tmp, send2, recv2, gains,
    send4, recv4, tmp3, depth, pacc,
    ld_sem, s1, r1, sh, rh, sz, rz, s2, r2, s4, r4, s3, r3, so, sf, rf, tokens,
):
    gz = lax.axis_index("gz")
    gy = lax.axis_index("gy")
    zc = lax.div(gz, W)
    w = lax.rem(gz, W)
    core = lax.rem(gz, 2)
    me = gy * W + w

    ws = [w] + [lax.rem(w + k, W) for k in range(1, W)]
    gys = [gy] + [lax.rem(gy + k, GY) for k in range(1, GY)]
    zs = [zc] + [lax.rem(zc + k, ZC) for k in range(1, ZC)]
    first_gz = gz - w
    plane_peers = [(dx, dw) for dx in (2, 1, 3, 0) for dw in (4, 3, 5, 2, 6, 1, 7, 0) if dx or dw]

    def plane_peer(peer):
        dx, dw = peer
        return (first_gz + ws[dw], gys[dx]), gys[dx] * W + ws[dw]

    def ring_peer(i):
        return zs[i] * W + w

    def halo_peer(dz, dy):
        return (lax.rem(gz + (NZ + dz), NZ), gys[dy % GY])

    barrier = pltpu.get_barrier_semaphore()

    def signal(target):
        pl.semaphore_signal(barrier, inc=1, device_id=target, device_id_type=MESH)

    loads = [
        pltpu.make_async_copy(src, dst, ld_sem.at[k])
        for k, (src, dst) in enumerate(
            [
                (field3, fv),
                (tx_in, tx),
                (ty_in.at[gy], ty),
                (field3, pad.at[1, :, 8:40, :]),
                (filt_in, filt),
                (depth_in, depth_w),
                (point_in, point_w),
                (tz_in, tz),
                (tzi_in, tzi),
            ]
        )
    ]
    for load in loads[:3]:
        load.start()
    for peer in plane_peers:
        signal(plane_peer(peer)[0])
    for i in (2, ZC - 2, 1, ZC - 1):
        signal((ring_peer(i), gy))
    for dz in (-1, 1):
        for dy in (-1, 0, 1):
            signal(halo_peer(dz, dy))
    loads[0].wait()
    for load in loads[3:]:
        load.start()
    for side, row in ((0, YL - 1), (1, 0)):
        edge[side] = fv[:, row, :]

    loads[1].wait()
    loads[2].wait()
    for p in range(2):
        total = None
        for ml in range(2):
            g = 2 * ml + p
            rows = jnp.concatenate(
                [fv[4 * s + g] for s in range(8)], axis=0
            )
            high, low = split(rows)
            value = dot(jnp.concatenate([high, low, high], axis=1), tx[ml])
            total = value if total is None else total + value
        high, low = split(total)
        for part in range(2):
            xh[part * 256 : (part + 1) * 256, p * 128 : (p + 1) * 128] = high[:, part * 128 : (part + 1) * 128]
            xl[part * 256 : (part + 1) * 256, p * 128 : (p + 1) * 128] = low[:, part * 128 : (part + 1) * 128]
    same = iota((MY, 8, 256), 1) == iota((MY, 8, 256), 2) // YL

    def spread(which):
        base = ty[which]
        wide = jnp.where(same, jnp.broadcast_to(base[:, None, :], (MY, 8, 256)), 0.0)
        return wide.reshape(128, 256).astype(BF16)

    y_high = jnp.concatenate([spread(0), spread(2)], axis=1)
    y_low = jnp.concatenate([spread(1), spread(3)], axis=1)
    y_both = jnp.concatenate([y_high, y_low], axis=0)
    result = dot(y_both, xh[...]) + dot(y_both, xl[...])
    yout[...] = result[0:128] + result[128:256]
    block = iota((8, 128), 1) // 16 % 4
    for p in range(2):
        for q in range(4):
            quad = [
                yout[(q * 4 + ky) * 8 : (q * 4 + ky + 1) * 8, p * 128 : (p + 1) * 128]
                for ky in range(4)
            ]
            for kxb in range(4):
                out = moved(quad[0], 0 - kxb)
                for ky in range(1, 4):
                    out = jnp.where(block == ky, moved(quad[ky], ky - kxb), out)
                send1[q * 8 + p * 4 + kxb] = out

    pl.semaphore_wait(barrier, 4 + 6 + 31)

    def copy1(i):
        target, t = plane_peer(i)
        return pltpu.make_async_remote_copy(
            send1.at[t], recv1.at[me], s1, r1, device_id=target, device_id_type=MESH
        )

    for peer in plane_peers:
        copy1(peer).start()
    own1 = pltpu.make_async_copy(send1.at[me], recv1.at[me], r1)
    own1.start()

    def copy_row(dz, side):
        dy = 1 if side == 0 else -1
        slot = (1 - dz) * 2 + side
        return pltpu.make_async_remote_copy(
            edge.at[side], hrow.at[slot], sh, rh.at[0 if dz == 0 else 1],
            device_id=halo_peer(dz, dy), device_id_type=MESH,
        )

    to_near = 1 - 2 * core

    def copy_plane(dz, chans):
        landed = {0: 1 - dz, CUTS[0]: 3, CUTS[1]: 1}[chans[0]]
        return pltpu.make_async_remote_copy(
            field3.at[chans[0] : chans[1]], pad.at[1 - dz, chans[0] : chans[1], 8:40, :], sz, rz.at[landed],
            device_id=halo_peer(dz, 0), device_id_type=MESH,
        )

    parts = ((0, CUTS[0]), (CUTS[0], CUTS[1]), (CUTS[1], C))
    crossing = jnp.logical_or(w == 0, w == W - 1)

    def cross(part):
        @pl.when(crossing)
        def _():
            copy_plane(-to_near, parts[part]).start()

    def send_tokens(which, reach):
        for i in (reach, ZC - reach):
            pl.semaphore_signal(
                tokens.at[which], inc=1, device_id=(ring_peer(i), gy), device_id_type=MESH
            )

    send_tokens(0, 2)
    for side in range(2):
        copy_row(0, side).start()
    copy_plane(to_near, (0, C)).start()
    cross(0)

    @pl.when(jnp.logical_not(crossing))
    def _():
        for part in parts:
            copy_plane(-to_near, part).start()

    for dz in (-1, 1):
        for side in range(2):
            copy_row(dz, side).start()
    def put_gains(tile, pair):
        for part in range(2):
            for ky in range(4):
                k = part * 4 + ky
                value = tile if k == 0 else pltpu.roll(tile, 128 - k * 16, 1)
                for r in range(2):
                    row = pl.multiple_of(pair * 64 + ky * 16 + r * 8, 8)
                    gains[part, pl.ds(row, 8), :] = value

    for load in loads[4:]:
        load.wait()
    fwide[:, 0:16] = filt[...]
    tile = fwide[0:8, :]
    for k in range(1, 8):
        moved_in = pltpu.roll(fwide[k * 8 : k * 8 + 8, :], k * 16, 1)
        tile = jnp.where(iota((8, 128), 1) // 16 == k, moved_in, tile)
    ftile[...] = tile
    put_gains(tile, lax.div(zc, 8))

    def put_rows(plane, slot):
        pad[plane, :, 7, :] = hrow[slot]
        pad[plane, :, 40, :] = hrow[slot + 1]

    def conv(plane, first, chans=(0, C)):
        def channels(step, carry):
            for k in range(4):
                c = step * 4 + k
                sums = [None, None, None]
                for b in range(3):
                    window = pad[plane, c, 7 + b : 39 + b, :]
                    for e in range(3):
                        term = depth_w[c, plane * 9 + b * 3 + e] * window
                        sums[e] = term if sums[e] is None else sums[e] + term
                value = sums[1] + pltpu.roll(sums[0], 1, 1) + pltpu.roll(sums[2], NX - 1, 1)
                depth[c] = value if first else depth[c] + value
            return carry

        lax.fori_loop(chans[0] // 4, chans[1] // 4, channels, 0)

    pl.semaphore_wait(tokens.at[0], 2)
    send_tokens(1, 4)

    pltpu.make_async_copy(recv1, recv1, r1).wait()
    for k in range(W):
        tmp[k * 8 : (k + 1) * 8, :] = (recv1[k] + recv1[8 + k]) + (recv1[16 + k] + recv1[24 + k])
    lower = iota((8, 128), 1) < 64
    for k in range(8):
        one = tmp[pl.ds(k // 2, 8, stride=8), :]
        two = tmp[pl.ds(k // 2 + 4, 8, stride=8), :]
        if k % 2 == 0:
            send2[k] = jnp.where(lower, one, pltpu.roll(two, 64, 1))
        else:
            send2[k] = jnp.where(lower, pltpu.roll(one, 64, 1), two)

    far_first = (8, 7, 9, 6, 10, 5, 11, 4, 12, 3, 13, 2, 14, 1, 15)
    pl.semaphore_wait(tokens.at[1], 2)

    def copy2(i):
        return pltpu.make_async_remote_copy(
            send2.at[lax.rem(zs[i], 8)], recv2.at[zc], s2, r2,
            device_id=(ring_peer(i), gy), device_id_type=MESH,
        )

    copyf = pltpu.make_async_remote_copy(
        ftile, ftile2, sf, rf, device_id=(ring_peer(8), gy), device_id_type=MESH
    )
    copyf.start()
    for i in far_first:
        copy2(i).start()
    own2 = pltpu.make_async_copy(send2.at[lax.rem(zc, 8)], recv2.at[zc], r2)
    own2.start()

    cross(1)
    loads[3].wait()

    def wait_rows(index, count):
        part = hrow.at[0:count]
        pltpu.make_async_copy(part, part, rh.at[index]).wait()

    wait_rows(0, 2)
    put_rows(1, 2)
    conv(1, True)

    wait_rows(1, 4)
    near = jnp.where(core == 0, 2, 0)
    far = 2 - near
    pltpu.make_async_copy(field3, pad.at[near, :, 8:40, :], rz.at[near]).wait()
    put_rows(near, near * 2)
    conv(near, False)

    grow = (iota((256, C), 0) // 8 == iota((256, C), 1)).astype(F32).astype(BF16)
    grow_t = (iota((C, 256), 1) // 8 == iota((C, 256), 0)).astype(F32).astype(BF16)
    diagonal = iota((256, 256), 0) % 8 == iota((256, 256), 1) % 8
    mixers = []
    for part in split(point_w[...]):
        tall = dot(grow, part).astype(BF16)
        mixers.append(jnp.where(diagonal, dot(tall, grow_t), 0.0).astype(BF16))
    copyf.wait_recv()
    put_gains(ftile2[...], 1 - lax.div(zc, 8))
    gain_re = jnp.transpose(gains[0])[0:16, :]
    gain_im = jnp.transpose(gains[1])[0:16, :]
    pltpu.make_async_copy(recv2, recv2, r2).wait()
    a_high, a_low = split(recv2[...].reshape(NZ, 128))
    both = dot(tz[...], jnp.concatenate([a_high, a_low], axis=0))
    modes = both[0:16] + both[32:48] + swapped(both[16:32] + both[48:64])
    filtered = modes * gain_re - swapped(modes) * gain_im
    stacked = jnp.concatenate([filtered, -swapped(filtered)], axis=0)
    f_high, f_low = split(stacked)
    both = dot(tzi[...], jnp.concatenate([f_high, f_low], axis=0))
    send4[...] = (both[0:128] + both[128:256]).reshape(ZC, 8, 128)

    def copy4(i):
        return pltpu.make_async_remote_copy(
            send4.at[zs[i]], recv4.at[pl.ds(pl.multiple_of(lax.rem(zc, 8) * 8, 8), 8), :], s4, r4,
            device_id=(ring_peer(i), gy), device_id_type=MESH,
        )

    nearer = (ZC - 4, 3, ZC - 3, 2, ZC - 2, 1, ZC - 1)
    for i in nearer:
        copy4(i).start()
    own4 = pltpu.make_async_copy(
        send4.at[zc], recv4.at[pl.ds(pl.multiple_of(lax.rem(zc, 8) * 8, 8), 8), :], r4
    )
    own4.start()

    cross(2)
    def wait_plane(plane, chans, landed):
        part = pad.at[plane, chans[0] : chans[1], 8:40, :]
        pltpu.make_async_copy(part, part, rz.at[landed]).wait()

    wait_plane(far, parts[0], far)
    put_rows(far, far * 2)
    conv(far, False, parts[0])
    pltpu.make_async_copy(recv4, recv4, r4).wait()
    for k in range(W):
        even = recv4[pl.ds(k, 4, stride=16), :]
        odd = recv4[pl.ds(8 + k, 4, stride=16), :]
        tmp3[k, 0:4] = jnp.where(lower[0:4], even, pltpu.roll(odd, 64, 1))
        tmp3[k, 4:8] = jnp.where(lower[0:4], pltpu.roll(even, 64, 1), odd)

    def copy3(i):
        target, t = plane_peer(i)
        return pltpu.make_async_remote_copy(
            tmp3.at[ws[i[1]]], recv3.at[w * 4 + gy], s3, r3,
            device_id=target, device_id_type=MESH,
        )

    for peer in plane_peers:
        copy3(peer).start()
    own3 = pltpu.make_async_copy(
        tmp3.at[w], recv3.at[w * 4 + gy], r3
    )
    own3.start()

    wait_plane(far, parts[1], 3)
    conv(far, False, parts[1])
    wait_plane(far, parts[2], 1)
    conv(far, False, parts[2])

    for k in range(YL // 8):
        d_high, d_low = split(depth[:, k * 8 : (k + 1) * 8, :].reshape(256, NX))
        value = dot(mixers[0], d_high) + dot(mixers[0], d_low) + dot(mixers[1], d_high)
        pacc[:, k * 8 : (k + 1) * 8, :] = value.reshape(C, 8, NX)
    put = pltpu.make_async_copy(pacc, point_out, so)
    put.start()

    for peer in plane_peers:
        copy1(peer).wait_send()
        copy3(peer).wait_send()
    for i in far_first:
        copy2(i).wait_send()
    for i in nearer:
        copy4(i).wait_send()
    copyf.wait_send()
    for dz in (-1, 0, 1):
        for side in range(2):
            copy_row(dz, side).wait_send()
    copy_plane(to_near, (0, C)).wait_send()
    for part in parts:
        copy_plane(-to_near, part).wait_send()

    pltpu.make_async_copy(recv3, recv3, r3).wait()
    put.wait()


def last_kernel(
    tiles_in, point_in, tyi_in, txi_in, bias_in, done_out,
    tiles, point, tyi, txi, bias, wide_yi, ld_sem, pt_sem, so,
):
    gy = lax.axis_index("gy")
    loads = [
        pltpu.make_async_copy(src, dst, ld_sem.at[k])
        for k, (src, dst) in enumerate(
            [(tyi_in.at[gy], tyi), (tiles_in, tiles), (bias_in, bias), (txi_in, txi)]
        )
    ]
    quarters = [pl.ds(k * 8, 8) for k in range(4)]
    points = [
        pltpu.make_async_copy(point_in.at[q], point.at[q], pt_sem.at[k]) for k, q in enumerate(quarters)
    ]
    for load in loads + points:
        load.start()
    block = iota((8, 128), 1) // 16 % 4
    same_i = iota((8, YL, 128), 0) == iota((8, YL, 128), 2) % 8
    loads[0].wait()
    for which in range(4):
        base = tyi[which]
        filled = jnp.where(same_i, jnp.broadcast_to(base[None], (8, YL, 128)), 0.0)
        row = which // 2 * 256
        filled = filled.reshape(256, 128).astype(BF16)
        for k in (0, 1) if which % 2 == 0 else (2,):
            wide_yi[row : row + 256, k * 128 : (k + 1) * 128] = filled
    loads[1].wait()
    loads[2].wait()
    columns = []
    for p in range(2):
        rows = []
        for ky in range(MY):
            q, k4 = ky // 4, ky % 4
            value = moved(tiles[p * 16 + q], 0 - k4)
            for kxb in range(1, 4):
                value = jnp.where(block == kxb, moved(tiles[(p * 4 + kxb) * 4 + q], kxb - k4), value)
            rows.append(value)
        columns.append(jnp.concatenate(rows, axis=0))
    r_high, r_low = split(jnp.concatenate(columns, axis=1))
    value = dot(wide_yi[...], jnp.concatenate([r_high, r_low, r_high], axis=0))
    y_halves = split(value)
    loads[3].wait()
    puts = []
    for step in range(4):
        points[step].wait()

        def gathered(half):
            real = half[step * 64 : (step + 1) * 64]
            imag = half[256 + step * 64 : 256 + (step + 1) * 64]
            return jnp.concatenate(
                [
                    jnp.concatenate(
                        [real[:, p * 128 : (p + 1) * 128], imag[:, p * 128 : (p + 1) * 128]], axis=1
                    )
                    for p in range(2)
                ],
                axis=0,
            )

        high, low = gathered(y_halves[0]), gathered(y_halves[1])
        spectral = dot(jnp.concatenate([high, low, high], axis=1), txi[...])
        for p in range(2):
            for sl in range(2):
                for ml in range(2):
                    ch = step * 8 + 4 * sl + 2 * ml + p
                    row = p * 64 + sl * 32
                    value = point[ch] + spectral[row : row + 32, ml * 256 : (ml + 1) * 256] + bias[0, ch]
                    point[ch] = 0.5 * value * (1.0 + lax.erf(value * (0.5**0.5)))
        chans = pl.ds(step * 8, 8)
        put = pltpu.make_async_copy(point.at[chans], done_out.at[chans], so.at[step])
        put.start()
        puts.append(put)
    for put in puts:
        put.wait()


def body(field, spectral_filter, depth_weight, point_weight, bias_vector):
    field3 = field.reshape(C, YL, NX)
    filt = spectral_filter.transpose(0, 2, 3, 1).reshape(64, 16)
    const = {name: jnp.asarray(value) for name, value in TABLES.items()}
    hbm = pl.BlockSpec(memory_space=pltpu.HBM)
    tiles, point = pl.pallas_call(
        wide_kernel,
        name="wide",
        out_shape=(
            jax.ShapeDtypeStruct((32, 8, 128), F32),
            jax.ShapeDtypeStruct((C, YL, NX), F32),
        ),
        in_specs=[hbm] * 8,
        out_specs=(hbm, hbm),
        scratch_shapes=[
            VMEM((C, YL, NX), F32),
            VMEM((64, 16), F32),
            VMEM((64, 128), F32),
            VMEM((8, 128), F32),
            VMEM((8, 128), F32),
            pltpu.SMEM((C, 27), F32),
            VMEM((C, C), F32),
            VMEM((2, 768, 256), BF16),
            VMEM((4, MY, 256), F32),
            VMEM((64, 256), BF16),
            VMEM((256, 64), BF16),
            VMEM((3, C, 48, NX), F32),
            VMEM((2, C, NX), F32),
            VMEM((6, C, NX), F32),
            VMEM((512, 256), BF16),
            VMEM((512, 256), BF16),
            VMEM((128, 256), F32),
            VMEM((32, 8, 128), F32),
            VMEM((32, 8, 128), F32),
            VMEM((64, 128), F32),
            VMEM((8, 8, 128), F32),
            VMEM((ZC, 8, 128), F32),
            VMEM((2, 128, 128), F32),
            VMEM((ZC, 8, 128), F32),
            VMEM((64, 128), F32),
            VMEM((W, 8, 128), F32),
            VMEM((C, YL, NX), F32),
            VMEM((C, YL, NX), F32),
            DMA((9,)), DMA, DMA, DMA, DMA((2,)), DMA, DMA((4,)), DMA, DMA, DMA, DMA, DMA, DMA, DMA, DMA, DMA,
            pltpu.SemaphoreType.REGULAR((2,)),
        ],
        compiler_params=pltpu.CompilerParams(
            collective_id=0, has_side_effects=True, vmem_limit_bytes=VMEM_ALL
        ),
    )(
        field3, filt, depth_weight, point_weight,
        const["tx"], const["ty"], const["tz"], const["tzi"],
    )
    value = pl.pallas_call(
        last_kernel,
        name="last",
        out_shape=jax.ShapeDtypeStruct((C, YL, NX), F32),
        in_specs=[hbm] * 5,
        out_specs=hbm,
        scratch_shapes=[
            VMEM((32, 8, 128), F32),
            VMEM((C, YL, NX), F32),
            VMEM((4, YL, 128), F32),
            VMEM((768, 512), BF16),
            pltpu.SMEM((1, C), F32),
            VMEM((512, 384), BF16),
            DMA((4,)), DMA((4,)), DMA((4,)),
        ],
        compiler_params=pltpu.CompilerParams(vmem_limit_bytes=VMEM_ALL),
    )(tiles, point, const["tyi"], const["txi"], bias_vector.reshape(1, C))
    return value.reshape(C, 1, YL, NX)


def solution(mesh):
    in_specs = (P(None, "gz", "gy", None), P(None, None, "gy", "gz"), P(), P(), P())
    out_specs = P(None, "gz", "gy", None)
    return jax.shard_map(body, mesh=mesh, in_specs=in_specs, out_specs=out_specs, check_vma=False)
```
